32 devices in a mesh: dp: 8 (over z, x), fsdp: 4 (over y, core).
Axes of the slice: x: 2, y: 2, z: 4, core: 2. Of those that a mesh axis runs over, the one named last changes fastest.
Arguments:
- latents: float32 [96, 256, 384], P(('dp', 'fsdp')), may hold values from -6 to 6
- conditioning: float32 [96, 384], P(('dp', 'fsdp')), may hold values from -6 to 6
- seq_counts: int32 [32], P(('dp', 'fsdp')), may hold values from 1 to 3, as said below
- cotangent: float32 [96, 256, 384], P(('dp', 'fsdp')), may hold values from -6 to 6
- ada_weight: bfloat16 [2, 384, 2304], P(None, 'fsdp'), may hold values from -0.3125 to 0.3125
- ada_bias: bfloat16 [2, 2304], P(None, 'fsdp'), may hold values from -2.390625 to 2.390625
- qkv_weight: bfloat16 [2, 384, 1152], P(None, 'fsdp'), may hold values from -0.3125 to 0.3125
- proj_weight: bfloat16 [2, 384, 384], P(None, 'fsdp'), may hold values from -6 to 6
- proj_bias: bfloat16 [2, 384], P(None, 'fsdp'), may hold values from -3.59375 to 3.59375
- up_weight: bfloat16 [2, 384, 1536], P(None, 'fsdp'), may hold values from -0.3125 to 0.3125
- up_bias: bfloat16 [2, 1536], P(None, 'fsdp'), may hold values from -3.59375 to 3.59375
- down_weight: bfloat16 [2, 1536, 384], P(None, 'fsdp'), may hold values from -0.15625 to 0.15625
- down_bias: bfloat16 [2, 384], P(None, 'fsdp'), may hold values from -3.59375 to 3.59375
Outputs:
- block_out: float32 [96, 256, 384], P(('dp', 'fsdp'))
- grad_latents: float32 [96, 256, 384], P(('dp', 'fsdp'))
- grad_conditioning: float32 [96, 384], P(('dp', 'fsdp'))
- grad_ada_weight: float32 [2, 384, 2304], P(None, 'fsdp')
- grad_ada_bias: float32 [2, 2304], P(None, 'fsdp')
- grad_qkv_weight: float32 [2, 384, 1152], P(None, 'fsdp')
- grad_proj_weight: float32 [2, 384, 384], P(None, 'fsdp')
- grad_proj_bias: float32 [2, 384], P(None, 'fsdp')
- grad_up_weight: float32 [2, 384, 1536], P(None, 'fsdp')
- grad_up_bias: float32 [2, 1536], P(None, 'fsdp')
- grad_down_weight: float32 [2, 1536, 384], P(None, 'fsdp')
- grad_down_bias: float32 [2, 384], P(None, 'fsdp')
The draws below stay inside these ranges and needn't reach their ends.
Inputs may be any that keep to these rules, and one draw needn't show every extreme that they name: `seq_counts`: number of live sequences of a device; its slots from that number on are padding.
All inputs are finite; a program needn't handle non-finite values.
Results may differ from the reference program's by a relative error of at most 0.014.
Values may be sent and summed in bfloat16 or wider, within the bound.
No kernel may reach another device: no remote copies, remote signals or barrier semaphores. Data moves between devices by JAX's collectives and lax.ppermute only.
A program may use at most 192 MiB of HBM per device.

```python
import jax
import jax.numpy as jnp
from jax import lax

D = 384
HEADS = 6
FF = 1536
L = 256
LAYERS = 2
SEQ_CAP = 3
SEQS = 96


def draw_conditioning(key, part):
    values = jnp.clip(jax.random.normal(key, (SEQS, D), jnp.float32), -6.0, 6.0)
    return values


def draw_seq_counts(key, part):
    device_count = SEQS // SEQ_CAP
    key_full = jax.random.fold_in(key, 11)
    key_place = jax.random.fold_in(key, 23)
    key_rest = jax.random.fold_in(key, 37)
    full_count = jax.random.randint(key_full, (), 1, device_count + 1, dtype=jnp.int32)
    order = jax.random.permutation(key_place, device_count).astype(jnp.int32)
    rest = jax.random.randint(key_rest, (device_count,), 1, SEQ_CAP + 1, dtype=jnp.int32)
    return jnp.where(order < full_count, jnp.int32(SEQ_CAP), rest).astype(jnp.int32)


def level_of(own_key, dims, cuts, low, high):
    def one(position, shards_of):
        steps = jax.random.uniform(jax.random.fold_in(jax.random.fold_in(own_key, 6), position), (shards_of,), jnp.float32, low / len(cuts), high / len(cuts))
        return jnp.repeat(jnp.exp(steps), dims[position] // shards_of).reshape((-1,) + (1,) * (len(dims) - position - 1))

    factor_of = one(*cuts[0])
    for cut in cuts[1:]:
        factor_of = factor_of * one(*cut)
    return factor_of


def normal_values(rng, extent, spread, reach, pieces=(), kind=jnp.bfloat16):
    values = jax.random.normal(rng, extent, jnp.float32) * spread
    if len(pieces) > 0:
        values = level_of(rng, extent, pieces, -0.22, 0.18) * values
    return jnp.clip(values, min=-reach, max=reach).astype(kind)


def setup_inputs(seed: int = 0) -> dict:
    splits = jax.random.split(jax.random.key(seed), 14)
    latents = normal_values(splits[0], (SEQS, L, D), 1.0, 6.0, ((0, 32),), jnp.float32)
    conditioning = draw_conditioning(jax.random.fold_in(splits[13], 71), 0)
    seq_counts = draw_seq_counts(jax.random.fold_in(splits[13], 71), 0)
    cotangent = normal_values(splits[3], (SEQS, L, D), 1.0, 6.0, ((0, 32),), jnp.float32)
    ada_weight = normal_values(splits[4], (LAYERS, D, 6 * D), D ** -0.5, 0.3125, ((1, 4),))
    ada_bias = normal_values(splits[5], (LAYERS, 6 * D), 0.6, 2.390625, ((1, 4),))
    qkv_weight = normal_values(splits[6], (LAYERS, D, 3 * D), D ** -0.5, 0.3125, ((1, 4),))
    proj_weight = normal_values(splits[7], (LAYERS, D, D), 1 ** -0.5, 6.0, ((1, 4),))
    proj_bias = normal_values(splits[8], (LAYERS, D), 0.9, 3.59375, ((1, 4),))
    up_weight = normal_values(splits[9], (LAYERS, D, FF), D ** -0.5, 0.3125, ((1, 4),))
    up_bias = normal_values(splits[10], (LAYERS, FF), 0.9, 3.59375, ((1, 4),))
    down_weight = normal_values(splits[11], (LAYERS, FF, D), FF ** -0.5, 0.15625, ((1, 4),))
    down_bias = normal_values(splits[12], (LAYERS, D), 0.9, 3.59375, ((1, 4),))
    return {"latents": latents, "conditioning": conditioning, "seq_counts": seq_counts, "cotangent": cotangent, "ada_weight": ada_weight, "ada_bias": ada_bias, "qkv_weight": qkv_weight, "proj_weight": proj_weight, "proj_bias": proj_bias, "up_weight": up_weight, "up_bias": up_bias, "down_weight": down_weight, "down_bias": down_bias}


NORM_EPS = 1e-06
GELU_K = 0.7978845608028654
GELU_C = 0.044715

def einsum_full(form, left, right):
    return jnp.einsum(form, left.astype(jnp.float32), right.astype(jnp.float32), precision=lax.Precision.HIGHEST)

def matmul_last(left, right):
    flat = left.reshape(-1, left.shape[-1])
    return jnp.dot(flat, right, preferred_element_type=jnp.float32).reshape(left.shape[:-1] + (right.shape[1],))

def matmul_back(left, right):
    flat = left.reshape(-1, left.shape[-1])
    return jnp.dot(flat, right.T, preferred_element_type=jnp.float32).reshape(left.shape[:-1] + (right.shape[0],))

def outer_total(left, right):
    return jnp.dot(left.reshape(-1, left.shape[-1]).T, right.reshape(-1, right.shape[-1]), preferred_element_type=jnp.float32)

def norm_rows(values):
    center = values - lax.optimization_barrier(jnp.mean(values, axis=-1, keepdims=True))
    inv_std = lax.rsqrt(lax.optimization_barrier(jnp.mean(center * center, axis=-1, keepdims=True)) + NORM_EPS)
    return (center * inv_std, inv_std)

def norm_back(normed, inv_std, grad_normed):
    mean_grad = lax.optimization_barrier(jnp.mean(grad_normed, axis=-1, keepdims=True))
    mean_prod = lax.optimization_barrier(jnp.mean(grad_normed * normed, axis=-1, keepdims=True))
    return inv_std * (grad_normed - mean_grad - normed * mean_prod)

def gelu_tanh(values):
    inner = GELU_K * (values + GELU_C * values * values * values)
    return 0.5 * values * (1.0 + jnp.tanh(inner))

def gelu_slope(values):
    tangent = jnp.tanh(GELU_K * (values + GELU_C * values * values * values))
    return 0.5 * (1.0 + tangent) + 0.5 * values * (1.0 - tangent * tangent) * GELU_K * (1.0 + 3.0 * GELU_C * values * values)

def silu_slope(values):
    sigm = jax.nn.sigmoid(values)
    return sigm * (1.0 + values * (1.0 - sigm))

def split_heads(qkv):
    seq_slots, length, triple = qkv.shape
    width = triple // 3
    split = qkv.reshape(seq_slots, length, 3, HEADS, width // HEADS)
    return (split[:, :, 0], split[:, :, 1], split[:, :, 2])

def attend(qkv):
    queries, keys, values = split_heads(qkv)
    scale = 1.0 / jnp.sqrt(jnp.float32(queries.shape[-1]))
    scores = einsum_full('sqhd,skhd->shqk', queries, keys) * scale
    top = lax.optimization_barrier(jnp.max(scores, axis=-1, keepdims=True))
    expo = jnp.exp(scores - top)
    probs = expo / lax.optimization_barrier(jnp.sum(expo, axis=-1, keepdims=True))
    probs_low = probs.astype(jnp.bfloat16)
    mixed = einsum_full('shqk,skhd->sqhd', probs_low, values).astype(jnp.bfloat16)
    return (probs, probs_low, mixed.reshape(qkv.shape[0], qkv.shape[1], -1))

def attend_back(qkv, probs, probs_low, grad_mixed):
    queries, keys, values = split_heads(qkv)
    scale = 1.0 / jnp.sqrt(jnp.float32(queries.shape[-1]))
    grad_heads = grad_mixed.reshape(values.shape)
    grad_probs = einsum_full('sqhd,skhd->shqk', grad_heads, values)
    grad_values = einsum_full('shqk,sqhd->skhd', probs_low, grad_heads)
    row_dot = lax.optimization_barrier(jnp.sum(probs * grad_probs, axis=-1, keepdims=True))
    grad_scores = (probs * (grad_probs - row_dot) * scale).astype(jnp.bfloat16)
    grad_queries = einsum_full('shqk,skhd->sqhd', grad_scores, keys)
    grad_keys = einsum_full('shqk,sqhd->skhd', grad_scores, queries)
    joined = jnp.stack([grad_queries, grad_keys, grad_values], axis=2)
    return joined.reshape(qkv.shape).astype(jnp.bfloat16)

def layer_parts(resid, cond, weights):
    ada_weight, ada_bias, qkv_weight, proj_weight, proj_bias, up_weight, up_bias, down_weight, down_bias = weights
    width = resid.shape[-1]
    act_low = jax.nn.silu(cond).astype(jnp.bfloat16)
    ada = jnp.dot(act_low, ada_weight, preferred_element_type=jnp.float32) + ada_bias.astype(jnp.float32)
    mods = [ada[:, None, piece_idx * width:(piece_idx + 1) * width] for piece_idx in range(6)]
    normed_one, inv_one = norm_rows(resid)
    attn_in = (normed_one * (1.0 + mods[1]) + mods[0]).astype(jnp.bfloat16)
    qkv = matmul_last(attn_in, qkv_weight).astype(jnp.bfloat16)
    probs, probs_low, mixed = attend(qkv)
    attn = matmul_last(mixed, proj_weight) + proj_bias.astype(jnp.float32)
    resid_one = resid + mods[2] * attn
    normed_two, inv_two = norm_rows(resid_one)
    mlp_in = (normed_two * (1.0 + mods[4]) + mods[3]).astype(jnp.bfloat16)
    pre_act = matmul_last(mlp_in, up_weight) + up_bias.astype(jnp.float32)
    hidden = gelu_tanh(pre_act).astype(jnp.bfloat16)
    branch = matmul_last(hidden, down_weight) + down_bias.astype(jnp.float32)
    result = resid_one + mods[5] * branch
    return dict(act_low=act_low, mods=mods, normed_one=normed_one, inv_one=inv_one, attn_in=attn_in, qkv=qkv, probs=probs, probs_low=probs_low, mixed=mixed, attn=attn, normed_two=normed_two, inv_two=inv_two, mlp_in=mlp_in, pre_act=pre_act, hidden=hidden, branch=branch, result=result)

def layer_backward(resid, cond, weights, grad_out):
    ada_weight, ada_bias, qkv_weight, proj_weight, proj_bias, up_weight, up_bias, down_weight, down_bias = weights
    saved = layer_parts(resid, cond, weights)
    mods = saved['mods']
    grad_gate_two = lax.optimization_barrier(jnp.sum(grad_out * saved['branch'], axis=1))
    grad_branch = grad_out * mods[5]
    grad_down_bias = lax.optimization_barrier(jnp.sum(grad_branch, axis=(0, 1)))
    branch_low = grad_branch.astype(jnp.bfloat16)
    grad_down_weight = outer_total(saved['hidden'], branch_low)
    grad_pre = matmul_back(branch_low, down_weight) * gelu_slope(saved['pre_act'])
    grad_up_bias = lax.optimization_barrier(jnp.sum(grad_pre, axis=(0, 1)))
    pre_low = grad_pre.astype(jnp.bfloat16)
    grad_up_weight = outer_total(saved['mlp_in'], pre_low)
    grad_mlp = matmul_back(pre_low, up_weight)
    grad_shift_two = lax.optimization_barrier(jnp.sum(grad_mlp, axis=1))
    grad_scale_two = lax.optimization_barrier(jnp.sum(grad_mlp * saved['normed_two'], axis=1))
    grad_one = grad_out + norm_back(saved['normed_two'], saved['inv_two'], grad_mlp * (1.0 + mods[4]))
    grad_gate_one = lax.optimization_barrier(jnp.sum(grad_one * saved['attn'], axis=1))
    grad_attn = grad_one * mods[2]
    grad_proj_bias = lax.optimization_barrier(jnp.sum(grad_attn, axis=(0, 1)))
    attn_low = grad_attn.astype(jnp.bfloat16)
    grad_proj_weight = outer_total(saved['mixed'], attn_low)
    grad_mixed = matmul_back(attn_low, proj_weight).astype(jnp.bfloat16)
    grad_qkv = attend_back(saved['qkv'], saved['probs'], saved['probs_low'], grad_mixed)
    grad_qkv_weight = outer_total(saved['attn_in'], grad_qkv)
    grad_in = matmul_back(grad_qkv, qkv_weight)
    grad_shift_one = lax.optimization_barrier(jnp.sum(grad_in, axis=1))
    grad_scale_one = lax.optimization_barrier(jnp.sum(grad_in * saved['normed_one'], axis=1))
    grad_resid = grad_one + norm_back(saved['normed_one'], saved['inv_one'], grad_in * (1.0 + mods[1]))
    grad_ada = jnp.concatenate([grad_shift_one, grad_scale_one, grad_gate_one, grad_shift_two, grad_scale_two, grad_gate_two], axis=-1)
    grad_ada_bias = lax.optimization_barrier(jnp.sum(grad_ada, axis=0))
    ada_low = grad_ada.astype(jnp.bfloat16)
    grad_ada_weight = jnp.dot(saved['act_low'].T, ada_low, preferred_element_type=jnp.float32)
    grad_cond = jnp.dot(ada_low, ada_weight.T, preferred_element_type=jnp.float32) * silu_slope(cond)
    grads = (grad_ada_weight, grad_ada_bias, grad_qkv_weight, grad_proj_weight, grad_proj_bias, grad_up_weight, grad_up_bias, grad_down_weight, grad_down_bias)
    return (grad_resid, grad_cond, grads)

def reference(latents, conditioning, seq_counts, cotangent, ada_weight, ada_bias, qkv_weight, proj_weight, proj_bias, up_weight, up_bias, down_weight, down_bias):
    stacks = (ada_weight, ada_bias, qkv_weight, proj_weight, proj_bias, up_weight, up_bias, down_weight, down_bias)
    layers = [tuple((stack[layer_idx] for stack in stacks)) for layer_idx in range(LAYERS)]
    blocks = SEQS // SEQ_CAP

    def one_block(totals, block_idx):
        start = (block_idx * SEQ_CAP).astype(jnp.int32)
        resid = lax.dynamic_slice_in_dim(latents, start, SEQ_CAP, 0)
        cond = lax.dynamic_slice_in_dim(conditioning, start, SEQ_CAP, 0)
        grad = lax.dynamic_slice_in_dim(cotangent, start, SEQ_CAP, 0)
        live = (jnp.arange(SEQ_CAP, dtype=jnp.int32) < seq_counts[block_idx]).astype(jnp.float32)[:, None, None]
        inputs = []
        current = resid
        for weights in layers:
            inputs.append(current)
            current = layer_parts(current, cond, weights)['result']
        output = current * live
        grad = grad * live
        grad_cond = jnp.zeros(cond.shape, jnp.float32)
        new_totals = list(totals)
        for layer_idx in reversed(range(LAYERS)):
            grad, cond_part, grads = layer_backward(inputs[layer_idx], cond, layers[layer_idx], grad)
            grad_cond = grad_cond + cond_part
            new_totals[layer_idx] = tuple((old + new for old, new in zip(totals[layer_idx], grads)))
        return (tuple(new_totals), (output, grad, grad_cond))
    initial = tuple((tuple((jnp.zeros(stack.shape[1:], jnp.float32) for stack in stacks)) for layer_idx in range(LAYERS)))
    totals, (outputs, grad_inputs, grad_conds) = lax.scan(one_block, initial, jnp.arange(blocks, dtype=jnp.int32))
    block_out = outputs.reshape(latents.shape)
    grad_latents = grad_inputs.reshape(latents.shape)
    grad_conditioning = grad_conds.reshape(conditioning.shape)
    stacked = [jnp.stack([totals[layer_idx][piece_idx] for layer_idx in range(LAYERS)], axis=0) for piece_idx in range(9)]
    return (block_out, grad_latents, grad_conditioning, stacked[0], stacked[1], stacked[2], stacked[3], stacked[4], stacked[5], stacked[6], stacked[7], stacked[8])
```

```python
import functools

import jax
import jax.numpy as jnp
from jax import lax
from jax.sharding import PartitionSpec as P

HEADS = 6
LAYERS = 2


NORM_EPS = 1e-06
GELU_K = 0.7978845608028654
GELU_C = 0.044715


def einsum_mixed(form, left, right):
    return jnp.einsum(form, left, right, preferred_element_type=jnp.float32)


def matmul_last(left, right):
    flat = left.reshape(-1, left.shape[-1])
    return jnp.dot(flat, right, preferred_element_type=jnp.float32).reshape(
        left.shape[:-1] + (right.shape[1],)
    )


def matmul_back(left, right):
    flat = left.reshape(-1, left.shape[-1])
    return jnp.dot(flat, right.T, preferred_element_type=jnp.float32).reshape(
        left.shape[:-1] + (right.shape[0],)
    )


def outer_total(left, right):
    return jnp.dot(
        left.reshape(-1, left.shape[-1]).T,
        right.reshape(-1, right.shape[-1]),
        preferred_element_type=jnp.float32,
    )


def norm_rows(values):
    center = values - jnp.mean(values, axis=-1, keepdims=True)
    inv_std = lax.rsqrt(jnp.mean(center * center, axis=-1, keepdims=True) + NORM_EPS)
    return (center * inv_std, inv_std)


def norm_back(normed, inv_std, grad_normed):
    mean_grad = jnp.mean(grad_normed, axis=-1, keepdims=True)
    mean_prod = jnp.mean(grad_normed * normed, axis=-1, keepdims=True)
    return inv_std * (grad_normed - mean_grad - normed * mean_prod)


def gelu_tanh(values):
    inner = GELU_K * (values + GELU_C * values * values * values)
    return 0.5 * values * (1.0 + jnp.tanh(inner))


def gelu_slope(values):
    tangent = jnp.tanh(GELU_K * (values + GELU_C * values * values * values))
    return 0.5 * (1.0 + tangent) + 0.5 * values * (1.0 - tangent * tangent) * GELU_K * (
        1.0 + 3.0 * GELU_C * values * values
    )


def silu_slope(values):
    sigm = jax.nn.sigmoid(values)
    return sigm * (1.0 + values * (1.0 - sigm))


def split_heads(qkv):
    seq_slots, length, triple = qkv.shape
    width = triple // 3
    split = qkv.reshape(seq_slots, length, 3, HEADS, width // HEADS)
    return (split[:, :, 0], split[:, :, 1], split[:, :, 2])


def attend(qkv):
    queries, keys, values = split_heads(qkv)
    scale = 1.0 / jnp.sqrt(jnp.float32(queries.shape[-1]))
    scores = einsum_mixed("sqhd,skhd->shqk", queries, keys) * scale
    top = jnp.max(scores, axis=-1, keepdims=True)
    expo = jnp.exp(scores - top)
    probs = expo / jnp.sum(expo, axis=-1, keepdims=True)
    probs_low = probs.astype(jnp.bfloat16)
    mixed = einsum_mixed("shqk,skhd->sqhd", probs_low, values).astype(jnp.bfloat16)
    return (probs, probs_low, mixed.reshape(qkv.shape[0], qkv.shape[1], -1))


def attend_back(qkv, probs, probs_low, grad_mixed):
    queries, keys, values = split_heads(qkv)
    scale = 1.0 / jnp.sqrt(jnp.float32(queries.shape[-1]))
    grad_heads = grad_mixed.reshape(values.shape)
    grad_probs = einsum_mixed("sqhd,skhd->shqk", grad_heads, values)
    grad_values = einsum_mixed("shqk,sqhd->skhd", probs_low, grad_heads)
    row_dot = jnp.sum(probs * grad_probs, axis=-1, keepdims=True)
    grad_scores = (probs * (grad_probs - row_dot) * scale).astype(jnp.bfloat16)
    grad_queries = einsum_mixed("shqk,skhd->sqhd", grad_scores, keys)
    grad_keys = einsum_mixed("shqk,sqhd->skhd", grad_scores, queries)
    joined = jnp.stack([grad_queries, grad_keys, grad_values], axis=2)
    return joined.reshape(qkv.shape).astype(jnp.bfloat16)


def layer_parts(resid, ada, weights):
    qkv_weight, proj_weight, proj_bias, up_weight, up_bias, down_weight, down_bias = weights
    width = resid.shape[-1]
    mods = [ada[:, None, piece_idx * width : (piece_idx + 1) * width] for piece_idx in range(6)]
    normed_one, inv_one = norm_rows(resid)
    attn_in = (normed_one * (1.0 + mods[1]) + mods[0]).astype(jnp.bfloat16)
    qkv = matmul_last(attn_in, qkv_weight).astype(jnp.bfloat16)
    probs, probs_low, mixed = attend(qkv)
    attn = matmul_last(mixed, proj_weight) + proj_bias.astype(jnp.float32)
    resid_one = resid + mods[2] * attn
    normed_two, inv_two = norm_rows(resid_one)
    mlp_in = (normed_two * (1.0 + mods[4]) + mods[3]).astype(jnp.bfloat16)
    pre_act = matmul_last(mlp_in, up_weight) + up_bias.astype(jnp.float32)
    hidden = gelu_tanh(pre_act).astype(jnp.bfloat16)
    branch = matmul_last(hidden, down_weight) + down_bias.astype(jnp.float32)
    result = resid_one + mods[5] * branch
    return dict(
        mods=mods,
        normed_one=normed_one,
        inv_one=inv_one,
        attn_in=attn_in,
        qkv=qkv,
        probs=probs,
        probs_low=probs_low,
        mixed=mixed,
        attn=attn,
        normed_two=normed_two,
        inv_two=inv_two,
        mlp_in=mlp_in,
        pre_act=pre_act,
        hidden=hidden,
        branch=branch,
        result=result,
    )


def layer_backward(saved, weights, grad_out):
    qkv_weight, proj_weight, proj_bias, up_weight, up_bias, down_weight, down_bias = weights
    mods = saved["mods"]
    grad_gate_two = jnp.sum(grad_out * saved["branch"], axis=1)
    grad_branch = grad_out * mods[5]
    grad_down_bias = jnp.sum(grad_branch, axis=(0, 1))
    branch_low = grad_branch.astype(jnp.bfloat16)
    grad_down_weight = outer_total(saved["hidden"], branch_low)
    grad_pre = matmul_back(branch_low, down_weight) * gelu_slope(saved["pre_act"])
    grad_up_bias = jnp.sum(grad_pre, axis=(0, 1))
    pre_low = grad_pre.astype(jnp.bfloat16)
    grad_up_weight = outer_total(saved["mlp_in"], pre_low)
    grad_mlp = matmul_back(pre_low, up_weight)
    grad_shift_two = jnp.sum(grad_mlp, axis=1)
    grad_scale_two = jnp.sum(grad_mlp * saved["normed_two"], axis=1)
    grad_one = grad_out + norm_back(
        saved["normed_two"], saved["inv_two"], grad_mlp * (1.0 + mods[4])
    )
    grad_gate_one = jnp.sum(grad_one * saved["attn"], axis=1)
    grad_attn = grad_one * mods[2]
    grad_proj_bias = jnp.sum(grad_attn, axis=(0, 1))
    attn_low = grad_attn.astype(jnp.bfloat16)
    grad_proj_weight = outer_total(saved["mixed"], attn_low)
    grad_mixed = matmul_back(attn_low, proj_weight).astype(jnp.bfloat16)
    grad_qkv = attend_back(saved["qkv"], saved["probs"], saved["probs_low"], grad_mixed)
    grad_qkv_weight = outer_total(saved["attn_in"], grad_qkv)
    grad_in = matmul_back(grad_qkv, qkv_weight)
    grad_shift_one = jnp.sum(grad_in, axis=1)
    grad_scale_one = jnp.sum(grad_in * saved["normed_one"], axis=1)
    grad_resid = grad_one + norm_back(
        saved["normed_one"], saved["inv_one"], grad_in * (1.0 + mods[1])
    )
    grad_ada = jnp.concatenate(
        [
            grad_shift_one,
            grad_scale_one,
            grad_gate_one,
            grad_shift_two,
            grad_scale_two,
            grad_gate_two,
        ],
        axis=-1,
    )
    bias_row = jnp.concatenate([grad_proj_bias, grad_up_bias, grad_down_bias])
    wide = (grad_qkv_weight, grad_proj_weight, grad_up_weight, grad_down_weight)
    return grad_resid, grad_ada, bias_row, wide


def bits_of(size):
    assert size & (size - 1) == 0
    return [1 << k for k in range(size.bit_length() - 1)]


def swap(value, axis, size, bit):
    return lax.ppermute(value, axis, [(i, i ^ bit) for i in range(size)])


def has_bit(axis, bit):
    return (lax.axis_index(axis) & bit) != 0


def gather_rel(value, axis, size):
    pieces = {0: value}
    for bit in reversed(bits_of(size)):
        for j in list(pieces):
            pieces[j ^ bit] = swap(pieces[j], axis, size, bit)
    return [pieces[j] for j in range(size)]


def to_absolute(pieces, axis):
    me = lax.axis_index(axis)
    out = jnp.zeros((len(pieces),) + pieces[0].shape, pieces[0].dtype)
    for j, piece in enumerate(pieces):
        out = lax.dynamic_update_index_in_dim(out, piece, me ^ j, 0)
    return out


def scatter_sum(blocks, axis, size, wire):
    blocks = dict(enumerate(blocks))
    for bit in bits_of(size):
        keep = [j for j in blocks if not j & bit]
        sent = jnp.concatenate([blocks[j | bit].astype(wire) for j in keep], axis=0)
        got = swap(sent, axis, size, bit)
        rows = got.shape[0] // len(keep)
        blocks = {
            j: blocks[j].astype(jnp.float32) + got[n * rows : (n + 1) * rows].astype(jnp.float32)
            for n, j in enumerate(keep)
        }
    return blocks[0]


def all_sum(value, axis, size, wire):
    bits = bits_of(size)
    trail = []
    for n, bit in enumerate(bits):
        width = value.shape[-1]
        if n < len(bits) - 1 and (width // 2) % 128 == 0:
            low, high = value[:, : width // 2], value[:, width // 2 :]
            upper = has_bit(axis, bit)
            sent = jnp.where(upper, low, high).astype(wire)
            kept = jnp.where(upper, high, low)
            value = kept.astype(jnp.float32) + swap(sent, axis, size, bit).astype(jnp.float32)
            trail.append(bit)
        else:
            low = value.astype(wire)
            value = low.astype(jnp.float32) + swap(low, axis, size, bit).astype(jnp.float32)
    if not trail:
        return value
    value = value.astype(wire)
    for bit in reversed(trail):
        other = swap(value, axis, size, bit)
        upper = has_bit(axis, bit)
        value = jnp.concatenate(
            [jnp.where(upper, other, value), jnp.where(upper, value, other)], axis=-1
        )
    return value.astype(jnp.float32)


def gather_all(value, stages):
    for axis, size, bit in stages:
        other = swap(value, axis, size, bit)
        upper = has_bit(axis, bit)
        value = jnp.concatenate(
            [jnp.where(upper, other, value), jnp.where(upper, value, other)], axis=0
        )
    return value


def pack_rows(qkv, proj, up, down):
    rows = qkv.shape[0]
    blocks = [down[n * rows : (n + 1) * rows] for n in range(down.shape[0] // rows)]
    return jnp.concatenate([qkv, proj, up] + blocks, axis=1)


def on_device(
    sizes,
    latents,
    conditioning,
    seq_counts,
    cotangent,
    ada_weight,
    ada_bias,
    qkv_weight,
    proj_weight,
    proj_bias,
    up_weight,
    up_bias,
    down_weight,
    down_bias,
):
    groups, shards = sizes
    bf16, f32 = jnp.bfloat16, jnp.float32
    slots, _, width = latents.shape
    rows = qkv_weight.shape[1]
    triple, inner = qkv_weight.shape[2], up_weight.shape[2]
    wide = ada_weight.shape[2]
    ratio = inner // width
    me = lax.axis_index("fsdp")

    packs = [
        pack_rows(qkv_weight[n], proj_weight[n], up_weight[n], down_weight[n])
        for n in range(LAYERS)
    ]
    fulls = []
    for n in range(LAYERS):
        full = to_absolute(gather_rel(packs[n], "fsdp", shards), "fsdp")
        edge = [0, triple, triple + width, triple + width + inner]
        down_full = full[:, :, edge[3] :].reshape(shards, rows, ratio, width)
        fulls.append(
            (
                full[:, :, : edge[1]].reshape(width, triple),
                full[:, :, edge[1] : edge[2]].reshape(width, width),
                full[:, :, edge[2] : edge[3]].reshape(width, inner),
                down_full.transpose(0, 2, 1, 3).reshape(inner, width),
            )
        )

    act = jax.nn.silu(conditioning).astype(bf16)
    shard_bias = jnp.concatenate([ada_bias, proj_bias, up_bias, down_bias], axis=1)
    bias_width = shard_bias.shape[1]
    small = jnp.concatenate([act.reshape(-1), shard_bias.reshape(-1)])
    small = to_absolute(gather_rel(small, "fsdp", shards), "fsdp")
    act_group = small[:, : slots * width].reshape(shards * slots, width)
    biases = small[:, slots * width :].reshape(shards, LAYERS, bias_width)
    act_cols = lax.dynamic_slice(act_group, (0, me * rows), (shards * slots, rows))
    partial = jnp.stack(
        [jnp.dot(act_cols, ada_weight[n], preferred_element_type=f32) for n in range(LAYERS)]
    ).reshape(LAYERS, shards, slots, wide)
    blocks = [
        lax.dynamic_index_in_dim(partial, me ^ j, 1, keepdims=False).reshape(LAYERS * slots, wide)
        for j in range(shards)
    ]
    ada = scatter_sum(blocks, "fsdp", shards, f32).reshape(LAYERS, slots, wide)
    cut = [0]
    for part in (ada_bias, proj_bias, up_bias, down_bias):
        cut.append(cut[-1] + part.shape[1])
    bias_of = [
        [biases[:, n, cut[k] : cut[k + 1]].reshape(-1).astype(f32) for k in range(4)]
        for n in range(LAYERS)
    ]

    live = (jnp.arange(slots, dtype=jnp.int32) < seq_counts[0]).astype(f32)[:, None, None]
    saved, weights = [], []
    current = latents
    for n in range(LAYERS):
        qkv_full, proj_full, up_full, down_full = fulls[n]
        ada_b, proj_b, up_b, down_b = bias_of[n]
        weights.append((qkv_full, proj_full, proj_b, up_full, up_b, down_full, down_b))
        saved.append(layer_parts(current, ada[n] + ada_b, weights[n]))
        current = saved[n]["result"]
    block_out = current * live
    grad = cotangent * live

    stages = [("dp", groups, bit) for bit in reversed(bits_of(groups))]
    stages += [("fsdp", shards, bit) for bit in reversed(bits_of(shards))]
    sums, gads, bias_rows = [None] * LAYERS, [None] * LAYERS, [None] * LAYERS
    acts = None
    for n in reversed(range(LAYERS)):
        grad, grad_ada, bias_row, (g_qkv, g_proj, g_up, g_down) = layer_backward(
            saved[n], weights[n], grad
        )
        down_rows = g_down.reshape(shards, ratio * rows, width)
        terms = []
        for j in range(shards):
            own = me ^ j
            terms.append(
                pack_rows(
                    lax.dynamic_slice_in_dim(g_qkv, own * rows, rows, 0),
                    lax.dynamic_slice_in_dim(g_proj, own * rows, rows, 0),
                    lax.dynamic_slice_in_dim(g_up, own * rows, rows, 0),
                    lax.dynamic_index_in_dim(down_rows, own, 0, keepdims=False),
                ).astype(bf16)
            )
        shard = scatter_sum(terms, "fsdp", shards, bf16)
        sums[n] = all_sum(shard, "dp", groups, bf16)
        rows_out = [grad_ada.astype(bf16), bias_row[None].astype(bf16)]
        if acts is None:
            flat = act.reshape(-1)
            flat = jnp.pad(flat, (0, -flat.shape[0] % wide)).reshape(-1, wide)
            rows_out.append(flat)
        message = jnp.concatenate(rows_out, axis=0)
        every = gather_all(message[None], stages)
        gads[n] = every[:, :slots]
        bias_rows[n] = every[:, slots]
        if acts is None:
            acts = every[:, slots + 1 :].reshape(every.shape[0], -1)[:, : slots * width]
            acts = acts.reshape(-1, width)

    acts_cols = lax.dynamic_slice(acts, (0, me * rows), (acts.shape[0], rows))
    g_ada = jnp.stack(
        [outer_total(acts_cols, gads[n].reshape(-1, wide)) for n in range(LAYERS)]
    )
    g_ada_bias = jnp.stack([jnp.sum(gads[n].astype(f32), axis=(0, 1)) for n in range(LAYERS)])
    g_bias = jnp.stack([jnp.sum(bias_rows[n].astype(f32), axis=0) for n in range(LAYERS)])

    place = jnp.int32(0)
    for k, bit in enumerate(reversed(bits_of(groups))):
        place = place + has_bit("dp", bit).astype(jnp.int32) * (1 << k)
    total = 0.0
    for n in range(LAYERS):
        grid = gads[n].reshape(shards, groups, slots, wide)
        mine = lax.dynamic_index_in_dim(grid, place, 1, keepdims=False).reshape(-1, wide)
        total = total + matmul_back(mine, ada_weight[n])
    total = total.reshape([2] * len(bits_of(shards)) + [slots, rows])
    order = tuple(reversed(range(len(bits_of(shards)))))
    total = total.transpose(order + (len(order), len(order) + 1)).reshape(shards, slots, rows)
    got = [lax.dynamic_index_in_dim(total, me, 0, keepdims=False)]
    for j in range(1, shards):
        sent = lax.dynamic_index_in_dim(total, me ^ j, 0, keepdims=False)
        got.append(swap(sent, "fsdp", shards, j))
    grad_cond = to_absolute(got, "fsdp").transpose(1, 0, 2).reshape(slots, width)
    grad_cond = grad_cond * silu_slope(conditioning)

    wide_sum = jnp.stack(sums)
    edge = [0, triple, triple + width, triple + width + inner]
    down_sum = wide_sum[:, :, edge[3] :].reshape(LAYERS, rows, ratio, width)
    own_inner = inner // shards
    return (
        block_out,
        grad,
        grad_cond,
        g_ada,
        lax.dynamic_slice_in_dim(g_ada_bias, me * (wide // shards), wide // shards, 1),
        wide_sum[:, :, : edge[1]],
        wide_sum[:, :, edge[1] : edge[2]],
        lax.dynamic_slice_in_dim(g_bias, me * rows, rows, 1),
        wide_sum[:, :, edge[2] : edge[3]],
        lax.dynamic_slice_in_dim(g_bias, width + me * own_inner, own_inner, 1),
        down_sum.transpose(0, 2, 1, 3).reshape(LAYERS, ratio * rows, width),
        lax.dynamic_slice_in_dim(g_bias, width + inner + me * rows, rows, 1),
    )


def solution(mesh):
    in_specs = (
        P(("dp", "fsdp"), None, None),
        P(("dp", "fsdp"), None),
        P(("dp", "fsdp")),
        P(("dp", "fsdp"), None, None),
        P(None, "fsdp", None),
        P(None, "fsdp"),
        P(None, "fsdp", None),
        P(None, "fsdp", None),
        P(None, "fsdp"),
        P(None, "fsdp", None),
        P(None, "fsdp"),
        P(None, "fsdp", None),
        P(None, "fsdp"),
    )
    out_specs = (
        P(("dp", "fsdp"), None, None),
        P(("dp", "fsdp"), None, None),
        P(("dp", "fsdp"), None),
        P(None, "fsdp", None),
        P(None, "fsdp"),
        P(None, "fsdp", None),
        P(None, "fsdp", None),
        P(None, "fsdp"),
        P(None, "fsdp", None),
        P(None, "fsdp"),
        P(None, "fsdp", None),
        P(None, "fsdp"),
    )
    return jax.shard_map(
        functools.partial(on_device, (mesh.shape["dp"], mesh.shape["fsdp"])), mesh=mesh, in_specs=in_specs, out_specs=out_specs, check_vma=False
    )
```

```python
import functools

import jax
import jax.numpy as jnp
from jax import lax
from jax.experimental import pallas as pl
from jax.experimental.pallas import tpu as pltpu
from jax.sharding import PartitionSpec as P

HEADS = 6
LAYERS = 2
VMEM_GRANT = 60 * 1024 * 1024


NORM_EPS = 1e-06
GELU_K = 0.7978845608028654
GELU_C = 0.044715


def matmul_back(left, right):
    flat = left.reshape(-1, left.shape[-1])
    return jnp.dot(flat, right.T, preferred_element_type=jnp.float32).reshape(
        left.shape[:-1] + (right.shape[0],)
    )


def outer_total(left, right):
    return jnp.dot(
        left.reshape(-1, left.shape[-1]).T,
        right.reshape(-1, right.shape[-1]),
        preferred_element_type=jnp.float32,
    )


def norm_rows(values):
    center = values - jnp.mean(values, axis=-1, keepdims=True)
    inv_std = lax.rsqrt(jnp.mean(center * center, axis=-1, keepdims=True) + NORM_EPS)
    return (center * inv_std, inv_std)


def norm_back(normed, inv_std, grad_normed):
    mean_grad = jnp.mean(grad_normed, axis=-1, keepdims=True)
    mean_prod = jnp.mean(grad_normed * normed, axis=-1, keepdims=True)
    return inv_std * (grad_normed - mean_grad - normed * mean_prod)


def gelu_tanh(values):
    inner = GELU_K * (values + GELU_C * values * values * values)
    return 0.5 * values * (1.0 + jnp.tanh(inner))


def silu_slope(values):
    sigm = jax.nn.sigmoid(values)
    return sigm * (1.0 + values * (1.0 - sigm))


def _nt(left, right):
    return lax.dot_general(
        left, right, (((1,), (1,)), ((), ())), preferred_element_type=jnp.float32
    )


def _nn(left, right):
    return jnp.dot(left, right, preferred_element_type=jnp.float32)


def _tn(left, right):
    return lax.dot_general(
        left, right, (((0,), (0,)), ((), ())), preferred_element_type=jnp.float32
    )


def halves(pair):
    lane = lax.broadcasted_iota(jnp.int32, (1, pair), 1)
    first = (lane < pair // 2).astype(jnp.float32)
    return first.astype(jnp.bfloat16), (1.0 - first).astype(jnp.bfloat16)


def load_plan(pieces, full, sems, me):
    qkv, proj, up, down = full
    shards = len(pieces)
    rows = qkv.shape[0] // shards
    width, triple, inner = proj.shape[1], qkv.shape[1], up.shape[1]
    ratio = down.shape[0] // (shards * rows)
    plan = [[], [], [], []]
    for j, piece in enumerate(pieces):
        own = me ^ j
        at = pl.ds(pl.multiple_of(own * rows, rows), rows)
        col = 0
        for n, (target, size) in enumerate(((qkv, triple), (proj, width), (up, inner))):
            plan[n].append(
                pltpu.make_async_copy(
                    piece.at[:, pl.ds(col, size)], target.at[at, :], sems.at[j, n]
                )
            )
            col += size
        for q in range(ratio):
            start = pl.multiple_of((own * ratio + q) * rows, rows)
            plan[3].append(
                pltpu.make_async_copy(
                    piece.at[:, pl.ds(col, width)], down.at[pl.ds(start, rows), :], sems.at[j, 3 + q]
                )
            )
            col += width
    return plan


def forward_kernel(
    shards, heads, info, resid, ada, biases, *rest
):
    pieces = rest[:shards]
    result, one_out, qkv_out, probs_out, mixed_out, attn_out, pre_out, branch_out = rest[
        shards : shards + 8
    ]
    w_qkv, w_proj, w_up, w_down, sems = rest[shards + 8 :]
    f32, bf16 = jnp.float32, jnp.bfloat16
    slot = pl.program_id(0)
    width, inner = w_proj.shape[1], w_up.shape[1]
    plan = load_plan(pieces, (w_qkv, w_proj, w_up, w_down), sems, info[1])

    @pl.when(slot == 0)
    def _():
        for group in plan:
            for copy in group:
                copy.start()
        for group in plan:
            for copy in group:
                copy.wait()

    @pl.when(slot < info[0])
    def _():
        mods = ada[0]
        value = resid[0]
        normed, _ = norm_rows(value)
        attn_in = (normed * (1.0 + mods[1:2]) + mods[0:1]).astype(bf16)
        qkv_out[0] = _nn(attn_in, w_qkv[...]).astype(bf16)
        pair = 2 * width // heads
        scale = 1.0 / (width // heads) ** 0.5
        masks = halves(pair)
        for p in range(heads // 2):
            query = qkv_out[0, :, p * pair : (p + 1) * pair]
            key = qkv_out[0, :, width + p * pair : width + (p + 1) * pair]
            val = qkv_out[0, :, 2 * width + p * pair : 2 * width + (p + 1) * pair]
            total = None
            for h in range(2):
                scores = _nt(query * masks[h], key) * scale
                expo = jnp.exp(scores - jnp.max(scores, axis=-1, keepdims=True))
                probs = (expo * (1.0 / jnp.sum(expo, axis=-1, keepdims=True))).astype(bf16)
                probs_out[0, 2 * p + h] = probs
                term = _nn(probs, val * masks[h])
                total = term if total is None else total + term
            mixed_out[0, :, p * pair : (p + 1) * pair] = total.astype(bf16)
        attn = _nn(mixed_out[0], w_proj[...]) + biases[:, :width]
        attn_out[0] = attn.astype(bf16)
        one = value + mods[2:3] * attn
        one_out[0] = one
        normed, _ = norm_rows(one)
        mlp_in = (normed * (1.0 + mods[4:5]) + mods[3:4]).astype(bf16)
        pre = _nn(mlp_in, w_up[...]) + biases[:, width : width + inner]
        pre_out[0] = pre
        hidden = gelu_tanh(pre).astype(bf16)
        branch = _nn(hidden, w_down[...]) + biases[:, width + inner :]
        branch_out[0] = branch.astype(bf16)
        result[0] = one + mods[5:6] * branch

    @pl.when(slot >= info[0])
    def _():
        result[0] = jnp.zeros_like(result[0])


def backward_kernel(shards, heads, info, grad, resid, one, ada, qkv, probs, mixed, attn, pre, branch, *rest):
    pieces = rest[:shards]
    grad_out, gada_out, bias_out, keep_out, send_out = rest[shards : shards + 5]
    w_qkv, w_proj, w_up, w_down, a_qkv, a_proj, a_up, a_down, g_heads, sems = rest[shards + 5 :]
    f32, bf16 = jnp.float32, jnp.bfloat16
    slot = pl.program_id(0)
    width, inner = w_proj.shape[1], w_up.shape[1]
    me = info[1]
    plan = load_plan(pieces, (w_qkv, w_proj, w_up, w_down), sems, me)

    @pl.when(slot == 0)
    def _():
        for group in plan:
            for copy in group:
                copy.start()
        a_qkv[...] = jnp.zeros_like(a_qkv)
        a_proj[...] = jnp.zeros_like(a_proj)
        a_up[...] = jnp.zeros_like(a_up)
        a_down[...] = jnp.zeros_like(a_down)
        bias_out[...] = jnp.zeros_like(bias_out)
        for group in plan:
            for copy in group:
                copy.wait()

    @pl.when(slot < info[0])
    def _():
        mods = ada[0]
        g = grad[0]
        gada_out[0, 5:6, :] = jnp.sum(g * branch[0].astype(f32), axis=0, keepdims=True)
        gbranch = g * mods[5:6]
        bias_out[:, width + inner :] += jnp.sum(gbranch, axis=0, keepdims=True)
        gb = gbranch.astype(bf16)
        u = pre[0]
        square = u * u
        tangent = jnp.tanh(GELU_K * (u + GELU_C * square * u))
        half = 0.5 * (1.0 + tangent)
        hidden = (u * half).astype(bf16)
        slope = half + 0.5 * u * (1.0 - tangent * tangent) * (
            GELU_K + (3.0 * GELU_C * GELU_K) * square
        )
        a_down[...] += _tn(hidden, gb)
        gpre = _nt(gb, w_down[...]) * slope
        bias_out[:, width : width + inner] += jnp.sum(gpre, axis=0, keepdims=True)
        gp = gpre.astype(bf16)
        normed, inv = norm_rows(one[0])
        mlp_in = (normed * (1.0 + mods[4:5]) + mods[3:4]).astype(bf16)
        a_up[...] += _tn(mlp_in, gp)
        gmlp = _nt(gp, w_up[...])
        gada_out[0, 3:4, :] = jnp.sum(gmlp, axis=0, keepdims=True)
        gada_out[0, 4:5, :] = jnp.sum(gmlp * normed, axis=0, keepdims=True)
        g1 = g + norm_back(normed, inv, gmlp * (1.0 + mods[4:5]))
        gada_out[0, 2:3, :] = jnp.sum(g1 * attn[0].astype(f32), axis=0, keepdims=True)
        gattn = g1 * mods[2:3]
        bias_out[:, :width] += jnp.sum(gattn, axis=0, keepdims=True)
        ga = gattn.astype(bf16)
        a_proj[...] += _tn(mixed[0], ga)
        gmixed = _nt(ga, w_proj[...]).astype(bf16)
        pair = 2 * width // heads
        scale = 1.0 / (width // heads) ** 0.5
        masks = halves(pair)
        for p in range(heads // 2):
            cut = slice(p * pair, (p + 1) * pair)
            query = qkv[0, :, p * pair : (p + 1) * pair]
            key = qkv[0, :, width + p * pair : width + (p + 1) * pair]
            val = qkv[0, :, 2 * width + p * pair : 2 * width + (p + 1) * pair]
            gm = gmixed[:, cut]
            gq, gk, gv = 0.0, 0.0, 0.0
            for h in range(2):
                low = probs[0, 2 * p + h]
                gm_h = gm * masks[h]
                gprobs = _nt(gm_h, val)
                wide = low.astype(f32)
                dot = jnp.sum(wide * gprobs, axis=-1, keepdims=True)
                gscores = (wide * (gprobs - dot) * scale).astype(bf16)
                gv = gv + _tn(low, gm_h)
                gq = gq + _nn(gscores, key * masks[h])
                gk = gk + _tn(gscores, query * masks[h])
            g_heads[:, p * pair : (p + 1) * pair] = gq.astype(bf16)
            g_heads[:, width + p * pair : width + (p + 1) * pair] = gk.astype(bf16)
            g_heads[:, 2 * width + p * pair : 2 * width + (p + 1) * pair] = gv.astype(bf16)
        normed, inv = norm_rows(resid[0])
        attn_in = (normed * (1.0 + mods[1:2]) + mods[0:1]).astype(bf16)
        a_qkv[...] += _tn(attn_in, g_heads[...])
        gin = _nt(g_heads[...], w_qkv[...])
        gada_out[0, 0:1, :] = jnp.sum(gin, axis=0, keepdims=True)
        gada_out[0, 1:2, :] = jnp.sum(gin * normed, axis=0, keepdims=True)
        grad_out[0] = g1 + norm_back(normed, inv, gin * (1.0 + mods[1:2]))

    @pl.when(slot >= info[0])
    def _():
        grad_out[0] = jnp.zeros_like(grad_out[0])
        gada_out[0] = jnp.zeros_like(gada_out[0])

    @pl.when(slot == pl.num_programs(0) - 1)
    def _():
        rows = a_qkv.shape[0] // shards
        ratio = a_down.shape[0] // (shards * rows)
        for j in range(shards):
            out = send_out if j & 1 else keep_out
            own = me ^ j
            at = pl.ds(pl.multiple_of(own * rows, rows), rows)
            col = 0
            for acc in (a_qkv, a_proj, a_up):
                size = acc.shape[1]
                out[j >> 1, :, col : col + size] = acc[at, :].astype(bf16)
                col += size
            for q in range(ratio):
                start = pl.multiple_of((own * ratio + q) * rows, rows)
                out[j >> 1, :, col : col + width] = a_down[pl.ds(start, rows), :].astype(bf16)
                col += width


def per_slot(shape):
    rest = (0,) * (len(shape) - 1)
    return pl.BlockSpec((1,) + tuple(shape[1:]), lambda slot, info: (slot,) + rest)


def whole_block(shape):
    zeros = (0,) * len(shape)
    return pl.BlockSpec(tuple(shape), lambda slot, info: zeros)


def forward_call(info, resid, ada, biases, pieces, dims):
    slots, length, width, triple, inner, heads = dims
    shards = len(pieces)
    f32, bf16 = jnp.float32, jnp.bfloat16
    shapes = [
        ((slots, length, width), f32),
        ((slots, length, width), f32),
        ((slots, length, triple), bf16),
        ((slots, heads, length, length), bf16),
        ((slots, length, width), bf16),
        ((slots, length, width), bf16),
        ((slots, length, inner), f32),
        ((slots, length, width), bf16),
    ]
    return pl.pallas_call(
        functools.partial(forward_kernel, shards, heads),
        out_shape=[jax.ShapeDtypeStruct(s, d) for s, d in shapes],
        grid_spec=pltpu.PrefetchScalarGridSpec(
            num_scalar_prefetch=1,
            grid=(slots,),
            in_specs=[per_slot(resid.shape), per_slot(ada.shape), whole_block(biases.shape)]
            + [pl.BlockSpec(memory_space=pl.ANY)] * shards,
            out_specs=[per_slot(s) for s, _ in shapes],
            scratch_shapes=[
                pltpu.VMEM((width, triple), bf16),
                pltpu.VMEM((width, width), bf16),
                pltpu.VMEM((width, inner), bf16),
                pltpu.VMEM((inner, width), bf16),
                pltpu.SemaphoreType.DMA((shards, 3 + inner // width)),
            ],
        ),
        compiler_params=pltpu.CompilerParams(vmem_limit_bytes=VMEM_GRANT),
        cost_estimate=pl.CostEstimate(
            flops=2 * slots * length * width * (triple + width + 2 * inner),
            bytes_accessed=slots * length * inner * 16,
            transcendentals=slots * length * (inner + heads * length),
        ),
        name="block_forward",
    )(info, resid, ada, biases, *pieces)


def backward_call(info, grad, resid, ada, saved, pieces, dims):
    slots, length, width, triple, inner, heads = dims
    one, qkv, probs, mixed, attn, pre, branch = saved
    shards = len(pieces)
    rows = width // shards
    f32, bf16 = jnp.float32, jnp.bfloat16
    columns = triple + width + 2 * inner
    half = (shards // 2, rows, columns)
    shapes = [
        ((slots, length, width), f32),
        (ada.shape, f32),
        ((1, 2 * width + inner), f32),
        (half, bf16),
        (half, bf16),
    ]
    args = (grad, resid, one, ada, qkv, probs, mixed, attn, pre, branch)
    return pl.pallas_call(
        functools.partial(backward_kernel, shards, heads),
        out_shape=[jax.ShapeDtypeStruct(s, d) for s, d in shapes],
        grid_spec=pltpu.PrefetchScalarGridSpec(
            num_scalar_prefetch=1,
            grid=(slots,),
            in_specs=[per_slot(a.shape) for a in args]
            + [pl.BlockSpec(memory_space=pl.ANY)] * shards,
            out_specs=[per_slot(shapes[0][0]), per_slot(ada.shape)]
            + [whole_block(s) for s, _ in shapes[2:]],
            scratch_shapes=[
                pltpu.VMEM((width, triple), bf16),
                pltpu.VMEM((width, width), bf16),
                pltpu.VMEM((width, inner), bf16),
                pltpu.VMEM((inner, width), bf16),
                pltpu.VMEM((width, triple), f32),
                pltpu.VMEM((width, width), f32),
                pltpu.VMEM((width, inner), f32),
                pltpu.VMEM((inner, width), f32),
                pltpu.VMEM((length, triple), bf16),
                pltpu.SemaphoreType.DMA((shards, 3 + inner // width)),
            ],
        ),
        compiler_params=pltpu.CompilerParams(vmem_limit_bytes=VMEM_GRANT),
        cost_estimate=pl.CostEstimate(
            flops=4 * slots * length * width * (triple + width + 2 * inner),
            bytes_accessed=slots * length * inner * 16,
            transcendentals=slots * length * inner,
        ),
        name="block_backward",
    )(info, *args, *pieces)


def bits_of(size):
    assert size & (size - 1) == 0
    return [1 << k for k in range(size.bit_length() - 1)]


def swap(value, axis, size, bit):
    return lax.ppermute(value, axis, [(i, i ^ bit) for i in range(size)])


def has_bit(axis, bit):
    return (lax.axis_index(axis) & bit) != 0


def gather_rel(value, axis, size):
    pieces = {0: value}
    for bit in reversed(bits_of(size)):
        for j in list(pieces):
            pieces[j ^ bit] = swap(pieces[j], axis, size, bit)
    return [pieces[j] for j in range(size)]


def to_absolute(pieces, axis):
    me = lax.axis_index(axis)
    out = jnp.zeros((len(pieces),) + pieces[0].shape, pieces[0].dtype)
    for j, piece in enumerate(pieces):
        out = lax.dynamic_update_index_in_dim(out, piece, me ^ j, 0)
    return out


def scatter_sum(blocks, axis, size, wire):
    blocks = dict(enumerate(blocks))
    for bit in bits_of(size):
        keep = [j for j in blocks if not j & bit]
        sent = jnp.concatenate([blocks[j | bit].astype(wire) for j in keep], axis=0)
        got = swap(sent, axis, size, bit)
        rows = got.shape[0] // len(keep)
        blocks = {
            j: blocks[j].astype(jnp.float32) + got[n * rows : (n + 1) * rows].astype(jnp.float32)
            for n, j in enumerate(keep)
        }
    return blocks[0]


def scatter_pair(kept, sent, axis, size, wire):
    got = swap(sent, axis, size, 1)
    count = kept.shape[0]
    blocks = [kept[n].astype(jnp.float32) + got[n].astype(jnp.float32) for n in range(count)]
    blocks = {n << 1: block for n, block in enumerate(blocks)}
    for bit in bits_of(size)[1:]:
        keep = [j for j in blocks if not j & bit]
        going = jnp.concatenate([blocks[j | bit].astype(wire) for j in keep], axis=0)
        back = swap(going, axis, size, bit)
        rows = back.shape[0] // len(keep)
        blocks = {
            j: blocks[j] + back[n * rows : (n + 1) * rows].astype(jnp.float32)
            for n, j in enumerate(keep)
        }
    return blocks[0]


def all_sum(value, axis, size, wire):
    bits = bits_of(size)
    trail = []
    for n, bit in enumerate(bits):
        width = value.shape[-1]
        if n < len(bits) - 1 and (width // 2) % 128 == 0:
            low, high = value[:, : width // 2], value[:, width // 2 :]
            upper = has_bit(axis, bit)
            sent = jnp.where(upper, low, high).astype(wire)
            kept = jnp.where(upper, high, low)
            value = kept.astype(jnp.float32) + swap(sent, axis, size, bit).astype(jnp.float32)
            trail.append(bit)
        else:
            low = value.astype(wire)
            value = low.astype(jnp.float32) + swap(low, axis, size, bit).astype(jnp.float32)
    if not trail:
        return value
    value = value.astype(wire)
    for bit in reversed(trail):
        other = swap(value, axis, size, bit)
        upper = has_bit(axis, bit)
        value = jnp.concatenate(
            [jnp.where(upper, other, value), jnp.where(upper, value, other)], axis=-1
        )
    return value.astype(jnp.float32)


def gather_all(value, stages):
    for axis, size, bit in stages:
        other = swap(value, axis, size, bit)
        upper = has_bit(axis, bit)
        value = jnp.concatenate(
            [jnp.where(upper, other, value), jnp.where(upper, value, other)], axis=0
        )
    return value


def pack_rows(qkv, proj, up, down):
    rows = qkv.shape[0]
    blocks = [down[n * rows : (n + 1) * rows] for n in range(down.shape[0] // rows)]
    return jnp.concatenate([qkv, proj, up] + blocks, axis=1)


def on_device(
    sizes,
    latents,
    conditioning,
    seq_counts,
    cotangent,
    ada_weight,
    ada_bias,
    qkv_weight,
    proj_weight,
    proj_bias,
    up_weight,
    up_bias,
    down_weight,
    down_bias,
):
    groups, shards = sizes
    bf16, f32 = jnp.bfloat16, jnp.float32
    slots, _, width = latents.shape
    rows = qkv_weight.shape[1]
    triple, inner = qkv_weight.shape[2], up_weight.shape[2]
    wide = ada_weight.shape[2]
    ratio = inner // width
    me = lax.axis_index("fsdp")

    packs = [
        pack_rows(qkv_weight[n], proj_weight[n], up_weight[n], down_weight[n])
        for n in range(LAYERS)
    ]
    pieces = [gather_rel(pack, "fsdp", shards) for pack in packs]

    act = jax.nn.silu(conditioning).astype(bf16)
    shard_bias = jnp.concatenate([ada_bias, proj_bias, up_bias, down_bias], axis=1)
    bias_width = shard_bias.shape[1]
    small = jnp.concatenate([act.reshape(-1), shard_bias.reshape(-1)])
    small = to_absolute(gather_rel(small, "fsdp", shards), "fsdp")
    act_group = small[:, : slots * width].reshape(shards * slots, width)
    biases = small[:, slots * width :].reshape(shards, LAYERS, bias_width)
    act_cols = lax.dynamic_slice(act_group, (0, me * rows), (shards * slots, rows))
    partial = jnp.stack(
        [jnp.dot(act_cols, ada_weight[n], preferred_element_type=f32) for n in range(LAYERS)]
    ).reshape(LAYERS, shards, slots, wide)
    blocks = [
        lax.dynamic_index_in_dim(partial, me ^ j, 1, keepdims=False).reshape(LAYERS * slots, wide)
        for j in range(shards)
    ]
    ada = scatter_sum(blocks, "fsdp", shards, f32).reshape(LAYERS, slots, wide)
    cut = [0]
    for part in (ada_bias, proj_bias, up_bias, down_bias):
        cut.append(cut[-1] + part.shape[1])
    bias_of = [
        [biases[:, n, cut[k] : cut[k + 1]].reshape(-1).astype(f32) for k in range(4)]
        for n in range(LAYERS)
    ]

    length = latents.shape[1]
    dims = (slots, length, width, triple, inner, HEADS)
    info = jnp.stack([seq_counts[0], me.astype(jnp.int32)])
    modulation, saved, inputs = [], [], []
    current = latents
    for n in range(LAYERS):
        ada_b, proj_b, up_b, down_b = bias_of[n]
        modulation.append((ada[n] + ada_b).reshape(slots, 6, width))
        row = jnp.concatenate([proj_b, up_b, down_b])[None]
        inputs.append(current)
        current, *kept = forward_call(info, current, modulation[n], row, pieces[n], dims)
        saved.append(kept)
    block_out = current
    grad = cotangent

    stages = [("dp", groups, bit) for bit in reversed(bits_of(groups))]
    stages += [("fsdp", shards, bit) for bit in reversed(bits_of(shards))]
    sums, gads, bias_rows = [None] * LAYERS, [None] * LAYERS, [None] * LAYERS
    acts = None
    for n in reversed(range(LAYERS)):
        grad, grad_ada, bias_row, stay, go = backward_call(
            info, grad, inputs[n], modulation[n], saved[n], pieces[n], dims
        )
        grad_ada = grad_ada.reshape(slots, wide)
        shard = scatter_pair(stay, go, "fsdp", shards, bf16)
        sums[n] = all_sum(shard, "dp", groups, bf16)
        rows_out = [grad_ada.astype(bf16), bias_row.astype(bf16)]
        if acts is None:
            flat = act.reshape(-1)
            flat = jnp.pad(flat, (0, -flat.shape[0] % wide)).reshape(-1, wide)
            rows_out.append(flat)
        message = jnp.concatenate(rows_out, axis=0)
        every = gather_all(message[None], stages)
        gads[n] = every[:, :slots]
        bias_rows[n] = every[:, slots]
        if acts is None:
            acts = every[:, slots + 1 :].reshape(every.shape[0], -1)[:, : slots * width]
            acts = acts.reshape(-1, width)

    acts_cols = lax.dynamic_slice(acts, (0, me * rows), (acts.shape[0], rows))
    g_ada = jnp.stack(
        [outer_total(acts_cols, gads[n].reshape(-1, wide)) for n in range(LAYERS)]
    )
    g_ada_bias = jnp.stack([jnp.sum(gads[n].astype(f32), axis=(0, 1)) for n in range(LAYERS)])
    g_bias = jnp.stack([jnp.sum(bias_rows[n].astype(f32), axis=0) for n in range(LAYERS)])

    place = jnp.int32(0)
    for k, bit in enumerate(reversed(bits_of(groups))):
        place = place + has_bit("dp", bit).astype(jnp.int32) * (1 << k)
    total = 0.0
    for n in range(LAYERS):
        grid = gads[n].reshape(shards, groups, slots, wide)
        mine = lax.dynamic_index_in_dim(grid, place, 1, keepdims=False).reshape(-1, wide)
        total = total + matmul_back(mine, ada_weight[n])
    total = total.reshape([2] * len(bits_of(shards)) + [slots, rows])
    order = tuple(reversed(range(len(bits_of(shards)))))
    total = total.transpose(order + (len(order), len(order) + 1)).reshape(shards, slots, rows)
    got = [lax.dynamic_index_in_dim(total, me, 0, keepdims=False)]
    for j in range(1, shards):
        sent = lax.dynamic_index_in_dim(total, me ^ j, 0, keepdims=False)
        got.append(swap(sent, "fsdp", shards, j))
    grad_cond = to_absolute(got, "fsdp").transpose(1, 0, 2).reshape(slots, width)
    grad_cond = grad_cond * silu_slope(conditioning)

    wide_sum = jnp.stack(sums)
    edge = [0, triple, triple + width, triple + width + inner]
    down_sum = wide_sum[:, :, edge[3] :].reshape(LAYERS, rows, ratio, width)
    own_inner = inner // shards
    return (
        block_out,
        grad,
        grad_cond,
        g_ada,
        lax.dynamic_slice_in_dim(g_ada_bias, me * (wide // shards), wide // shards, 1),
        wide_sum[:, :, : edge[1]],
        wide_sum[:, :, edge[1] : edge[2]],
        lax.dynamic_slice_in_dim(g_bias, me * rows, rows, 1),
        wide_sum[:, :, edge[2] : edge[3]],
        lax.dynamic_slice_in_dim(g_bias, width + me * own_inner, own_inner, 1),
        down_sum.transpose(0, 2, 1, 3).reshape(LAYERS, ratio * rows, width),
        lax.dynamic_slice_in_dim(g_bias, width + inner + me * rows, rows, 1),
    )


def solution(mesh):
    in_specs = (
        P(("dp", "fsdp"), None, None),
        P(("dp", "fsdp"), None),
        P(("dp", "fsdp")),
        P(("dp", "fsdp"), None, None),
        P(None, "fsdp", None),
        P(None, "fsdp"),
        P(None, "fsdp", None),
        P(None, "fsdp", None),
        P(None, "fsdp"),
        P(None, "fsdp", None),
        P(None, "fsdp"),
        P(None, "fsdp", None),
        P(None, "fsdp"),
    )
    out_specs = (
        P(("dp", "fsdp"), None, None),
        P(("dp", "fsdp"), None, None),
        P(("dp", "fsdp"), None),
        P(None, "fsdp", None),
        P(None, "fsdp"),
        P(None, "fsdp", None),
        P(None, "fsdp", None),
        P(None, "fsdp"),
        P(None, "fsdp", None),
        P(None, "fsdp"),
        P(None, "fsdp", None),
        P(None, "fsdp"),
    )
    return jax.shard_map(
        functools.partial(on_device, (mesh.shape["dp"], mesh.shape["fsdp"])), mesh=mesh, in_specs=in_specs, out_specs=out_specs, check_vma=False
    )
```

```python
import functools

import jax
import jax.numpy as jnp
from jax import lax
from jax.experimental import pallas as pl
from jax.experimental.pallas import tpu as pltpu
from jax.sharding import PartitionSpec as P


HEADS = 6
LAYERS = 2
VMEM_GRANT = 60 * 1024 * 1024


NORM_EPS = 1e-06
GELU_K = 0.7978845608028654
GELU_C = 0.044715


def matmul_back(left, right):
    flat = left.reshape(-1, left.shape[-1])
    return jnp.dot(flat, right.T, preferred_element_type=jnp.float32).reshape(
        left.shape[:-1] + (right.shape[0],)
    )


def outer_total(left, right):
    return jnp.dot(
        left.reshape(-1, left.shape[-1]).T,
        right.reshape(-1, right.shape[-1]),
        preferred_element_type=jnp.float32,
    )


def norm_rows(values):
    center = values - jnp.mean(values, axis=-1, keepdims=True)
    inv_std = lax.rsqrt(jnp.mean(center * center, axis=-1, keepdims=True) + NORM_EPS)
    return (center * inv_std, inv_std)


def norm_back(normed, inv_std, grad_normed):
    mean_grad = jnp.mean(grad_normed, axis=-1, keepdims=True)
    mean_prod = jnp.mean(grad_normed * normed, axis=-1, keepdims=True)
    return inv_std * (grad_normed - mean_grad - normed * mean_prod)


def silu_slope(values):
    sigm = jax.nn.sigmoid(values)
    return sigm * (1.0 + values * (1.0 - sigm))


def bits_of(size):
    assert size & (size - 1) == 0
    return [1 << k for k in range(size.bit_length() - 1)]


def swap(value, axis, size, bit):
    return lax.ppermute(value, axis, [(i, i ^ bit) for i in range(size)])


def has_bit(axis, bit):
    return (lax.axis_index(axis) & bit) != 0


def _nt(left, right):
    return lax.dot_general(
        left, right, (((1,), (1,)), ((), ())), preferred_element_type=jnp.float32
    )


def _nn(left, right):
    return jnp.dot(left, right, preferred_element_type=jnp.float32)


def _tn(left, right):
    return lax.dot_general(
        left, right, (((0,), (0,)), ((), ())), preferred_element_type=jnp.float32
    )


def lane_halves(pair):
    lane = lax.broadcasted_iota(jnp.int32, (1, pair), 1)
    first = (lane < pair // 2).astype(jnp.float32)
    return first.astype(jnp.bfloat16), (1.0 - first).astype(jnp.bfloat16)


def block_order(shards):
    bits = shards.bit_length() - 1
    return [sum(((n >> k) & 1) << (bits - 1 - k) for k in range(bits)) for n in range(shards)]


def attn_plan(pieces, w_qkv, w_proj, sems, me):
    rows = w_qkv.shape[0] // len(pieces)
    triple, width = w_qkv.shape[1], w_proj.shape[1]
    plan = [[], []]
    for j, piece in enumerate(pieces):
        at = pl.ds(pl.multiple_of((me ^ j) * rows, rows), rows)
        for n, (target, col, size) in enumerate(((w_qkv, 0, triple), (w_proj, triple, width))):
            source = piece.at[:, pl.ds(col, size)]
            plan[n].append(pltpu.make_async_copy(source, target.at[at, :], sems.at[j, n]))
    return plan


def mlp_plan(pieces, w_up, w_down, sems, me):
    rows = w_up.shape[0] // len(pieces)
    inner, width = w_down.shape
    ratio = inner // width
    plan = [[], []]
    for j, piece in enumerate(pieces):
        own = me ^ j
        at = pl.ds(pl.multiple_of(own * rows, rows), rows)
        source = piece.at[:, pl.ds(0, inner)]
        plan[0].append(pltpu.make_async_copy(source, w_up.at[at, :], sems.at[j, 0]))
        for q in range(ratio):
            at = pl.ds(pl.multiple_of((own * ratio + q) * rows, rows), rows)
            source = piece.at[:, pl.ds(inner + q * width, width)]
            plan[1].append(pltpu.make_async_copy(source, w_down.at[at, :], sems.at[j, 1 + q]))
    return plan


def start_all(plan):
    for group in plan:
        for copy in group:
            copy.start()


def wait_first(slot, group):
    @pl.when(slot == 0)
    def _():
        for copy in group:
            copy.wait()


def forward_body(slot, heads, value, mods, biases, weights, plans, saved):
    w_qkv, w_proj, w_up, w_down = weights
    one_out, qkv, probs_out, mixed, attn_out, hidden_out, slope_out, branch_out = saved
    bf16 = jnp.bfloat16
    width, inner = w_proj.shape[1], w_up.shape[1]
    normed, _ = norm_rows(value)
    attn_in = (normed * (1.0 + mods[1:2]) + mods[0:1]).astype(bf16)
    wait_first(slot, plans[0][0])
    qkv[...] = _nn(attn_in, w_qkv[...]).astype(bf16)
    pair = 2 * width // heads
    scale = 1.0 / (width // heads) ** 0.5
    masks = lane_halves(pair)
    for p in range(heads // 2):
        query = qkv[:, p * pair : (p + 1) * pair]
        key = qkv[:, width + p * pair : width + (p + 1) * pair]
        val = qkv[:, 2 * width + p * pair : 2 * width + (p + 1) * pair]
        total = None
        for h in range(2):
            scores = _nt(query * masks[h], key) * scale
            expo = jnp.exp(scores - jnp.max(scores, axis=-1, keepdims=True))
            probs = (expo * (1.0 / jnp.sum(expo, axis=-1, keepdims=True))).astype(bf16)
            probs_out[2 * p + h] = probs
            term = _nn(probs, val * masks[h])
            total = term if total is None else total + term
        mixed[:, p * pair : (p + 1) * pair] = total.astype(bf16)
    wait_first(slot, plans[0][1])
    attn = _nn(mixed[...], w_proj[...]) + biases[:, :width]
    attn_out[...] = attn.astype(bf16)
    one = value + mods[2:3] * attn
    one_out[...] = one
    normed, _ = norm_rows(one)
    mlp_in = (normed * (1.0 + mods[4:5]) + mods[3:4]).astype(bf16)
    wait_first(slot, plans[1][0])
    u = _nn(mlp_in, w_up[...]) + biases[:, width : width + inner]
    square = u * u
    tangent = jnp.tanh(GELU_K * (u + GELU_C * square * u))
    half = 0.5 * (1.0 + tangent)
    hidden_out[...] = (u * half).astype(bf16)
    slope = half + 0.5 * u * (1.0 - tangent * tangent) * (
        GELU_K + (3.0 * GELU_C * GELU_K) * square
    )
    slope_out[...] = slope.astype(bf16)
    wait_first(slot, plans[1][1])
    branch = _nn(hidden_out[...], w_down[...]) + biases[:, width + inner :]
    branch_out[...] = branch.astype(bf16)
    return one + mods[5:6] * branch


def mlp_back_body(slot, g, mods, one, hidden, slope, branch, weights, plan, sums, gada, bias_up, bias_down):
    w_up, w_down = weights
    a_up, a_down = sums
    f32, bf16 = jnp.float32, jnp.bfloat16
    gada[2:3, :] = jnp.sum(g * branch[...].astype(f32), axis=0, keepdims=True)
    gbranch = g * mods[5:6]
    bias_down[...] += jnp.sum(gbranch, axis=0, keepdims=True)
    gb = gbranch.astype(bf16)
    a_down[...] += _tn(hidden[...], gb)
    wait_first(slot, plan[1])
    gpre = _nt(gb, w_down[...]) * slope[...].astype(f32)
    bias_up[...] += jnp.sum(gpre, axis=0, keepdims=True)
    gp = gpre.astype(bf16)
    normed, inv = norm_rows(one[...])
    mlp_in = (normed * (1.0 + mods[4:5]) + mods[3:4]).astype(bf16)
    a_up[...] += _tn(mlp_in, gp)
    wait_first(slot, plan[0])
    gmlp = _nt(gp, w_up[...])
    gada[0:1, :] = jnp.sum(gmlp, axis=0, keepdims=True)
    gada[1:2, :] = jnp.sum(gmlp * normed, axis=0, keepdims=True)
    return g + norm_back(normed, inv, gmlp * (1.0 + mods[4:5]))


def attn_back_body(slot, heads, g1, mods, resid, qkv, probs, mixed, attn, weights, plan, sums, g_heads, gada, bias_proj):
    w_qkv, w_proj = weights
    a_qkv, a_proj = sums
    f32, bf16 = jnp.float32, jnp.bfloat16
    width = w_proj.shape[1]
    gada[2:3, :] = jnp.sum(g1 * attn[...].astype(f32), axis=0, keepdims=True)
    gattn = g1 * mods[2:3]
    bias_proj[...] += jnp.sum(gattn, axis=0, keepdims=True)
    ga = gattn.astype(bf16)
    a_proj[...] += _tn(mixed[...], ga)
    wait_first(slot, plan[1])
    gmixed = _nt(ga, w_proj[...]).astype(bf16)
    pair = 2 * width // heads
    scale = 1.0 / (width // heads) ** 0.5
    masks = lane_halves(pair)
    for p in range(heads // 2):
        query = qkv[:, p * pair : (p + 1) * pair]
        key = qkv[:, width + p * pair : width + (p + 1) * pair]
        val = qkv[:, 2 * width + p * pair : 2 * width + (p + 1) * pair]
        gm = gmixed[:, p * pair : (p + 1) * pair]
        gq, gk, gv = 0.0, 0.0, 0.0
        for h in range(2):
            low = probs[2 * p + h]
            gm_h = gm * masks[h]
            gprobs = _nt(gm_h, val)
            full = low.astype(f32)
            dot = jnp.sum(full * gprobs, axis=-1, keepdims=True)
            gscores = (full * (gprobs - dot) * scale).astype(bf16)
            gv = gv + _tn(low, gm_h)
            gq = gq + _nn(gscores, key * masks[h])
            gk = gk + _tn(gscores, query * masks[h])
        g_heads[:, p * pair : (p + 1) * pair] = gq.astype(bf16)
        g_heads[:, width + p * pair : width + (p + 1) * pair] = gk.astype(bf16)
        g_heads[:, 2 * width + p * pair : 2 * width + (p + 1) * pair] = gv.astype(bf16)
    normed, inv = norm_rows(resid)
    attn_in = (normed * (1.0 + mods[1:2]) + mods[0:1]).astype(bf16)
    a_qkv[...] += _tn(attn_in, g_heads[...])
    wait_first(slot, plan[0])
    gin = _nt(g_heads[...], w_qkv[...])
    gada[0:1, :] = jnp.sum(gin, axis=0, keepdims=True)
    gada[1:2, :] = jnp.sum(gin * normed, axis=0, keepdims=True)
    return g1 + norm_back(normed, inv, gin * (1.0 + mods[1:2]))


def emit_attn(shards, me, a_qkv, a_proj, keep, send):
    rows, triple = a_qkv.shape[0] // shards, a_qkv.shape[1]
    for n, j in enumerate(block_order(shards)):
        out, row = (keep, n) if n < shards // 2 else (send, n - shards // 2)
        at = pl.ds(pl.multiple_of((me ^ j) * rows, rows), rows)
        out[row, :, :triple] = a_qkv[at, :].astype(jnp.bfloat16)
        out[row, :, triple:] = a_proj[at, :].astype(jnp.bfloat16)


def emit_mlp(shards, me, a_up, a_down, keep, send):
    rows, inner = a_up.shape[0] // shards, a_up.shape[1]
    width = a_down.shape[1]
    ratio = inner // width
    for n, j in enumerate(block_order(shards)):
        out, row = (keep, n) if n < shards // 2 else (send, n - shards // 2)
        own = me ^ j
        at = pl.ds(pl.multiple_of(own * rows, rows), rows)
        out[row, :, :inner] = a_up[at, :].astype(jnp.bfloat16)
        for q in range(ratio):
            at = pl.ds(pl.multiple_of((own * ratio + q) * rows, rows), rows)
            col = inner + q * width
            out[row, :, col : col + width] = a_down[at, :].astype(jnp.bfloat16)


def clear(*refs):
    for ref in refs:
        ref[...] = jnp.zeros_like(ref[...])


def forward_kernel(shards, heads, info, resid, ada, biases, *rest):
    attn_pieces, mlp_pieces, rest = rest[:shards], rest[shards : 2 * shards], rest[2 * shards :]
    result, saved, rest = rest[0], rest[1:9], rest[9:]
    w_qkv, w_proj, w_up, w_down, attn_sems, mlp_sems = rest
    slot = pl.program_id(0)
    plans = (
        attn_plan(attn_pieces, w_qkv, w_proj, attn_sems, info[1]),
        mlp_plan(mlp_pieces, w_up, w_down, mlp_sems, info[1]),
    )

    @pl.when(slot == 0)
    def _():
        start_all(plans[0])
        start_all(plans[1])

    @pl.when(slot < info[0])
    def _():
        result[0] = forward_body(
            slot,
            heads,
            resid[0],
            ada[0],
            biases,
            (w_qkv, w_proj, w_up, w_down),
            plans,
            [ref.at[0] for ref in saved],
        )

    @pl.when(slot >= info[0])
    def _():
        clear(result)


def last_block_kernel(shards, heads, info, resid, grad, ada, biases, *rest):
    attn_pieces, mlp_pieces, rest = rest[:shards], rest[shards : 2 * shards], rest[2 * shards :]
    result, grad_out, gada_attn, gada_mlp, bias_proj, bias_up, bias_down = rest[:7]
    attn_keep, attn_send, mlp_keep, mlp_send = rest[7:11]
    w_qkv, w_proj, w_up, w_down, a_qkv, a_proj, a_up, a_down, g_heads = rest[11:20]
    saved, attn_sems, mlp_sems = rest[20:28], rest[28], rest[29]
    one, qkv, probs, mixed, attn, hidden, slope, branch = saved
    slot, me = pl.program_id(0), info[1]
    plans = (
        attn_plan(attn_pieces, w_qkv, w_proj, attn_sems, me),
        mlp_plan(mlp_pieces, w_up, w_down, mlp_sems, me),
    )
    done = [[], []]

    @pl.when(slot == 0)
    def _():
        start_all(plans[0])
        start_all(plans[1])
        clear(a_qkv, a_proj, a_up, a_down, bias_proj, bias_up, bias_down)

    @pl.when(slot < info[0])
    def _():
        mods, value = ada[0], resid[0]
        weights = (w_qkv, w_proj, w_up, w_down)
        result[0] = forward_body(slot, heads, value, mods, biases, weights, plans, saved)
        g1 = mlp_back_body(
            slot, grad[0], mods, one, hidden, slope, branch, weights[2:], done, (a_up, a_down),
            gada_mlp.at[0], bias_up, bias_down,
        )
        grad_out[0] = attn_back_body(
            slot, heads, g1, mods, value, qkv, probs, mixed, attn, weights[:2], done,
            (a_qkv, a_proj), g_heads, gada_attn.at[0], bias_proj,
        )

    @pl.when(slot >= info[0])
    def _():
        clear(result, grad_out, gada_attn, gada_mlp)

    @pl.when(slot == pl.num_programs(0) - 1)
    def _():
        emit_attn(shards, me, a_qkv, a_proj, attn_keep, attn_send)
        emit_mlp(shards, me, a_up, a_down, mlp_keep, mlp_send)


def mlp_back_kernel(shards, heads, info, grad, ada, one, hidden, slope, branch, *rest):
    pieces, rest = rest[:shards], rest[shards:]
    grad_out, gada, bias_up, bias_down, keep, send, w_up, w_down, a_up, a_down, sems = rest
    slot, me = pl.program_id(0), info[1]
    plan = mlp_plan(pieces, w_up, w_down, sems, me)

    @pl.when(slot == 0)
    def _():
        start_all(plan)
        clear(a_up, a_down, bias_up, bias_down)

    @pl.when(slot < info[0])
    def _():
        grad_out[0] = mlp_back_body(
            slot, grad[0], ada[0], one.at[0], hidden.at[0], slope.at[0], branch.at[0],
            (w_up, w_down), plan, (a_up, a_down), gada.at[0], bias_up, bias_down,
        )

    @pl.when(slot >= info[0])
    def _():
        clear(gada)

    @pl.when(slot == pl.num_programs(0) - 1)
    def _():
        emit_mlp(shards, me, a_up, a_down, keep, send)


def attn_back_kernel(shards, heads, info, grad, resid, ada, qkv, probs, mixed, attn, *rest):
    pieces, rest = rest[:shards], rest[shards:]
    grad_out, gada, bias_proj, keep, send, w_qkv, w_proj, a_qkv, a_proj, g_heads, sems = rest
    slot, me = pl.program_id(0), info[1]
    plan = attn_plan(pieces, w_qkv, w_proj, sems, me)

    @pl.when(slot == 0)
    def _():
        start_all(plan)
        clear(a_qkv, a_proj, bias_proj)

    @pl.when(slot < info[0])
    def _():
        grad_out[0] = attn_back_body(
            slot, heads, grad[0], ada[0], resid[0], qkv.at[0], probs.at[0], mixed.at[0],
            attn.at[0], (w_qkv, w_proj), plan, (a_qkv, a_proj), g_heads, gada.at[0], bias_proj,
        )

    @pl.when(slot >= info[0])
    def _():
        clear(grad_out, gada)

    @pl.when(slot == pl.num_programs(0) - 1)
    def _():
        emit_attn(shards, me, a_qkv, a_proj, keep, send)


def per_slot(shape):
    rest = (0,) * (len(shape) - 1)
    return pl.BlockSpec((1,) + tuple(shape[1:]), lambda slot, info: (slot,) + rest)


def whole_block(shape):
    zeros = (0,) * len(shape)
    return pl.BlockSpec(tuple(shape), lambda slot, info: zeros)


def run_kernel(kernel, dims, info, blocked, fixed, pieces, outs, fixed_outs, scratch, passes):
    slots, length, width, triple, inner, heads, shards = dims
    shapes = list(outs) + list(fixed_outs)
    return pl.pallas_call(
        functools.partial(kernel, shards, heads),
        out_shape=[jax.ShapeDtypeStruct(s, d) for s, d in shapes],
        grid_spec=pltpu.PrefetchScalarGridSpec(
            num_scalar_prefetch=1,
            grid=(slots,),
            in_specs=[per_slot(a.shape) for a in blocked]
            + [whole_block(a.shape) for a in fixed]
            + [pl.BlockSpec(memory_space=pl.ANY)] * len(pieces),
            out_specs=[per_slot(s) for s, _ in outs] + [whole_block(s) for s, _ in fixed_outs],
            scratch_shapes=scratch,
        ),
        compiler_params=pltpu.CompilerParams(vmem_limit_bytes=VMEM_GRANT),
        cost_estimate=pl.CostEstimate(
            flops=passes * slots * length * width * (triple + width + 2 * inner),
            bytes_accessed=passes * slots * length * inner * 4,
            transcendentals=slots * length * inner,
        ),
    )(info, *blocked, *fixed, *pieces)


def kernel_parts(dims):
    slots, length, width, triple, inner, heads, shards = dims
    f32, bf16 = jnp.float32, jnp.bfloat16
    rows, ratio = width // shards, inner // width
    saved = [
        ((length, width), f32),
        ((length, triple), bf16),
        ((heads, length, length), bf16),
        ((length, width), bf16),
        ((length, width), bf16),
        ((length, inner), bf16),
        ((length, inner), bf16),
        ((length, width), bf16),
    ]
    w_attn = [pltpu.VMEM((width, triple), bf16), pltpu.VMEM((width, width), bf16)]
    w_mlp = [pltpu.VMEM((width, inner), bf16), pltpu.VMEM((inner, width), bf16)]
    a_attn = [pltpu.VMEM((width, triple), f32), pltpu.VMEM((width, width), f32)]
    a_mlp = [pltpu.VMEM((width, inner), f32), pltpu.VMEM((inner, width), f32)]
    heads_buf = [pltpu.VMEM((length, triple), bf16)]
    sems = [pltpu.SemaphoreType.DMA((shards, 2)), pltpu.SemaphoreType.DMA((shards, 1 + ratio))]
    rows_of = ((slots, length, width), f32)
    gada = ((slots, 3, width), f32)
    bias = [((1, width), f32), ((1, inner), f32), ((1, width), f32)]
    half = (shards // 2, rows)
    out_attn = [(half + (triple + width,), bf16)] * 2
    out_mlp = [(half + (2 * inner,), bf16)] * 2
    return saved, w_attn, w_mlp, a_attn, a_mlp, heads_buf, sems, rows_of, gada, bias, out_attn, out_mlp


def forward_call(dims, info, resid, ada, biases, attn_pieces, mlp_pieces):
    saved, w_attn, w_mlp, _, _, _, sems, rows_of, *_ = kernel_parts(dims)
    outs = [rows_of] + [((dims[0],) + s, d) for s, d in saved]
    return run_kernel(
        forward_kernel, dims, info, (resid, ada), (biases,),
        attn_pieces + mlp_pieces, outs, [], w_attn + w_mlp + sems, 2,
    )


def last_block_call(dims, info, resid, grad, ada, biases, attn_pieces, mlp_pieces):
    parts = kernel_parts(dims)
    saved, w_attn, w_mlp, a_attn, a_mlp, heads_buf, sems, rows_of, gada, bias, out_attn, out_mlp = parts
    scratch = w_attn + w_mlp + a_attn + a_mlp + heads_buf
    scratch += [pltpu.VMEM(s, d) for s, d in saved] + sems
    return run_kernel(
        last_block_kernel, dims, info, (resid, grad, ada), (biases,),
        attn_pieces + mlp_pieces, [rows_of, rows_of, gada, gada], bias + out_attn + out_mlp,
        scratch, 6,
    )


def mlp_back_call(dims, info, grad, ada, one, hidden, slope, branch, pieces):
    parts = kernel_parts(dims)
    _, _, w_mlp, _, a_mlp, _, sems, rows_of, gada, bias, _, out_mlp = parts
    return run_kernel(
        mlp_back_kernel, dims, info, (grad, ada, one, hidden, slope, branch), (),
        pieces, [rows_of, gada], bias[1:] + out_mlp, w_mlp + a_mlp + sems[1:], 2,
    )


def attn_back_call(dims, info, grad, resid, ada, qkv, probs, mixed, attn, pieces):
    parts = kernel_parts(dims)
    _, w_attn, _, a_attn, _, heads_buf, sems, rows_of, gada, bias, out_attn, _ = parts
    return run_kernel(
        attn_back_kernel, dims, info,
        (grad, resid, ada, qkv, probs, mixed, attn), (), pieces, [rows_of, gada],
        bias[:1] + out_attn, w_attn + a_attn + heads_buf + sems[:1], 2,
    )


def gather_rel(value, axis, size):
    pieces = {0: value}
    for bit in reversed(bits_of(size)):
        for j in list(pieces):
            pieces[j ^ bit] = swap(pieces[j], axis, size, bit)
    return [pieces[j] for j in range(size)]


def gather_all(value, stages):
    for axis, size, bit in stages:
        other = swap(value, axis, size, bit)
        upper = has_bit(axis, bit)
        value = jnp.concatenate(
            [jnp.where(upper, other, value), jnp.where(upper, value, other)], axis=0
        )
    return value


def to_absolute(pieces, axis):
    me = lax.axis_index(axis)
    out = jnp.zeros((len(pieces),) + pieces[0].shape, pieces[0].dtype)
    for j, piece in enumerate(pieces):
        out = lax.dynamic_update_index_in_dim(out, piece, me ^ j, 0)
    return out


def scatter_sum(blocks, axis, size):
    blocks = dict(enumerate(blocks))
    for bit in bits_of(size):
        keep = [j for j in blocks if not j & bit]
        got = swap(jnp.stack([blocks[j | bit] for j in keep]), axis, size, bit)
        blocks = {j: blocks[j] + got[n] for n, j in enumerate(keep)}
    return blocks[0]


def reduce_message(kept, sent, plan):
    f32, wire = jnp.float32, kept.dtype
    value, trail = kept, []
    for n, (axis, size, bit, kind) in enumerate(plan):
        if kind == "rows":
            if n == 0:
                stay, go = kept, sent
            else:
                half = value.shape[0] // 2
                stay, go = value[:half], value[half:]
        elif kind == "columns":
            half = value.shape[-1] // 2
            upper = has_bit(axis, bit)
            low, high = value[..., :half], value[..., half:]
            stay, go = jnp.where(upper, high, low), jnp.where(upper, low, high)
            trail.append((axis, size, bit))
        else:
            stay, go = value, value
        got = swap(go, axis, size, bit)
        value = (stay.astype(f32) + got.astype(f32)).astype(wire)
    value = value[0]
    for axis, size, bit in reversed(trail):
        other = swap(value, axis, size, bit)
        upper = has_bit(axis, bit)
        value = jnp.concatenate(
            [jnp.where(upper, other, value), jnp.where(upper, value, other)], axis=-1
        )
    return value


def message_plan(groups, shards, columns, dp_early):
    shard_stages = [("fsdp", shards, bit, "rows") for bit in bits_of(shards)]
    group_stages = []
    for bit in bits_of(groups):
        if 2 * bit < groups and (columns // 2) % 128 == 0:
            columns //= 2
            group_stages.append(("dp", groups, bit, "columns"))
        else:
            group_stages.append(("dp", groups, bit, "full"))
    if dp_early:
        return shard_stages[:1] + group_stages[:1] + shard_stages[1:] + group_stages[1:]
    return shard_stages + group_stages


def on_device(
    sizes,
    latents,
    conditioning,
    seq_counts,
    cotangent,
    ada_weight,
    ada_bias,
    qkv_weight,
    proj_weight,
    proj_bias,
    up_weight,
    up_bias,
    down_weight,
    down_bias,
):
    groups, shards = sizes
    bf16, f32 = jnp.bfloat16, jnp.float32
    slots, length, width = latents.shape
    rows = qkv_weight.shape[1]
    triple, inner = qkv_weight.shape[2], up_weight.shape[2]
    wide = ada_weight.shape[2]
    ratio = inner // width
    me = lax.axis_index("fsdp")
    shard_stages = [("fsdp", shards, bit) for bit in bits_of(shards)]

    act = jax.nn.silu(conditioning).astype(bf16)
    shard_bias = jnp.concatenate([ada_bias, proj_bias, up_bias, down_bias], axis=1)
    bias_width = shard_bias.shape[1]
    small = jnp.concatenate([act.reshape(-1), shard_bias.reshape(-1)])[None]
    small = gather_all(small, shard_stages)

    attn_pieces, mlp_pieces = [], []
    for n in range(LAYERS):
        pack = jnp.concatenate([qkv_weight[n], proj_weight[n]], axis=1)
        attn_pieces.append(gather_rel(pack, "fsdp", shards))
        blocks = [down_weight[n, q * rows : (q + 1) * rows] for q in range(ratio)]
        pack = jnp.concatenate([up_weight[n]] + blocks, axis=1)
        mlp_pieces.append(gather_rel(pack, "fsdp", shards))

    act_group = small[:, : slots * width].reshape(shards * slots, width)
    biases = small[:, slots * width :].reshape(shards, LAYERS, bias_width)
    act_cols = lax.dynamic_slice(act_group, (0, me * rows), (shards * slots, rows))
    partial = jnp.stack(
        [jnp.dot(act_cols, ada_weight[n], preferred_element_type=f32) for n in range(LAYERS)]
    ).reshape(LAYERS, shards, slots, wide)
    blocks = [
        lax.dynamic_index_in_dim(partial, me ^ j, 1, keepdims=False).reshape(LAYERS * slots, wide)
        for j in range(shards)
    ]
    ada = scatter_sum(blocks, "fsdp", shards).reshape(LAYERS, slots, wide)
    cut = [0]
    for part in (ada_bias, proj_bias, up_bias, down_bias):
        cut.append(cut[-1] + part.shape[1])
    bias_of = [
        [biases[:, n, cut[k] : cut[k + 1]].reshape(-1).astype(f32) for k in range(4)]
        for n in range(LAYERS)
    ]
    modulation = [(ada[n] + bias_of[n][0]).reshape(slots, 6, width) for n in range(LAYERS)]
    bias_rows = [jnp.concatenate(bias_of[n][1:])[None] for n in range(LAYERS)]

    dims = (slots, length, width, triple, inner, HEADS, shards)
    info = jnp.stack([seq_counts[0], me.astype(jnp.int32)])
    top = LAYERS - 1
    inputs, saved = [], []
    current = latents
    for n in range(top):
        inputs.append(current)
        current, *kept = forward_call(
            dims, info, current, modulation[n], bias_rows[n], attn_pieces[n], mlp_pieces[n]
        )
        saved.append(kept)
    sums = [None] * LAYERS
    small_rows = [None] * LAYERS
    attn_stages = message_plan(groups, shards, triple + width, True)
    mlp_stages = message_plan(groups, shards, 2 * inner, False)

    def reduce_layer(n, attn_pair, mlp_pair):
        mlp = reduce_message(*mlp_pair, mlp_stages)
        attn = reduce_message(*attn_pair, attn_stages)
        sums[n] = (attn, mlp)

    def note_rows(n, gada_attn, gada_mlp, bias_grads):
        flat = jnp.concatenate([gada_attn, gada_mlp], axis=1).reshape(slots, wide)
        small_rows[n] = jnp.concatenate([flat, jnp.concatenate(bias_grads, axis=1)], axis=0)

    outs = last_block_call(
        dims, info, current, cotangent, modulation[top], bias_rows[top],
        attn_pieces[top], mlp_pieces[top],
    )
    block_out, grad, gada_attn, gada_mlp, b_proj, b_up, b_down = outs[:7]
    reduce_layer(top, outs[7:9], outs[9:11])
    note_rows(top, gada_attn, gada_mlp, (b_proj, b_up, b_down))
    for n in reversed(range(top)):
        one, qkv, probs, mixed, attn, hidden, slope, branch = saved[n]
        g1, gada_mlp, b_up, b_down, *mlp_pair = mlp_back_call(
            dims, info, grad, modulation[n], one, hidden, slope, branch, mlp_pieces[n]
        )
        grad, gada_attn, b_proj, *attn_pair = attn_back_call(
            dims, info, g1, inputs[n], modulation[n], qkv, probs, mixed, attn, attn_pieces[n]
        )
        reduce_layer(n, attn_pair, mlp_pair)
        note_rows(n, gada_attn, gada_mlp, (b_proj, b_up, b_down))

    flat = act.reshape(-1)
    flat = jnp.pad(flat, (0, -flat.shape[0] % wide)).reshape(-1, wide)
    message = jnp.concatenate([row.astype(bf16) for row in small_rows] + [flat], axis=0)
    stages = [("dp", groups, bit) for bit in reversed(bits_of(groups))]
    stages += [("fsdp", shards, bit) for bit in reversed(bits_of(shards))]
    every = gather_all(message[None], stages)
    per_layer = slots + 1
    gads = [every[:, n * per_layer : n * per_layer + slots] for n in range(LAYERS)]
    acts = every[:, LAYERS * per_layer :].reshape(every.shape[0], -1)[:, : slots * width]
    acts = acts.reshape(-1, width)
    acts_cols = lax.dynamic_slice(acts, (0, me * rows), (acts.shape[0], rows))
    g_ada = jnp.stack([outer_total(acts_cols, gads[n].reshape(-1, wide)) for n in range(LAYERS)])
    totals = jnp.sum(every[:, : LAYERS * per_layer].astype(f32), axis=0)
    totals = totals.reshape(LAYERS, per_layer, wide)
    g_ada_bias = jnp.sum(totals[:, :slots], axis=1)
    g_bias = totals[:, slots]

    place = jnp.int32(0)
    for k, bit in enumerate(reversed(bits_of(groups))):
        place = place + has_bit("dp", bit).astype(jnp.int32) * (1 << k)
    grid = every.reshape((shards, groups) + every.shape[1:])
    mine = lax.dynamic_index_in_dim(grid, place, 1, keepdims=False)
    total = 0.0
    for n in range(LAYERS):
        part = mine[:, n * per_layer : n * per_layer + slots].reshape(-1, wide)
        total = total + matmul_back(part, ada_weight[n])
    total = total.reshape([2] * len(bits_of(shards)) + [slots, rows])
    order = tuple(reversed(range(len(bits_of(shards)))))
    total = total.transpose(order + (len(order), len(order) + 1)).reshape(shards, slots, rows)
    got = [lax.dynamic_index_in_dim(total, me, 0, keepdims=False)]
    for j in range(1, shards):
        sent = lax.dynamic_index_in_dim(total, me ^ j, 0, keepdims=False)
        got.append(swap(sent, "fsdp", shards, j))
    grad_cond = to_absolute(got, "fsdp").transpose(1, 0, 2).reshape(slots, width)
    grad_cond = grad_cond * silu_slope(conditioning)

    def stacked(k, first, last):
        return jnp.stack([sums[n][k][:, first:last] for n in range(LAYERS)]).astype(f32)

    down_sum = jnp.stack(
        [
            jnp.concatenate(
                [
                    sums[n][1][:, inner + q * width : inner + (q + 1) * width]
                    for q in range(ratio)
                ],
                axis=0,
            )
            for n in range(LAYERS)
        ]
    ).astype(f32)
    own_inner = inner // shards
    return (
        block_out,
        grad,
        grad_cond,
        g_ada,
        lax.dynamic_slice_in_dim(g_ada_bias, me * (wide // shards), wide // shards, 1),
        stacked(0, 0, triple),
        stacked(0, triple, triple + width),
        lax.dynamic_slice_in_dim(g_bias, me * rows, rows, 1),
        stacked(1, 0, inner),
        lax.dynamic_slice_in_dim(g_bias, width + me * own_inner, own_inner, 1),
        down_sum,
        lax.dynamic_slice_in_dim(g_bias, width + inner + me * rows, rows, 1),
    )


def solution(mesh):
    in_specs = (
        P(("dp", "fsdp"), None, None),
        P(("dp", "fsdp"), None),
        P(("dp", "fsdp")),
        P(("dp", "fsdp"), None, None),
        P(None, "fsdp", None),
        P(None, "fsdp"),
        P(None, "fsdp", None),
        P(None, "fsdp", None),
        P(None, "fsdp"),
        P(None, "fsdp", None),
        P(None, "fsdp"),
        P(None, "fsdp", None),
        P(None, "fsdp"),
    )
    out_specs = (
        P(("dp", "fsdp"), None, None),
        P(("dp", "fsdp"), None, None),
        P(("dp", "fsdp"), None),
        P(None, "fsdp", None),
        P(None, "fsdp"),
        P(None, "fsdp", None),
        P(None, "fsdp", None),
        P(None, "fsdp"),
        P(None, "fsdp", None),
        P(None, "fsdp"),
        P(None, "fsdp", None),
        P(None, "fsdp"),
    )
    sizes = (mesh.shape["dp"], mesh.shape["fsdp"])
    return jax.shard_map(
        functools.partial(on_device, sizes),
        mesh=mesh,
        in_specs=in_specs,
        out_specs=out_specs,
        check_vma=False,
    )
```

```python
import functools

import jax
import jax.numpy as jnp
from jax import lax
from jax.experimental import pallas as pl
from jax.experimental.pallas import tpu as pltpu
from jax.sharding import PartitionSpec as P


HEADS = 6
LAYERS = 2
VMEM_GRANT = 60 * 1024 * 1024


NORM_EPS = 1e-06
GELU_K = 0.7978845608028654
GELU_C = 0.044715


def matmul_back(left, right):
    flat = left.reshape(-1, left.shape[-1])
    return jnp.dot(flat, right.T, preferred_element_type=jnp.float32).reshape(
        left.shape[:-1] + (right.shape[0],)
    )


def outer_total(left, right):
    return jnp.dot(
        left.reshape(-1, left.shape[-1]).T,
        right.reshape(-1, right.shape[-1]),
        preferred_element_type=jnp.float32,
    )


def norm_rows(values):
    center = values - jnp.mean(values, axis=-1, keepdims=True)
    inv_std = lax.rsqrt(jnp.mean(center * center, axis=-1, keepdims=True) + NORM_EPS)
    return (center * inv_std, inv_std)


def norm_back(normed, inv_std, grad_normed):
    mean_grad = jnp.mean(grad_normed, axis=-1, keepdims=True)
    mean_prod = jnp.mean(grad_normed * normed, axis=-1, keepdims=True)
    return inv_std * (grad_normed - mean_grad - normed * mean_prod)


def silu_slope(values):
    sigm = jax.nn.sigmoid(values)
    return sigm * (1.0 + values * (1.0 - sigm))


def bits_of(size):
    assert size & (size - 1) == 0
    return [1 << k for k in range(size.bit_length() - 1)]


def swap(value, axis, size, bit):
    return lax.ppermute(value, axis, [(i, i ^ bit) for i in range(size)])


def has_bit(axis, bit):
    return (lax.axis_index(axis) & bit) != 0


def _nt(left, right):
    return lax.dot_general(
        left, right, (((1,), (1,)), ((), ())), preferred_element_type=jnp.float32
    )


def _nn(left, right):
    return jnp.dot(left, right, preferred_element_type=jnp.float32)


def _tn(left, right):
    return lax.dot_general(
        left, right, (((0,), (0,)), ((), ())), preferred_element_type=jnp.float32
    )


def lane_halves(pair):
    lane = lax.broadcasted_iota(jnp.int32, (1, pair), 1)
    first = (lane < pair // 2).astype(jnp.float32)
    return first.astype(jnp.bfloat16), (1.0 - first).astype(jnp.bfloat16)


def block_order(shards):
    bits = shards.bit_length() - 1
    return [sum(((n >> k) & 1) << (bits - 1 - k) for k in range(bits)) for n in range(shards)]


def attn_plan(pieces, w_qkv, w_proj, sems, me):
    rows = w_qkv.shape[0] // len(pieces)
    triple, width = w_qkv.shape[1], w_proj.shape[1]
    plan = [[], []]
    for j, piece in enumerate(pieces):
        at = pl.ds(pl.multiple_of((me ^ j) * rows, rows), rows)
        for n, (target, col, size) in enumerate(((w_qkv, 0, triple), (w_proj, triple, width))):
            source = piece.at[:, pl.ds(col, size)]
            plan[n].append(pltpu.make_async_copy(source, target.at[at, :], sems.at[j, n]))
    return plan


def mlp_plan(pieces, w_up, w_down, sems, me):
    rows = w_up.shape[0] // len(pieces)
    inner, width = w_down.shape
    ratio = inner // width
    plan = [[], []]
    for j, piece in enumerate(pieces):
        own = me ^ j
        at = pl.ds(pl.multiple_of(own * rows, rows), rows)
        source = piece.at[:, pl.ds(0, inner)]
        plan[0].append(pltpu.make_async_copy(source, w_up.at[at, :], sems.at[j, 0]))
        for q in range(ratio):
            at = pl.ds(pl.multiple_of((own * ratio + q) * rows, rows), rows)
            source = piece.at[:, pl.ds(inner + q * width, width)]
            plan[1].append(pltpu.make_async_copy(source, w_down.at[at, :], sems.at[j, 1 + q]))
    return plan


def start_all(plan):
    for group in plan:
        for copy in group:
            copy.start()


def wait_first(slot, group):
    @pl.when(slot == 0)
    def _():
        for copy in group:
            copy.wait()


def forward_body(slot, heads, value, mods, biases, weights, plans, saved):
    w_qkv, w_proj, w_up, w_down = weights
    one_out, qkv, probs_out, mixed, attn_out, hidden_out, slope_out, branch_out = saved
    bf16 = jnp.bfloat16
    width, inner = w_proj.shape[1], w_up.shape[1]
    normed, _ = norm_rows(value)
    attn_in = (normed * (1.0 + mods[1:2]) + mods[0:1]).astype(bf16)
    wait_first(slot, plans[0][0])
    qkv[...] = _nn(attn_in, w_qkv[...]).astype(bf16)
    pair = 2 * width // heads
    scale = 1.0 / (width // heads) ** 0.5
    masks = lane_halves(pair)
    for p in range(heads // 2):
        query = qkv[:, p * pair : (p + 1) * pair]
        key = qkv[:, width + p * pair : width + (p + 1) * pair]
        val = qkv[:, 2 * width + p * pair : 2 * width + (p + 1) * pair]
        total = None
        for h in range(2):
            scores = _nt(query * masks[h], key) * scale
            expo = jnp.exp(scores - jnp.max(scores, axis=-1, keepdims=True))
            probs = (expo * (1.0 / jnp.sum(expo, axis=-1, keepdims=True))).astype(bf16)
            probs_out[2 * p + h] = probs
            term = _nn(probs, val * masks[h])
            total = term if total is None else total + term
        mixed[:, p * pair : (p + 1) * pair] = total.astype(bf16)
    wait_first(slot, plans[0][1])
    attn = _nn(mixed[...], w_proj[...]) + biases[:, :width]
    attn_out[...] = attn.astype(bf16)
    one = value + mods[2:3] * attn
    one_out[...] = one
    normed, _ = norm_rows(one)
    mlp_in = (normed * (1.0 + mods[4:5]) + mods[3:4]).astype(bf16)
    wait_first(slot, plans[1][0])
    u = _nn(mlp_in, w_up[...]) + biases[:, width : width + inner]
    square = u * u
    tangent = jnp.tanh(GELU_K * (u + GELU_C * square * u))
    half = 0.5 * (1.0 + tangent)
    hidden_out[...] = (u * half).astype(bf16)
    slope = half + 0.5 * u * (1.0 - tangent * tangent) * (
        GELU_K + (3.0 * GELU_C * GELU_K) * square
    )
    slope_out[...] = slope.astype(bf16)
    wait_first(slot, plans[1][1])
    branch = _nn(hidden_out[...], w_down[...]) + biases[:, width + inner :]
    branch_out[...] = branch.astype(bf16)
    return one + mods[5:6] * branch


def mlp_back_body(slot, g, mods, one, hidden, slope, branch, weights, plan, sums, gada, bias_up, bias_down):
    w_up, w_down = weights
    a_up, a_down = sums
    f32, bf16 = jnp.float32, jnp.bfloat16
    gada[2:3, :] = jnp.sum(g * branch[...].astype(f32), axis=0, keepdims=True)
    gbranch = g * mods[5:6]
    bias_down[...] += jnp.sum(gbranch, axis=0, keepdims=True)
    gb = gbranch.astype(bf16)
    a_down[...] += _tn(hidden[...], gb)
    wait_first(slot, plan[1])
    gpre = _nt(gb, w_down[...]) * slope[...].astype(f32)
    bias_up[...] += jnp.sum(gpre, axis=0, keepdims=True)
    gp = gpre.astype(bf16)
    normed, inv = norm_rows(one[...])
    mlp_in = (normed * (1.0 + mods[4:5]) + mods[3:4]).astype(bf16)
    a_up[...] += _tn(mlp_in, gp)
    wait_first(slot, plan[0])
    gmlp = _nt(gp, w_up[...])
    gada[0:1, :] = jnp.sum(gmlp, axis=0, keepdims=True)
    gada[1:2, :] = jnp.sum(gmlp * normed, axis=0, keepdims=True)
    return g + norm_back(normed, inv, gmlp * (1.0 + mods[4:5]))


def attn_back_body(slot, heads, g1, mods, resid, qkv, probs, mixed, attn, weights, plan, sums, g_heads, gada, bias_proj):
    w_qkv, w_proj = weights
    a_qkv, a_proj = sums
    f32, bf16 = jnp.float32, jnp.bfloat16
    width = w_proj.shape[1]
    gada[2:3, :] = jnp.sum(g1 * attn[...].astype(f32), axis=0, keepdims=True)
    gattn = g1 * mods[2:3]
    bias_proj[...] += jnp.sum(gattn, axis=0, keepdims=True)
    ga = gattn.astype(bf16)
    a_proj[...] += _tn(mixed[...], ga)
    wait_first(slot, plan[1])
    gmixed = _nt(ga, w_proj[...]).astype(bf16)
    pair = 2 * width // heads
    scale = 1.0 / (width // heads) ** 0.5
    masks = lane_halves(pair)
    for p in range(heads // 2):
        query = qkv[:, p * pair : (p + 1) * pair]
        key = qkv[:, width + p * pair : width + (p + 1) * pair]
        val = qkv[:, 2 * width + p * pair : 2 * width + (p + 1) * pair]
        gm = gmixed[:, p * pair : (p + 1) * pair]
        gq, gk, gv = 0.0, 0.0, 0.0
        for h in range(2):
            low = probs[2 * p + h]
            gm_h = gm * masks[h]
            gprobs = _nt(gm_h, val)
            full = low.astype(f32)
            dot = jnp.sum(full * gprobs, axis=-1, keepdims=True)
            gscores = (full * (gprobs - dot) * scale).astype(bf16)
            gv = gv + _tn(low, gm_h)
            gq = gq + _nn(gscores, key * masks[h])
            gk = gk + _tn(gscores, query * masks[h])
        g_heads[:, p * pair : (p + 1) * pair] = gq.astype(bf16)
        g_heads[:, width + p * pair : width + (p + 1) * pair] = gk.astype(bf16)
        g_heads[:, 2 * width + p * pair : 2 * width + (p + 1) * pair] = gv.astype(bf16)
    normed, inv = norm_rows(resid)
    attn_in = (normed * (1.0 + mods[1:2]) + mods[0:1]).astype(bf16)
    a_qkv[...] += _tn(attn_in, g_heads[...])
    wait_first(slot, plan[0])
    gin = _nt(g_heads[...], w_qkv[...])
    gada[0:1, :] = jnp.sum(gin, axis=0, keepdims=True)
    gada[1:2, :] = jnp.sum(gin * normed, axis=0, keepdims=True)
    return g1 + norm_back(normed, inv, gin * (1.0 + mods[1:2]))


def emit_attn(shards, me, a_qkv, a_proj, keep, send):
    rows, triple = a_qkv.shape[0] // shards, a_qkv.shape[1]
    for n, j in enumerate(block_order(shards)):
        out, row = (keep, n) if n < shards // 2 else (send, n - shards // 2)
        at = pl.ds(pl.multiple_of((me ^ j) * rows, rows), rows)
        out[row, :, :triple] = a_qkv[at, :].astype(jnp.bfloat16)
        out[row, :, triple:] = a_proj[at, :].astype(jnp.bfloat16)


def emit_mlp(shards, me, a_up, a_down, keep, send):
    rows, inner = a_up.shape[0] // shards, a_up.shape[1]
    width = a_down.shape[1]
    ratio = inner // width
    for n, j in enumerate(block_order(shards)):
        out, row = (keep, n) if n < shards // 2 else (send, n - shards // 2)
        own = me ^ j
        at = pl.ds(pl.multiple_of(own * rows, rows), rows)
        out[row, :, :inner] = a_up[at, :].astype(jnp.bfloat16)
        for q in range(ratio):
            at = pl.ds(pl.multiple_of((own * ratio + q) * rows, rows), rows)
            col = inner + q * width
            out[row, :, col : col + width] = a_down[at, :].astype(jnp.bfloat16)


def clear(*refs):
    for ref in refs:
        ref[...] = jnp.zeros_like(ref[...])


def forward_kernel(shards, heads, info, resid, ada, biases, *rest):
    attn_pieces, mlp_pieces, rest = rest[:shards], rest[shards : 2 * shards], rest[2 * shards :]
    result, saved, rest = rest[0], rest[1:9], rest[9:]
    w_qkv, w_proj, w_up, w_down, attn_sems, mlp_sems = rest
    slot = pl.program_id(0)
    plans = (
        attn_plan(attn_pieces, w_qkv, w_proj, attn_sems, info[1]),
        mlp_plan(mlp_pieces, w_up, w_down, mlp_sems, info[1]),
    )

    @pl.when(slot == 0)
    def _():
        start_all(plans[0])
        start_all(plans[1])

    @pl.when(slot < info[0])
    def _():
        result[0] = forward_body(
            slot,
            heads,
            resid[0],
            ada[0],
            biases,
            (w_qkv, w_proj, w_up, w_down),
            plans,
            [ref.at[0] for ref in saved],
        )

    @pl.when(slot >= info[0])
    def _():
        clear(result)


def last_block_kernel(shards, heads, info, resid, grad, ada, biases, *rest):
    attn_pieces, mlp_pieces, rest = rest[:shards], rest[shards : 2 * shards], rest[2 * shards :]
    result, grad_out, gada_attn, gada_mlp, bias_proj, bias_up, bias_down = rest[:7]
    attn_keep, attn_send, mlp_keep, mlp_send = rest[7:11]
    w_qkv, w_proj, w_up, w_down, a_qkv, a_proj, a_up, a_down, g_heads = rest[11:20]
    saved, attn_sems, mlp_sems = rest[20:28], rest[28], rest[29]
    one, qkv, probs, mixed, attn, hidden, slope, branch = saved
    slot, me = pl.program_id(0), info[1]
    plans = (
        attn_plan(attn_pieces, w_qkv, w_proj, attn_sems, me),
        mlp_plan(mlp_pieces, w_up, w_down, mlp_sems, me),
    )
    done = [[], []]

    @pl.when(slot == 0)
    def _():
        start_all(plans[0])
        start_all(plans[1])
        clear(a_qkv, a_proj, a_up, a_down, bias_proj, bias_up, bias_down)

    @pl.when(slot < info[0])
    def _():
        mods, value = ada[0], resid[0]
        weights = (w_qkv, w_proj, w_up, w_down)
        result[0] = forward_body(slot, heads, value, mods, biases, weights, plans, saved)
        g1 = mlp_back_body(
            slot, grad[0], mods, one, hidden, slope, branch, weights[2:], done, (a_up, a_down),
            gada_mlp.at[0], bias_up, bias_down,
        )
        grad_out[0] = attn_back_body(
            slot, heads, g1, mods, value, qkv, probs, mixed, attn, weights[:2], done,
            (a_qkv, a_proj), g_heads, gada_attn.at[0], bias_proj,
        )

    @pl.when(slot >= info[0])
    def _():
        clear(result, grad_out, gada_attn, gada_mlp)

    @pl.when(slot == pl.num_programs(0) - 1)
    def _():
        emit_attn(shards, me, a_qkv, a_proj, attn_keep, attn_send)
        emit_mlp(shards, me, a_up, a_down, mlp_keep, mlp_send)


def mlp_back_kernel(shards, heads, info, grad, ada, one, hidden, slope, branch, *rest):
    pieces, rest = rest[:shards], rest[shards:]
    grad_out, gada, bias_up, bias_down, keep, send, w_up, w_down, a_up, a_down, sems = rest
    slot, me = pl.program_id(0), info[1]
    plan = mlp_plan(pieces, w_up, w_down, sems, me)

    @pl.when(slot == 0)
    def _():
        start_all(plan)
        clear(a_up, a_down, bias_up, bias_down)

    @pl.when(slot < info[0])
    def _():
        grad_out[0] = mlp_back_body(
            slot, grad[0], ada[0], one.at[0], hidden.at[0], slope.at[0], branch.at[0],
            (w_up, w_down), plan, (a_up, a_down), gada.at[0], bias_up, bias_down,
        )

    @pl.when(slot >= info[0])
    def _():
        clear(gada)

    @pl.when(slot == pl.num_programs(0) - 1)
    def _():
        emit_mlp(shards, me, a_up, a_down, keep, send)


def attn_back_kernel(shards, heads, info, grad, resid, ada, qkv, probs, mixed, attn, *rest):
    pieces, rest = rest[:shards], rest[shards:]
    grad_out, gada, bias_proj, keep, send, w_qkv, w_proj, a_qkv, a_proj, g_heads, sems = rest
    slot, me = pl.program_id(0), info[1]
    plan = attn_plan(pieces, w_qkv, w_proj, sems, me)

    @pl.when(slot == 0)
    def _():
        start_all(plan)
        clear(a_qkv, a_proj, bias_proj)

    @pl.when(slot < info[0])
    def _():
        grad_out[0] = attn_back_body(
            slot, heads, grad[0], ada[0], resid[0], qkv.at[0], probs.at[0], mixed.at[0],
            attn.at[0], (w_qkv, w_proj), plan, (a_qkv, a_proj), g_heads, gada.at[0], bias_proj,
        )

    @pl.when(slot >= info[0])
    def _():
        clear(grad_out, gada)

    @pl.when(slot == pl.num_programs(0) - 1)
    def _():
        emit_attn(shards, me, a_qkv, a_proj, keep, send)


def unpack_kernel(flag, *refs):
    g_qkv, g_proj, g_up, g_down = refs[-4:]
    triple, width, inner = g_qkv.shape[2], g_proj.shape[2], g_up.shape[2]
    rows, edge = g_qkv.shape[1], (triple + width) // 2

    def write(first):
        for n in range(LAYERS):
            low, high = refs[2 * n + first], refs[2 * n + 1 - first]
            g_qkv[n, :, :edge] = low[:, :edge].astype(jnp.float32)
            g_qkv[n, :, edge:] = high[:, : triple - edge].astype(jnp.float32)
            g_proj[n] = high[:, triple - edge : edge].astype(jnp.float32)
            g_up[n] = low[:, edge:].astype(jnp.float32)
            for q in range(inner // width):
                part = high[:, edge + q * width : edge + (q + 1) * width]
                g_down[n, q * rows : (q + 1) * rows, :] = part.astype(jnp.float32)

    @pl.when(flag[0] == 0)
    def _():
        write(0)

    @pl.when(flag[0] != 0)
    def _():
        write(1)


def unpack_call(flag, sums, sizes):
    triple, width, inner = sizes
    rows = sums[0][0].shape[0]
    shapes = [
        (LAYERS, rows, triple),
        (LAYERS, rows, width),
        (LAYERS, rows, inner),
        (LAYERS, inner // width * rows, width),
    ]
    parts = [half for pair in sums for half in pair]
    return pl.pallas_call(
        unpack_kernel,
        out_shape=[jax.ShapeDtypeStruct(s, jnp.float32) for s in shapes],
        in_specs=[pl.BlockSpec(memory_space=pltpu.SMEM)]
        + [pl.BlockSpec(memory_space=pltpu.VMEM)] * len(parts),
        out_specs=[pl.BlockSpec(memory_space=pltpu.VMEM)] * len(shapes),
        name="unpack",
    )(flag, *parts)


def per_slot(shape):
    rest = (0,) * (len(shape) - 1)
    return pl.BlockSpec((1,) + tuple(shape[1:]), lambda slot, info: (slot,) + rest)


def whole_block(shape):
    zeros = (0,) * len(shape)
    return pl.BlockSpec(tuple(shape), lambda slot, info: zeros)


def run_kernel(kernel, dims, info, blocked, fixed, pieces, outs, fixed_outs, scratch, passes):
    slots, length, width, triple, inner, heads, shards = dims
    shapes = list(outs) + list(fixed_outs)
    return pl.pallas_call(
        functools.partial(kernel, shards, heads),
        out_shape=[jax.ShapeDtypeStruct(s, d) for s, d in shapes],
        grid_spec=pltpu.PrefetchScalarGridSpec(
            num_scalar_prefetch=1,
            grid=(slots,),
            in_specs=[per_slot(a.shape) for a in blocked]
            + [whole_block(a.shape) for a in fixed]
            + [pl.BlockSpec(memory_space=pl.ANY)] * len(pieces),
            out_specs=[per_slot(s) for s, _ in outs] + [whole_block(s) for s, _ in fixed_outs],
            scratch_shapes=scratch,
        ),
        compiler_params=pltpu.CompilerParams(vmem_limit_bytes=VMEM_GRANT),
        cost_estimate=pl.CostEstimate(
            flops=passes * slots * length * width * (triple + width + 2 * inner),
            bytes_accessed=passes * slots * length * inner * 4,
            transcendentals=slots * length * inner,
        ),
    )(info, *blocked, *fixed, *pieces)


def kernel_parts(dims):
    slots, length, width, triple, inner, heads, shards = dims
    f32, bf16 = jnp.float32, jnp.bfloat16
    rows, ratio = width // shards, inner // width
    saved = [
        ((length, width), f32),
        ((length, triple), bf16),
        ((heads, length, length), bf16),
        ((length, width), bf16),
        ((length, width), bf16),
        ((length, inner), bf16),
        ((length, inner), bf16),
        ((length, width), bf16),
    ]
    w_attn = [pltpu.VMEM((width, triple), bf16), pltpu.VMEM((width, width), bf16)]
    w_mlp = [pltpu.VMEM((width, inner), bf16), pltpu.VMEM((inner, width), bf16)]
    a_attn = [pltpu.VMEM((width, triple), f32), pltpu.VMEM((width, width), f32)]
    a_mlp = [pltpu.VMEM((width, inner), f32), pltpu.VMEM((inner, width), f32)]
    heads_buf = [pltpu.VMEM((length, triple), bf16)]
    sems = [pltpu.SemaphoreType.DMA((shards, 2)), pltpu.SemaphoreType.DMA((shards, 1 + ratio))]
    rows_of = ((slots, length, width), f32)
    gada = ((slots, 3, width), f32)
    bias = [((1, width), f32), ((1, inner), f32), ((1, width), f32)]
    half = (shards // 2, rows)
    out_attn = [(half + (triple + width,), bf16)] * 2
    out_mlp = [(half + (2 * inner,), bf16)] * 2
    return saved, w_attn, w_mlp, a_attn, a_mlp, heads_buf, sems, rows_of, gada, bias, out_attn, out_mlp


def forward_call(dims, info, resid, ada, biases, attn_pieces, mlp_pieces):
    saved, w_attn, w_mlp, _, _, _, sems, rows_of, *_ = kernel_parts(dims)
    outs = [rows_of] + [((dims[0],) + s, d) for s, d in saved]
    return run_kernel(
        forward_kernel, dims, info, (resid, ada), (biases,),
        attn_pieces + mlp_pieces, outs, [], w_attn + w_mlp + sems, 2,
    )


def last_block_call(dims, info, resid, grad, ada, biases, attn_pieces, mlp_pieces):
    parts = kernel_parts(dims)
    saved, w_attn, w_mlp, a_attn, a_mlp, heads_buf, sems, rows_of, gada, bias, out_attn, out_mlp = parts
    scratch = w_attn + w_mlp + a_attn + a_mlp + heads_buf
    scratch += [pltpu.VMEM(s, d) for s, d in saved] + sems
    return run_kernel(
        last_block_kernel, dims, info, (resid, grad, ada), (biases,),
        attn_pieces + mlp_pieces, [rows_of, rows_of, gada, gada], bias + out_attn + out_mlp,
        scratch, 6,
    )


def mlp_back_call(dims, info, grad, ada, one, hidden, slope, branch, pieces):
    parts = kernel_parts(dims)
    _, _, w_mlp, _, a_mlp, _, sems, rows_of, gada, bias, _, out_mlp = parts
    return run_kernel(
        mlp_back_kernel, dims, info, (grad, ada, one, hidden, slope, branch), (),
        pieces, [rows_of, gada], bias[1:] + out_mlp, w_mlp + a_mlp + sems[1:], 2,
    )


def attn_back_call(dims, info, grad, resid, ada, qkv, probs, mixed, attn, pieces):
    parts = kernel_parts(dims)
    _, w_attn, _, a_attn, _, heads_buf, sems, rows_of, gada, bias, out_attn, _ = parts
    return run_kernel(
        attn_back_kernel, dims, info,
        (grad, resid, ada, qkv, probs, mixed, attn), (), pieces, [rows_of, gada],
        bias[:1] + out_attn, w_attn + a_attn + heads_buf + sems[:1], 2,
    )


def gather_rel(value, axis, size):
    pieces = {0: value}
    for bit in reversed(bits_of(size)):
        for j in list(pieces):
            pieces[j ^ bit] = swap(pieces[j], axis, size, bit)
    return [pieces[j] for j in range(size)]


def gather_all(value, stages):
    for axis, size, bit in stages:
        other = swap(value, axis, size, bit)
        upper = has_bit(axis, bit)
        value = jnp.concatenate(
            [jnp.where(upper, other, value), jnp.where(upper, value, other)], axis=0
        )
    return value


def to_absolute(pieces, axis):
    me = lax.axis_index(axis)
    out = jnp.zeros((len(pieces),) + pieces[0].shape, pieces[0].dtype)
    for j, piece in enumerate(pieces):
        out = lax.dynamic_update_index_in_dim(out, piece, me ^ j, 0)
    return out


def scatter_sum(blocks, axis, size):
    blocks = dict(enumerate(blocks))
    for bit in bits_of(size):
        keep = [j for j in blocks if not j & bit]
        got = swap(jnp.stack([blocks[j | bit] for j in keep]), axis, size, bit)
        blocks = {j: blocks[j] + got[n] for n, j in enumerate(keep)}
    return blocks[0]


def halves_of(left, right, kind, upper):
    if kind == "rows":
        half = left.shape[0] // 2
        return left[:half] + right[:half], left[half:] + right[half:]
    if kind == "columns":
        half = left.shape[-1] // 2
        low = left[..., :half] + right[..., :half]
        high = left[..., half:] + right[..., half:]
        return jnp.where(upper, high, low), jnp.where(upper, low, high)
    value = left + right
    return value, value


def run_stages(left, right, plan):
    trail = []
    for axis, size, bit, kind in plan:
        stay, go = halves_of(left, right, kind, has_bit(axis, bit))
        left, right = stay, swap(go, axis, size, bit)
        if kind == "columns":
            trail.append((axis, size, bit))
    return left, right, trail


def widen(value, axis, size, bit):
    other = swap(value, axis, size, bit)
    upper = has_bit(axis, bit)
    return jnp.where(upper, other, value), jnp.where(upper, value, other)


def early_plans(groups, shards):
    first, *others = [("fsdp", shards, bit, "rows") for bit in bits_of(shards)]
    cut = [("dp", groups, 1, "columns")]
    return first, cut + others, others + cut


def late_plan(groups, columns):
    plan = []
    for bit in bits_of(groups)[1:]:
        if 2 * bit < groups and (columns // 2) % 128 == 0:
            columns //= 2
            plan.append(("dp", groups, bit, "columns"))
        else:
            plan.append(("dp", groups, bit, "full"))
    return plan


def early_sum(kept, sent, first, plan):
    got = swap(sent, *first[:3])
    left, right, _ = run_stages(kept, got, plan)
    return left, right


def late_sum(attn, mlp, groups):
    value = jnp.concatenate([attn[0][0] + attn[1][0], mlp[0][0] + mlp[1][0]], axis=-1)
    left, right, trail = value, None, []
    plan = late_plan(groups, value.shape[-1])
    for axis, size, bit, kind in plan:
        if right is None:
            half = left.shape[-1] // 2
            upper = has_bit(axis, bit)
            stay, go = left, left
            if kind == "columns":
                low, high = left[:, :half], left[:, half:]
                stay, go = jnp.where(upper, high, low), jnp.where(upper, low, high)
        else:
            stay, go = halves_of(left, right, kind, has_bit(axis, bit))
        left, right = stay, swap(go, axis, size, bit)
        if kind == "columns":
            trail.append((axis, size, bit))
    value = left if right is None else left + right
    for stage in reversed(trail):
        value = jnp.concatenate(widen(value, *stage), axis=-1)
    return value, swap(value, "dp", groups, 1)


def on_device(
    sizes,
    latents,
    conditioning,
    seq_counts,
    cotangent,
    ada_weight,
    ada_bias,
    qkv_weight,
    proj_weight,
    proj_bias,
    up_weight,
    up_bias,
    down_weight,
    down_bias,
):
    groups, shards = sizes
    bf16, f32 = jnp.bfloat16, jnp.float32
    slots, length, width = latents.shape
    rows = qkv_weight.shape[1]
    triple, inner = qkv_weight.shape[2], up_weight.shape[2]
    wide = ada_weight.shape[2]
    ratio = inner // width
    me = lax.axis_index("fsdp")
    shard_stages = [("fsdp", shards, bit) for bit in bits_of(shards)]

    act = jax.nn.silu(conditioning).astype(bf16)
    shard_bias = jnp.concatenate([ada_bias, proj_bias, up_bias, down_bias], axis=1)
    bias_width = shard_bias.shape[1]
    small = jnp.concatenate([act.reshape(-1), shard_bias.reshape(-1)])[None]
    small = gather_all(small, shard_stages)

    attn_pieces, mlp_pieces = [], []
    for n in range(LAYERS):
        pack = jnp.concatenate([qkv_weight[n], proj_weight[n]], axis=1)
        attn_pieces.append(gather_rel(pack, "fsdp", shards))
        blocks = [down_weight[n, q * rows : (q + 1) * rows] for q in range(ratio)]
        pack = jnp.concatenate([up_weight[n]] + blocks, axis=1)
        mlp_pieces.append(gather_rel(pack, "fsdp", shards))

    act_group = small[:, : slots * width].reshape(shards * slots, width)
    biases = small[:, slots * width :].reshape(shards, LAYERS, bias_width)
    act_cols = lax.dynamic_slice(act_group, (0, me * rows), (shards * slots, rows))
    partial = jnp.stack(
        [jnp.dot(act_cols, ada_weight[n], preferred_element_type=f32) for n in range(LAYERS)]
    ).reshape(LAYERS, shards, slots, wide)
    blocks = [
        lax.dynamic_index_in_dim(partial, me ^ j, 1, keepdims=False).reshape(LAYERS * slots, wide)
        for j in range(shards)
    ]
    ada = scatter_sum(blocks, "fsdp", shards).reshape(LAYERS, slots, wide)
    cut = [0]
    for part in (ada_bias, proj_bias, up_bias, down_bias):
        cut.append(cut[-1] + part.shape[1])
    bias_of = [
        [biases[:, n, cut[k] : cut[k + 1]].reshape(-1).astype(f32) for k in range(4)]
        for n in range(LAYERS)
    ]
    modulation = [(ada[n] + bias_of[n][0]).reshape(slots, 6, width) for n in range(LAYERS)]
    bias_rows = [jnp.concatenate(bias_of[n][1:])[None] for n in range(LAYERS)]

    dims = (slots, length, width, triple, inner, HEADS, shards)
    info = jnp.stack([seq_counts[0], me.astype(jnp.int32)])
    top = LAYERS - 1
    inputs, saved = [], []
    current = latents
    for n in range(top):
        inputs.append(current)
        current, *kept = forward_call(
            dims, info, current, modulation[n], bias_rows[n], attn_pieces[n], mlp_pieces[n]
        )
        saved.append(kept)
    sums = [None] * LAYERS
    small_rows = [None] * LAYERS
    first, attn_plan_of, mlp_plan_of = early_plans(groups, shards)

    def reduce_layer(n, attn_pair, mlp_pair):
        mlp = early_sum(*mlp_pair, first, mlp_plan_of)
        attn = early_sum(*attn_pair, first, attn_plan_of)
        sums[n] = late_sum(attn, mlp, groups)

    def note_rows(n, gada_attn, gada_mlp, bias_grads):
        flat = jnp.concatenate([gada_attn, gada_mlp], axis=1).reshape(slots, wide)
        small_rows[n] = jnp.concatenate([flat, jnp.concatenate(bias_grads, axis=1)], axis=0)

    outs = last_block_call(
        dims, info, current, cotangent, modulation[top], bias_rows[top],
        attn_pieces[top], mlp_pieces[top],
    )
    block_out, grad, gada_attn, gada_mlp, b_proj, b_up, b_down = outs[:7]
    reduce_layer(top, outs[7:9], outs[9:11])
    note_rows(top, gada_attn, gada_mlp, (b_proj, b_up, b_down))
    for n in reversed(range(top)):
        one, qkv, probs, mixed, attn, hidden, slope, branch = saved[n]
        g1, gada_mlp, b_up, b_down, *mlp_pair = mlp_back_call(
            dims, info, grad, modulation[n], one, hidden, slope, branch, mlp_pieces[n]
        )
        grad, gada_attn, b_proj, *attn_pair = attn_back_call(
            dims, info, g1, inputs[n], modulation[n], qkv, probs, mixed, attn, attn_pieces[n]
        )
        reduce_layer(n, attn_pair, mlp_pair)
        note_rows(n, gada_attn, gada_mlp, (b_proj, b_up, b_down))

    flat = act.reshape(-1)
    flat = jnp.pad(flat, (0, -flat.shape[0] % wide)).reshape(-1, wide)
    message = jnp.concatenate([row.astype(bf16) for row in small_rows] + [flat], axis=0)
    stages = [("dp", groups, bit) for bit in reversed(bits_of(groups))]
    stages += [("fsdp", shards, bit) for bit in reversed(bits_of(shards))]
    every = gather_all(message[None], stages)
    per_layer = slots + 1
    gads = [every[:, n * per_layer : n * per_layer + slots] for n in range(LAYERS)]
    acts = every[:, LAYERS * per_layer :].reshape(every.shape[0], -1)[:, : slots * width]
    acts = acts.reshape(-1, width)
    acts_cols = lax.dynamic_slice(acts, (0, me * rows), (acts.shape[0], rows))
    g_ada = jnp.stack([outer_total(acts_cols, gads[n].reshape(-1, wide)) for n in range(LAYERS)])
    totals = jnp.sum(every[:, : LAYERS * per_layer].astype(f32), axis=0)
    totals = totals.reshape(LAYERS, per_layer, wide)
    g_ada_bias = jnp.sum(totals[:, :slots], axis=1)
    g_bias = totals[:, slots]

    place = jnp.int32(0)
    for k, bit in enumerate(reversed(bits_of(groups))):
        place = place + has_bit("dp", bit).astype(jnp.int32) * (1 << k)
    grid = every.reshape((shards, groups) + every.shape[1:])
    mine = lax.dynamic_index_in_dim(grid, place, 1, keepdims=False)
    total = 0.0
    for n in range(LAYERS):
        part = mine[:, n * per_layer : n * per_layer + slots].reshape(-1, wide)
        total = total + matmul_back(part, ada_weight[n])
    total = total.reshape([2] * len(bits_of(shards)) + [slots, rows])
    order = tuple(reversed(range(len(bits_of(shards)))))
    total = total.transpose(order + (len(order), len(order) + 1)).reshape(shards, slots, rows)
    got = [lax.dynamic_index_in_dim(total, me, 0, keepdims=False)]
    for j in range(1, shards):
        sent = lax.dynamic_index_in_dim(total, me ^ j, 0, keepdims=False)
        got.append(swap(sent, "fsdp", shards, j))
    grad_cond = to_absolute(got, "fsdp").transpose(1, 0, 2).reshape(slots, width)
    grad_cond = grad_cond * silu_slope(conditioning)

    upper = has_bit("dp", 1).astype(jnp.int32)[None]
    g_qkv, g_proj, g_up, down_sum = unpack_call(upper, sums, (triple, width, inner))
    own_inner = inner // shards
    return (
        block_out,
        grad,
        grad_cond,
        g_ada,
        lax.dynamic_slice_in_dim(g_ada_bias, me * (wide // shards), wide // shards, 1),
        g_qkv,
        g_proj,
        lax.dynamic_slice_in_dim(g_bias, me * rows, rows, 1),
        g_up,
        lax.dynamic_slice_in_dim(g_bias, width + me * own_inner, own_inner, 1),
        down_sum,
        lax.dynamic_slice_in_dim(g_bias, width + inner + me * rows, rows, 1),
    )


def solution(mesh):
    in_specs = (
        P(("dp", "fsdp"), None, None),
        P(("dp", "fsdp"), None),
        P(("dp", "fsdp")),
        P(("dp", "fsdp"), None, None),
        P(None, "fsdp", None),
        P(None, "fsdp"),
        P(None, "fsdp", None),
        P(None, "fsdp", None),
        P(None, "fsdp"),
        P(None, "fsdp", None),
        P(None, "fsdp"),
        P(None, "fsdp", None),
        P(None, "fsdp"),
    )
    out_specs = (
        P(("dp", "fsdp"), None, None),
        P(("dp", "fsdp"), None, None),
        P(("dp", "fsdp"), None),
        P(None, "fsdp", None),
        P(None, "fsdp"),
        P(None, "fsdp", None),
        P(None, "fsdp", None),
        P(None, "fsdp"),
        P(None, "fsdp", None),
        P(None, "fsdp"),
        P(None, "fsdp", None),
        P(None, "fsdp"),
    )
    sizes = (mesh.shape["dp"], mesh.shape["fsdp"])
    return jax.shard_map(
        functools.partial(on_device, sizes),
        mesh=mesh,
        in_specs=in_specs,
        out_specs=out_specs,
        check_vma=False,
    )
```

```python
import functools

import jax
import jax.numpy as jnp
from jax import lax
from jax.experimental import pallas as pl
from jax.experimental.pallas import tpu as pltpu
from jax.sharding import PartitionSpec as P


HEADS = 6
LAYERS = 2
VMEM_GRANT = 60 * 1024 * 1024


NORM_EPS = 1e-06
GELU_K = 0.7978845608028654
GELU_C = 0.044715


def matmul_back(left, right):
    flat = left.reshape(-1, left.shape[-1])
    return jnp.dot(flat, right.T, preferred_element_type=jnp.float32).reshape(
        left.shape[:-1] + (right.shape[0],)
    )


def outer_total(left, right):
    return jnp.dot(
        left.reshape(-1, left.shape[-1]).T,
        right.reshape(-1, right.shape[-1]),
        preferred_element_type=jnp.float32,
    )


def norm_rows(values):
    center = values - jnp.mean(values, axis=-1, keepdims=True)
    inv_std = lax.rsqrt(jnp.mean(center * center, axis=-1, keepdims=True) + NORM_EPS)
    return (center * inv_std, inv_std)


def norm_back(normed, inv_std, grad_normed):
    mean_grad = jnp.mean(grad_normed, axis=-1, keepdims=True)
    mean_prod = jnp.mean(grad_normed * normed, axis=-1, keepdims=True)
    return inv_std * (grad_normed - mean_grad - normed * mean_prod)


def silu_slope(values):
    sigm = jax.nn.sigmoid(values)
    return sigm * (1.0 + values * (1.0 - sigm))


def bits_of(size):
    assert size & (size - 1) == 0
    return [1 << k for k in range(size.bit_length() - 1)]


def swap(value, axis, size, bit):
    return lax.ppermute(value, axis, [(i, i ^ bit) for i in range(size)])


def has_bit(axis, bit):
    return (lax.axis_index(axis) & bit) != 0


def _nt(left, right):
    return lax.dot_general(
        left, right, (((1,), (1,)), ((), ())), preferred_element_type=jnp.float32
    )


def _nn(left, right):
    return jnp.dot(left, right, preferred_element_type=jnp.float32)


def _tn(left, right):
    return lax.dot_general(
        left, right, (((0,), (0,)), ((), ())), preferred_element_type=jnp.float32
    )


def lane_halves(pair):
    lane = lax.broadcasted_iota(jnp.int32, (1, pair), 1)
    first = (lane < pair // 2).astype(jnp.float32)
    return first.astype(jnp.bfloat16), (1.0 - first).astype(jnp.bfloat16)


def block_order(shards):
    bits = shards.bit_length() - 1
    return [sum(((n >> k) & 1) << (bits - 1 - k) for k in range(bits)) for n in range(shards)]


def attn_plan(pieces, w_qkv, w_proj, sems, me):
    rows = w_qkv.shape[0] // len(pieces)
    triple, width = w_qkv.shape[1], w_proj.shape[1]
    plan = [[], []]
    for j, piece in enumerate(pieces):
        at = pl.ds(pl.multiple_of((me ^ j) * rows, rows), rows)
        for n, (target, col, size) in enumerate(((w_qkv, 0, triple), (w_proj, triple, width))):
            source = piece.at[:, pl.ds(col, size)]
            plan[n].append(pltpu.make_async_copy(source, target.at[at, :], sems.at[j, n]))
    return plan


def mlp_plan(pieces, w_up, w_down, sems, me):
    rows = w_up.shape[0] // len(pieces)
    inner, width = w_down.shape
    ratio = inner // width
    plan = [[], []]
    for j, piece in enumerate(pieces):
        own = me ^ j
        at = pl.ds(pl.multiple_of(own * rows, rows), rows)
        source = piece.at[:, pl.ds(0, inner)]
        plan[0].append(pltpu.make_async_copy(source, w_up.at[at, :], sems.at[j, 0]))
        for q in range(ratio):
            at = pl.ds(pl.multiple_of((own * ratio + q) * rows, rows), rows)
            source = piece.at[:, pl.ds(inner + q * width, width)]
            plan[1].append(pltpu.make_async_copy(source, w_down.at[at, :], sems.at[j, 1 + q]))
    return plan


def start_all(plan):
    for group in plan:
        for copy in group:
            copy.start()


def wait_first(slot, group):
    @pl.when(slot == 0)
    def _():
        for copy in group:
            copy.wait()


def forward_body(slot, heads, value, mods, biases, weights, plans, saved):
    w_qkv, w_proj, w_up, w_down = weights
    one_out, qkv, probs_out, mixed, attn_out, hidden_out, slope_out, branch_out = saved
    bf16 = jnp.bfloat16
    width, inner = w_proj.shape[1], w_up.shape[1]
    normed, _ = norm_rows(value)
    attn_in = (normed * (1.0 + mods[1:2]) + mods[0:1]).astype(bf16)
    wait_first(slot, plans[0][0])
    qkv[...] = _nn(attn_in, w_qkv[...]).astype(bf16)
    pair = 2 * width // heads
    scale = 1.0 / (width // heads) ** 0.5
    masks = lane_halves(pair)
    for p in range(heads // 2):
        query = qkv[:, p * pair : (p + 1) * pair]
        key = qkv[:, width + p * pair : width + (p + 1) * pair]
        val = qkv[:, 2 * width + p * pair : 2 * width + (p + 1) * pair]
        total = None
        for h in range(2):
            scores = _nt(query * masks[h], key) * scale
            expo = jnp.exp(scores - jnp.max(scores, axis=-1, keepdims=True))
            probs = (expo * (1.0 / jnp.sum(expo, axis=-1, keepdims=True))).astype(bf16)
            probs_out[2 * p + h] = probs
            term = _nn(probs, val * masks[h])
            total = term if total is None else total + term
        mixed[:, p * pair : (p + 1) * pair] = total.astype(bf16)
    wait_first(slot, plans[0][1])
    attn = _nn(mixed[...], w_proj[...]) + biases[:, :width]
    attn_out[...] = attn.astype(bf16)
    one = value + mods[2:3] * attn
    one_out[...] = one
    normed, _ = norm_rows(one)
    mlp_in = (normed * (1.0 + mods[4:5]) + mods[3:4]).astype(bf16)
    wait_first(slot, plans[1][0])
    u = _nn(mlp_in, w_up[...]) + biases[:, width : width + inner]
    square = u * u
    tangent = jnp.tanh(GELU_K * (u + GELU_C * square * u))
    half = 0.5 * (1.0 + tangent)
    hidden_out[...] = (u * half).astype(bf16)
    slope = half + 0.5 * u * (1.0 - tangent * tangent) * (
        GELU_K + (3.0 * GELU_C * GELU_K) * square
    )
    slope_out[...] = slope.astype(bf16)
    wait_first(slot, plans[1][1])
    branch = _nn(hidden_out[...], w_down[...]) + biases[:, width + inner :]
    branch_out[...] = branch.astype(bf16)
    return one + mods[5:6] * branch


def mlp_back_body(slot, g, mods, one, hidden, slope, branch, weights, plan, sums, gada, bias_up, bias_down):
    w_up, w_down = weights
    a_up, a_down = sums
    f32, bf16 = jnp.float32, jnp.bfloat16
    gada[2:3, :] = jnp.sum(g * branch[...].astype(f32), axis=0, keepdims=True)
    gbranch = g * mods[5:6]
    bias_down[...] += jnp.sum(gbranch, axis=0, keepdims=True)
    gb = gbranch.astype(bf16)
    a_down[...] += _tn(hidden[...], gb)
    wait_first(slot, plan[1])
    gpre = _nt(gb, w_down[...]) * slope[...].astype(f32)
    bias_up[...] += jnp.sum(gpre, axis=0, keepdims=True)
    gp = gpre.astype(bf16)
    normed, inv = norm_rows(one[...])
    mlp_in = (normed * (1.0 + mods[4:5]) + mods[3:4]).astype(bf16)
    a_up[...] += _tn(mlp_in, gp)
    wait_first(slot, plan[0])
    gmlp = _nt(gp, w_up[...])
    gada[0:1, :] = jnp.sum(gmlp, axis=0, keepdims=True)
    gada[1:2, :] = jnp.sum(gmlp * normed, axis=0, keepdims=True)
    return g + norm_back(normed, inv, gmlp * (1.0 + mods[4:5]))


def attn_back_body(slot, heads, g1, mods, resid, qkv, probs, mixed, attn, weights, plan, sums, g_heads, gada, bias_proj):
    w_qkv, w_proj = weights
    a_qkv, a_proj = sums
    f32, bf16 = jnp.float32, jnp.bfloat16
    width = w_proj.shape[1]
    gada[2:3, :] = jnp.sum(g1 * attn[...].astype(f32), axis=0, keepdims=True)
    gattn = g1 * mods[2:3]
    bias_proj[...] += jnp.sum(gattn, axis=0, keepdims=True)
    ga = gattn.astype(bf16)
    a_proj[...] += _tn(mixed[...], ga)
    wait_first(slot, plan[1])
    gmixed = _nt(ga, w_proj[...]).astype(bf16)
    pair = 2 * width // heads
    scale = 1.0 / (width // heads) ** 0.5
    masks = lane_halves(pair)
    for p in range(heads // 2):
        query = qkv[:, p * pair : (p + 1) * pair]
        key = qkv[:, width + p * pair : width + (p + 1) * pair]
        val = qkv[:, 2 * width + p * pair : 2 * width + (p + 1) * pair]
        gm = gmixed[:, p * pair : (p + 1) * pair]
        gq, gk, gv = 0.0, 0.0, 0.0
        for h in range(2):
            low = probs[2 * p + h]
            gm_h = gm * masks[h]
            gprobs = _nt(gm_h, val)
            full = low.astype(f32)
            dot = jnp.sum(full * gprobs, axis=-1, keepdims=True)
            gscores = (full * (gprobs - dot) * scale).astype(bf16)
            gv = gv + _tn(low, gm_h)
            gq = gq + _nn(gscores, key * masks[h])
            gk = gk + _tn(gscores, query * masks[h])
        g_heads[:, p * pair : (p + 1) * pair] = gq.astype(bf16)
        g_heads[:, width + p * pair : width + (p + 1) * pair] = gk.astype(bf16)
        g_heads[:, 2 * width + p * pair : 2 * width + (p + 1) * pair] = gv.astype(bf16)
    normed, inv = norm_rows(resid)
    attn_in = (normed * (1.0 + mods[1:2]) + mods[0:1]).astype(bf16)
    a_qkv[...] += _tn(attn_in, g_heads[...])
    wait_first(slot, plan[0])
    gin = _nt(g_heads[...], w_qkv[...])
    gada[0:1, :] = jnp.sum(gin, axis=0, keepdims=True)
    gada[1:2, :] = jnp.sum(gin * normed, axis=0, keepdims=True)
    return g1 + norm_back(normed, inv, gin * (1.0 + mods[1:2]))


def emit_attn(shards, me, a_qkv, a_proj, keep, send):
    rows, triple = a_qkv.shape[0] // shards, a_qkv.shape[1]
    for n, j in enumerate(block_order(shards)):
        out, row = (keep, n) if n < shards // 2 else (send, n - shards // 2)
        at = pl.ds(pl.multiple_of((me ^ j) * rows, rows), rows)
        out[row, :, :triple] = a_qkv[at, :].astype(jnp.bfloat16)
        out[row, :, triple:] = a_proj[at, :].astype(jnp.bfloat16)


def emit_mlp(shards, me, a_up, a_down, keep, send):
    rows, inner = a_up.shape[0] // shards, a_up.shape[1]
    width = a_down.shape[1]
    ratio = inner // width
    for n, j in enumerate(block_order(shards)):
        out, row = (keep, n) if n < shards // 2 else (send, n - shards // 2)
        own = me ^ j
        at = pl.ds(pl.multiple_of(own * rows, rows), rows)
        out[row, :, :inner] = a_up[at, :].astype(jnp.bfloat16)
        for q in range(ratio):
            at = pl.ds(pl.multiple_of((own * ratio + q) * rows, rows), rows)
            col = inner + q * width
            out[row, :, col : col + width] = a_down[at, :].astype(jnp.bfloat16)


def clear(*refs):
    for ref in refs:
        ref[...] = jnp.zeros_like(ref[...])


def forward_kernel(shards, heads, info, resid, ada, biases, *rest):
    attn_pieces, mlp_pieces, rest = rest[:shards], rest[shards : 2 * shards], rest[2 * shards :]
    result, saved, rest = rest[0], rest[1:9], rest[9:]
    w_qkv, w_proj, w_up, w_down, attn_sems, mlp_sems = rest
    slot = pl.program_id(0)
    plans = (
        attn_plan(attn_pieces, w_qkv, w_proj, attn_sems, info[1]),
        mlp_plan(mlp_pieces, w_up, w_down, mlp_sems, info[1]),
    )

    @pl.when(slot == 0)
    def _():
        start_all(plans[0])
        start_all(plans[1])

    @pl.when(slot < info[0])
    def _():
        result[0] = forward_body(
            slot,
            heads,
            resid[0],
            ada[0],
            biases,
            (w_qkv, w_proj, w_up, w_down),
            plans,
            [ref.at[0] for ref in saved],
        )

    @pl.when(slot >= info[0])
    def _():
        clear(result)


def last_block_kernel(shards, heads, info, resid, grad, ada, biases, *rest):
    attn_pieces, mlp_pieces, rest = rest[:shards], rest[shards : 2 * shards], rest[2 * shards :]
    result, grad_out, gada_attn, gada_mlp, bias_proj, bias_up, bias_down = rest[:7]
    attn_keep, attn_send, mlp_keep, mlp_send = rest[7:11]
    w_qkv, w_proj, w_up, w_down, a_qkv, a_proj, a_up, a_down, g_heads = rest[11:20]
    saved, attn_sems, mlp_sems = rest[20:28], rest[28], rest[29]
    one, qkv, probs, mixed, attn, hidden, slope, branch = saved
    slot, me = pl.program_id(0), info[1]
    plans = (
        attn_plan(attn_pieces, w_qkv, w_proj, attn_sems, me),
        mlp_plan(mlp_pieces, w_up, w_down, mlp_sems, me),
    )
    done = [[], []]

    @pl.when(slot == 0)
    def _():
        start_all(plans[0])
        start_all(plans[1])
        clear(a_qkv, a_proj, a_up, a_down, bias_proj, bias_up, bias_down)

    @pl.when(slot < info[0])
    def _():
        mods, value = ada[0], resid[0]
        weights = (w_qkv, w_proj, w_up, w_down)
        result[0] = forward_body(slot, heads, value, mods, biases, weights, plans, saved)
        g1 = mlp_back_body(
            slot, grad[0], mods, one, hidden, slope, branch, weights[2:], done, (a_up, a_down),
            gada_mlp.at[0], bias_up, bias_down,
        )
        grad_out[0] = attn_back_body(
            slot, heads, g1, mods, value, qkv, probs, mixed, attn, weights[:2], done,
            (a_qkv, a_proj), g_heads, gada_attn.at[0], bias_proj,
        )

    @pl.when(slot >= info[0])
    def _():
        clear(result, grad_out, gada_attn, gada_mlp)

    @pl.when(slot == pl.num_programs(0) - 1)
    def _():
        emit_attn(shards, me, a_qkv, a_proj, attn_keep, attn_send)
        emit_mlp(shards, me, a_up, a_down, mlp_keep, mlp_send)


def mlp_back_kernel(shards, heads, info, grad, ada, one, hidden, slope, branch, *rest):
    pieces, rest = rest[:shards], rest[shards:]
    grad_out, gada, bias_up, bias_down, keep, send, w_up, w_down, a_up, a_down, sems = rest
    slot, me = pl.program_id(0), info[1]
    plan = mlp_plan(pieces, w_up, w_down, sems, me)

    @pl.when(slot == 0)
    def _():
        start_all(plan)
        clear(a_up, a_down, bias_up, bias_down)

    @pl.when(slot < info[0])
    def _():
        grad_out[0] = mlp_back_body(
            slot, grad[0], ada[0], one.at[0], hidden.at[0], slope.at[0], branch.at[0],
            (w_up, w_down), plan, (a_up, a_down), gada.at[0], bias_up, bias_down,
        )

    @pl.when(slot >= info[0])
    def _():
        clear(gada)

    @pl.when(slot == pl.num_programs(0) - 1)
    def _():
        emit_mlp(shards, me, a_up, a_down, keep, send)


def attn_back_kernel(shards, heads, info, grad, resid, ada, qkv, probs, mixed, attn, *rest):
    pieces, rest = rest[:shards], rest[shards:]
    grad_out, gada, bias_proj, keep, send, w_qkv, w_proj, a_qkv, a_proj, g_heads, sems = rest
    slot, me = pl.program_id(0), info[1]
    plan = attn_plan(pieces, w_qkv, w_proj, sems, me)

    @pl.when(slot == 0)
    def _():
        start_all(plan)
        clear(a_qkv, a_proj, bias_proj)

    @pl.when(slot < info[0])
    def _():
        grad_out[0] = attn_back_body(
            slot, heads, grad[0], ada[0], resid[0], qkv.at[0], probs.at[0], mixed.at[0],
            attn.at[0], (w_qkv, w_proj), plan, (a_qkv, a_proj), g_heads, gada.at[0], bias_proj,
        )

    @pl.when(slot >= info[0])
    def _():
        clear(grad_out, gada)

    @pl.when(slot == pl.num_programs(0) - 1)
    def _():
        emit_attn(shards, me, a_qkv, a_proj, keep, send)


def unpack_kernel(flag, *refs):
    g_qkv, g_proj, g_up, g_down = refs[-4:]
    triple, width, inner = g_qkv.shape[2], g_proj.shape[2], g_up.shape[2]
    rows, edge = g_qkv.shape[1], (triple + width) // 2

    def write(first):
        for n in range(LAYERS):
            low, high = refs[2 * n + first], refs[2 * n + 1 - first]
            g_qkv[n, :, :edge] = low[:, :edge].astype(jnp.float32)
            g_qkv[n, :, edge:] = high[:, : triple - edge].astype(jnp.float32)
            g_proj[n] = high[:, triple - edge : edge].astype(jnp.float32)
            g_up[n] = low[:, edge:].astype(jnp.float32)
            for q in range(inner // width):
                part = high[:, edge + q * width : edge + (q + 1) * width]
                g_down[n, q * rows : (q + 1) * rows, :] = part.astype(jnp.float32)

    @pl.when(flag[0] == 0)
    def _():
        write(0)

    @pl.when(flag[0] != 0)
    def _():
        write(1)


def unpack_call(flag, sums, sizes):
    triple, width, inner = sizes
    rows = sums[0][0].shape[0]
    shapes = [
        (LAYERS, rows, triple),
        (LAYERS, rows, width),
        (LAYERS, rows, inner),
        (LAYERS, inner // width * rows, width),
    ]
    parts = [half for pair in sums for half in pair]
    return pl.pallas_call(
        unpack_kernel,
        out_shape=[jax.ShapeDtypeStruct(s, jnp.float32) for s in shapes],
        in_specs=[pl.BlockSpec(memory_space=pltpu.SMEM)]
        + [pl.BlockSpec(memory_space=pltpu.VMEM)] * len(parts),
        out_specs=[pl.BlockSpec(memory_space=pltpu.VMEM)] * len(shapes),
        name="unpack",
    )(flag, *parts)


def small_kernel(starts, act, *refs):
    out, work = refs[-2:]
    work[...] = jnp.zeros_like(work[...])
    for part, start in zip(refs[:-2], starts):
        work[:LAYERS, start : start + part.shape[1]] = part[...].astype(jnp.float32)
    work[LAYERS : LAYERS + act.shape[0], : act.shape[1]] = act[...].astype(jnp.float32)
    out[...] = work[...].astype(out.dtype)


def small_call(act, parts):
    starts, total = [], 0
    for part in parts:
        starts.append(total)
        total += -(-part.shape[1] // 128) * 128
    shape = (-(-(LAYERS + act.shape[0]) // 16) * 16, max(total, act.shape[1]))
    out = pl.pallas_call(
        functools.partial(small_kernel, starts),
        out_shape=jax.ShapeDtypeStruct(shape, jnp.bfloat16),
        in_specs=[pl.BlockSpec(memory_space=pltpu.VMEM)] * (1 + len(parts)),
        out_specs=pl.BlockSpec(memory_space=pltpu.VMEM),
        scratch_shapes=[pltpu.VMEM(shape, jnp.float32)],
        name="small_rows",
    )(act, *parts)
    return out, starts


def gad_kernel(*refs):
    out, work = refs[-2:]
    if work.shape[0] > LAYERS * (refs[0].shape[0] + 1):
        work[...] = jnp.zeros_like(work[...])
    for n in range(LAYERS):
        attn, mlp, proj, up, down = refs[5 * n : 5 * n + 5]
        slots, _, width = attn.shape
        base = n * (slots + 1)
        for s in range(slots):
            for k in range(3):
                row = slice(base + s, base + s + 1)
                work[row, k * width : (k + 1) * width] = attn[s, k : k + 1, :]
                work[row, (3 + k) * width : (4 + k) * width] = mlp[s, k : k + 1, :]
        row = slice(base + slots, base + slots + 1)
        inner = up.shape[1]
        work[row, :width] = proj[...]
        work[row, width : width + inner] = up[...]
        work[row, width + inner :] = down[...]
    out[...] = work[...].astype(out.dtype)


def gad_call(layers, wide):
    slots = layers[0][0].shape[0]
    shape = (-(-LAYERS * (slots + 1) // 8) * 8, wide)
    parts = [part for layer in layers for part in layer]
    return pl.pallas_call(
        gad_kernel,
        out_shape=jax.ShapeDtypeStruct(shape, jnp.bfloat16),
        in_specs=[pl.BlockSpec(memory_space=pltpu.VMEM)] * len(parts),
        out_specs=pl.BlockSpec(memory_space=pltpu.VMEM),
        scratch_shapes=[pltpu.VMEM(shape, jnp.float32)],
        name="gad_rows",
    )(*parts)


def per_slot(shape):
    rest = (0,) * (len(shape) - 1)
    return pl.BlockSpec((1,) + tuple(shape[1:]), lambda slot, info: (slot,) + rest)


def whole_block(shape):
    zeros = (0,) * len(shape)
    return pl.BlockSpec(tuple(shape), lambda slot, info: zeros)


def run_kernel(kernel, dims, info, blocked, fixed, pieces, outs, fixed_outs, scratch, passes):
    slots, length, width, triple, inner, heads, shards = dims
    shapes = list(outs) + list(fixed_outs)
    return pl.pallas_call(
        functools.partial(kernel, shards, heads),
        out_shape=[jax.ShapeDtypeStruct(s, d) for s, d in shapes],
        grid_spec=pltpu.PrefetchScalarGridSpec(
            num_scalar_prefetch=1,
            grid=(slots,),
            in_specs=[per_slot(a.shape) for a in blocked]
            + [whole_block(a.shape) for a in fixed]
            + [pl.BlockSpec(memory_space=pl.ANY)] * len(pieces),
            out_specs=[per_slot(s) for s, _ in outs] + [whole_block(s) for s, _ in fixed_outs],
            scratch_shapes=scratch,
        ),
        compiler_params=pltpu.CompilerParams(vmem_limit_bytes=VMEM_GRANT),
        cost_estimate=pl.CostEstimate(
            flops=passes * slots * length * width * (triple + width + 2 * inner),
            bytes_accessed=passes * slots * length * inner * 4,
            transcendentals=slots * length * inner,
        ),
    )(info, *blocked, *fixed, *pieces)


def kernel_parts(dims):
    slots, length, width, triple, inner, heads, shards = dims
    f32, bf16 = jnp.float32, jnp.bfloat16
    rows, ratio = width // shards, inner // width
    saved = [
        ((length, width), f32),
        ((length, triple), bf16),
        ((heads, length, length), bf16),
        ((length, width), bf16),
        ((length, width), bf16),
        ((length, inner), bf16),
        ((length, inner), bf16),
        ((length, width), bf16),
    ]
    w_attn = [pltpu.VMEM((width, triple), bf16), pltpu.VMEM((width, width), bf16)]
    w_mlp = [pltpu.VMEM((width, inner), bf16), pltpu.VMEM((inner, width), bf16)]
    a_attn = [pltpu.VMEM((width, triple), f32), pltpu.VMEM((width, width), f32)]
    a_mlp = [pltpu.VMEM((width, inner), f32), pltpu.VMEM((inner, width), f32)]
    heads_buf = [pltpu.VMEM((length, triple), bf16)]
    sems = [pltpu.SemaphoreType.DMA((shards, 2)), pltpu.SemaphoreType.DMA((shards, 1 + ratio))]
    rows_of = ((slots, length, width), f32)
    gada = ((slots, 3, width), f32)
    bias = [((1, width), f32), ((1, inner), f32), ((1, width), f32)]
    half = (shards // 2, rows)
    out_attn = [(half + (triple + width,), bf16)] * 2
    out_mlp = [(half + (2 * inner,), bf16)] * 2
    return saved, w_attn, w_mlp, a_attn, a_mlp, heads_buf, sems, rows_of, gada, bias, out_attn, out_mlp


def forward_call(dims, info, resid, ada, biases, attn_pieces, mlp_pieces):
    saved, w_attn, w_mlp, _, _, _, sems, rows_of, *_ = kernel_parts(dims)
    outs = [rows_of] + [((dims[0],) + s, d) for s, d in saved]
    return run_kernel(
        forward_kernel, dims, info, (resid, ada), (biases,),
        attn_pieces + mlp_pieces, outs, [], w_attn + w_mlp + sems, 2,
    )


def last_block_call(dims, info, resid, grad, ada, biases, attn_pieces, mlp_pieces):
    parts = kernel_parts(dims)
    saved, w_attn, w_mlp, a_attn, a_mlp, heads_buf, sems, rows_of, gada, bias, out_attn, out_mlp = parts
    scratch = w_attn + w_mlp + a_attn + a_mlp + heads_buf
    scratch += [pltpu.VMEM(s, d) for s, d in saved] + sems
    return run_kernel(
        last_block_kernel, dims, info, (resid, grad, ada), (biases,),
        attn_pieces + mlp_pieces, [rows_of, rows_of, gada, gada], bias + out_attn + out_mlp,
        scratch, 6,
    )


def mlp_back_call(dims, info, grad, ada, one, hidden, slope, branch, pieces):
    parts = kernel_parts(dims)
    _, _, w_mlp, _, a_mlp, _, sems, rows_of, gada, bias, _, out_mlp = parts
    return run_kernel(
        mlp_back_kernel, dims, info, (grad, ada, one, hidden, slope, branch), (),
        pieces, [rows_of, gada], bias[1:] + out_mlp, w_mlp + a_mlp + sems[1:], 2,
    )


def attn_back_call(dims, info, grad, resid, ada, qkv, probs, mixed, attn, pieces):
    parts = kernel_parts(dims)
    _, w_attn, _, a_attn, _, heads_buf, sems, rows_of, gada, bias, out_attn, _ = parts
    return run_kernel(
        attn_back_kernel, dims, info,
        (grad, resid, ada, qkv, probs, mixed, attn), (), pieces, [rows_of, gada],
        bias[:1] + out_attn, w_attn + a_attn + heads_buf + sems[:1], 2,
    )


def gather_rel(value, axis, size):
    pieces = {0: value}
    for bit in reversed(bits_of(size)):
        for j in list(pieces):
            pieces[j ^ bit] = swap(pieces[j], axis, size, bit)
    return [pieces[j] for j in range(size)]


def gather_all(value, stages, fast=False):
    for axis, size, bit in stages:
        other = swap(value, axis, size, bit)
        upper = has_bit(axis, bit)
        both = [jnp.where(upper, other, value), jnp.where(upper, value, other)]
        if fast:
            value = jnp.stack(both, axis=1).reshape((-1,) + value.shape[1:])
        else:
            value = jnp.concatenate(both, axis=0)
    return value


def to_absolute(pieces, axis):
    me = lax.axis_index(axis)
    out = jnp.zeros((len(pieces),) + pieces[0].shape, pieces[0].dtype)
    for j, piece in enumerate(pieces):
        out = lax.dynamic_update_index_in_dim(out, piece, me ^ j, 0)
    return out


def scatter_sum(blocks, axis, size):
    blocks = dict(enumerate(blocks))
    for bit in bits_of(size):
        keep = [j for j in blocks if not j & bit]
        got = swap(jnp.stack([blocks[j | bit] for j in keep]), axis, size, bit)
        blocks = {j: blocks[j] + got[n] for n, j in enumerate(keep)}
    return blocks[0]


def halves_of(left, right, kind, upper):
    if kind == "rows":
        half = left.shape[0] // 2
        return left[:half] + right[:half], left[half:] + right[half:]
    if kind == "columns":
        half = left.shape[-1] // 2
        low = left[..., :half] + right[..., :half]
        high = left[..., half:] + right[..., half:]
        return jnp.where(upper, high, low), jnp.where(upper, low, high)
    value = left + right
    return value, value


def run_stages(left, right, plan):
    trail = []
    for axis, size, bit, kind in plan:
        stay, go = halves_of(left, right, kind, has_bit(axis, bit))
        left, right = stay, swap(go, axis, size, bit)
        if kind == "columns":
            trail.append((axis, size, bit))
    return left, right, trail


def widen(value, axis, size, bit):
    other = swap(value, axis, size, bit)
    upper = has_bit(axis, bit)
    return jnp.where(upper, other, value), jnp.where(upper, value, other)


def early_plans(groups, shards):
    first, *others = [("fsdp", shards, bit, "rows") for bit in bits_of(shards)]
    cut = [("dp", groups, 1, "columns")]
    return first, cut + others, others + cut


def late_plan(groups, columns):
    plan = []
    for bit in bits_of(groups)[1:]:
        if 2 * bit < groups and (columns // 2) % 128 == 0:
            columns //= 2
            plan.append(("dp", groups, bit, "columns"))
        else:
            plan.append(("dp", groups, bit, "full"))
    return plan


def early_sum(kept, sent, first, plan):
    got = swap(sent, *first[:3])
    left, right, _ = run_stages(kept, got, plan)
    return left, right


def late_sum(attn, mlp, groups):
    value = jnp.concatenate([attn[0][0] + attn[1][0], mlp[0][0] + mlp[1][0]], axis=-1)
    left, right, trail = value, None, []
    plan = late_plan(groups, value.shape[-1])
    for axis, size, bit, kind in plan:
        if right is None:
            half = left.shape[-1] // 2
            upper = has_bit(axis, bit)
            stay, go = left, left
            if kind == "columns":
                low, high = left[:, :half], left[:, half:]
                stay, go = jnp.where(upper, high, low), jnp.where(upper, low, high)
        else:
            stay, go = halves_of(left, right, kind, has_bit(axis, bit))
        left, right = stay, swap(go, axis, size, bit)
        if kind == "columns":
            trail.append((axis, size, bit))
    value = left if right is None else left + right
    for stage in reversed(trail):
        value = jnp.concatenate(widen(value, *stage), axis=-1)
    return value, swap(value, "dp", groups, 1)


def on_device(
    sizes,
    latents,
    conditioning,
    seq_counts,
    cotangent,
    ada_weight,
    ada_bias,
    qkv_weight,
    proj_weight,
    proj_bias,
    up_weight,
    up_bias,
    down_weight,
    down_bias,
):
    groups, shards = sizes
    bf16, f32 = jnp.bfloat16, jnp.float32
    slots, length, width = latents.shape
    rows = qkv_weight.shape[1]
    triple, inner = qkv_weight.shape[2], up_weight.shape[2]
    wide = ada_weight.shape[2]
    ratio = inner // width
    me = lax.axis_index("fsdp")
    shard_stages = [("fsdp", shards, bit) for bit in bits_of(shards)]

    act = jax.nn.silu(conditioning).astype(bf16)
    parts = (ada_bias, proj_bias, up_bias, down_bias)
    small, starts = small_call(act, parts)
    small = gather_all(small[None], shard_stages[::-1], fast=True)

    attn_pieces, mlp_pieces = [], []
    for n in range(LAYERS):
        pack = jnp.concatenate([qkv_weight[n], proj_weight[n]], axis=1)
        attn_pieces.append(gather_rel(pack, "fsdp", shards))
        blocks = [down_weight[n, q * rows : (q + 1) * rows] for q in range(ratio)]
        pack = jnp.concatenate([up_weight[n]] + blocks, axis=1)
        mlp_pieces.append(gather_rel(pack, "fsdp", shards))

    act_group = small[:, LAYERS : LAYERS + slots, :width].reshape(shards * slots, width)
    group_stages = [("dp", groups, bit) for bit in bits_of(groups)[:1] + bits_of(groups)[:0:-1]]
    acts = gather_all(act_group.reshape(1, shards, slots, width), group_stages)
    counts = len(group_stages), len(shard_stages)
    acts = acts.reshape([2] * sum(counts) + [slots, width])
    order = list(range(sum(counts)))[: counts[0] - 1 : -1] + list(range(counts[0]))
    acts = acts.transpose(order + [sum(counts), sum(counts) + 1]).reshape(-1, slots, width)
    act_cols = lax.dynamic_slice(act_group, (0, me * rows), (shards * slots, rows))
    partial = jnp.stack(
        [jnp.dot(act_cols, ada_weight[n], preferred_element_type=f32) for n in range(LAYERS)]
    ).reshape(LAYERS, shards, slots, wide)
    blocks = [
        lax.dynamic_index_in_dim(partial, me ^ j, 1, keepdims=False).reshape(LAYERS * slots, wide)
        for j in range(shards)
    ]
    ada = scatter_sum(blocks, "fsdp", shards).reshape(LAYERS, slots, wide)
    bias_of = [
        [
            small[:, n, start : start + part.shape[1]].reshape(-1).astype(f32)
            for part, start in zip(parts, starts)
        ]
        for n in range(LAYERS)
    ]
    modulation = [(ada[n] + bias_of[n][0]).reshape(slots, 6, width) for n in range(LAYERS)]
    bias_rows = [jnp.concatenate(bias_of[n][1:])[None] for n in range(LAYERS)]

    dims = (slots, length, width, triple, inner, HEADS, shards)
    info = jnp.stack([seq_counts[0], me.astype(jnp.int32)])
    top = LAYERS - 1
    inputs, saved = [], []
    current = latents
    for n in range(top):
        inputs.append(current)
        current, *kept = forward_call(
            dims, info, current, modulation[n], bias_rows[n], attn_pieces[n], mlp_pieces[n]
        )
        saved.append(kept)
    sums = [None] * LAYERS
    small_rows = [None] * LAYERS
    first, attn_plan_of, mlp_plan_of = early_plans(groups, shards)

    def reduce_layer(n, attn_pair, mlp_pair):
        mlp = early_sum(*mlp_pair, first, mlp_plan_of)
        attn = early_sum(*attn_pair, first, attn_plan_of)
        sums[n] = late_sum(attn, mlp, groups)

    outs = last_block_call(
        dims, info, current, cotangent, modulation[top], bias_rows[top],
        attn_pieces[top], mlp_pieces[top],
    )
    block_out, grad, gada_attn, gada_mlp, b_proj, b_up, b_down = outs[:7]
    reduce_layer(top, outs[7:9], outs[9:11])
    small_rows[top] = (gada_attn, gada_mlp, b_proj, b_up, b_down)
    for n in reversed(range(top)):
        one, qkv, probs, mixed, attn, hidden, slope, branch = saved[n]
        g1, gada_mlp, b_up, b_down, *mlp_pair = mlp_back_call(
            dims, info, grad, modulation[n], one, hidden, slope, branch, mlp_pieces[n]
        )
        grad, gada_attn, b_proj, *attn_pair = attn_back_call(
            dims, info, g1, inputs[n], modulation[n], qkv, probs, mixed, attn, attn_pieces[n]
        )
        reduce_layer(n, attn_pair, mlp_pair)
        small_rows[n] = (gada_attn, gada_mlp, b_proj, b_up, b_down)

    message = gad_call(small_rows, wide)
    stages = group_stages + shard_stages[::-1]
    every = gather_all(message[None], stages)
    per_layer = slots + 1
    acts_cols = lax.dynamic_slice(acts, (0, 0, me * rows), acts.shape[:2] + (rows,))
    tail_rows = message.shape[0] - slots
    flat = every.reshape(-1, wide)
    g_ada = jnp.stack(
        [
            outer_total(
                jnp.pad(
                    acts_cols, ((0, 0), (n * per_layer, tail_rows - n * per_layer), (0, 0))
                ).reshape(-1, rows),
                flat,
            )
            for n in range(LAYERS)
        ]
    )
    totals = jnp.sum(every.astype(f32), axis=0)
    g_ada_bias = jnp.stack(
        [jnp.sum(totals[n * per_layer : n * per_layer + slots], axis=0) for n in range(LAYERS)]
    )
    g_bias = jnp.stack([totals[n * per_layer + slots] for n in range(LAYERS)])

    begin = [
        has_bit(axis, bit).astype(jnp.int32) if axis == "dp" else jnp.int32(0)
        for axis, _, bit in reversed(stages)
    ]
    extent = [1 if axis == "dp" else 2 for axis, _, _ in stages[::-1]]
    grid = every.reshape([2] * len(stages) + list(message.shape))
    zero = jnp.int32(0)
    mine = lax.dynamic_slice(grid, begin + [zero, zero], extent + list(message.shape))
    mine = mine.reshape(-1, wide)
    total = 0.0
    for n in range(LAYERS):
        part = matmul_back(mine, ada_weight[n]).reshape(shards, -1, rows)
        total = total + part[:, n * per_layer : n * per_layer + slots]
    total = total.reshape([2] * len(bits_of(shards)) + [slots, rows])
    order = tuple(reversed(range(len(bits_of(shards)))))
    total = total.transpose(order + (len(order), len(order) + 1)).reshape(shards, slots, rows)
    got = [lax.dynamic_index_in_dim(total, me, 0, keepdims=False)]
    for j in range(1, shards):
        sent = lax.dynamic_index_in_dim(total, me ^ j, 0, keepdims=False)
        got.append(swap(sent, "fsdp", shards, j))
    grad_cond = to_absolute(got, "fsdp").transpose(1, 0, 2).reshape(slots, width)
    grad_cond = grad_cond * silu_slope(conditioning)

    upper = has_bit("dp", 1).astype(jnp.int32)[None]
    g_qkv, g_proj, g_up, down_sum = unpack_call(upper, sums, (triple, width, inner))
    own_inner = inner // shards
    return (
        block_out,
        grad,
        grad_cond,
        g_ada,
        lax.dynamic_slice_in_dim(g_ada_bias, me * (wide // shards), wide // shards, 1),
        g_qkv,
        g_proj,
        lax.dynamic_slice_in_dim(g_bias, me * rows, rows, 1),
        g_up,
        lax.dynamic_slice_in_dim(g_bias, width + me * own_inner, own_inner, 1),
        down_sum,
        lax.dynamic_slice_in_dim(g_bias, width + inner + me * rows, rows, 1),
    )


def solution(mesh):
    in_specs = (
        P(("dp", "fsdp"), None, None),
        P(("dp", "fsdp"), None),
        P(("dp", "fsdp")),
        P(("dp", "fsdp"), None, None),
        P(None, "fsdp", None),
        P(None, "fsdp"),
        P(None, "fsdp", None),
        P(None, "fsdp", None),
        P(None, "fsdp"),
        P(None, "fsdp", None),
        P(None, "fsdp"),
        P(None, "fsdp", None),
        P(None, "fsdp"),
    )
    out_specs = (
        P(("dp", "fsdp"), None, None),
        P(("dp", "fsdp"), None, None),
        P(("dp", "fsdp"), None),
        P(None, "fsdp", None),
        P(None, "fsdp"),
        P(None, "fsdp", None),
        P(None, "fsdp", None),
        P(None, "fsdp"),
        P(None, "fsdp", None),
        P(None, "fsdp"),
        P(None, "fsdp", None),
        P(None, "fsdp"),
    )
    sizes = (mesh.shape["dp"], mesh.shape["fsdp"])
    return jax.shard_map(
        functools.partial(on_device, sizes),
        mesh=mesh,
        in_specs=in_specs,
        out_specs=out_specs,
        check_vma=False,
    )
```

```python
import functools

import jax
import jax.numpy as jnp
from jax import lax
from jax.experimental import pallas as pl
from jax.experimental.pallas import tpu as pltpu
from jax.sharding import PartitionSpec as P


HEADS = 6
LAYERS = 2
VMEM_GRANT = 60 * 1024 * 1024


NORM_EPS = 1e-06
GELU_K = 0.7978845608028654
GELU_C = 0.044715


def matmul_back(left, right):
    flat = left.reshape(-1, left.shape[-1])
    return jnp.dot(flat, right.T, preferred_element_type=jnp.float32).reshape(
        left.shape[:-1] + (right.shape[0],)
    )


def outer_total(left, right):
    return jnp.dot(
        left.reshape(-1, left.shape[-1]).T,
        right.reshape(-1, right.shape[-1]),
        preferred_element_type=jnp.float32,
    )


def norm_rows(values):
    center = values - jnp.mean(values, axis=-1, keepdims=True)
    inv_std = lax.rsqrt(jnp.mean(center * center, axis=-1, keepdims=True) + NORM_EPS)
    return (center * inv_std, inv_std)


def norm_back(normed, inv_std, grad_normed):
    mean_grad = jnp.mean(grad_normed, axis=-1, keepdims=True)
    mean_prod = jnp.mean(grad_normed * normed, axis=-1, keepdims=True)
    return inv_std * (grad_normed - mean_grad - normed * mean_prod)


def silu_slope(values):
    sigm = jax.nn.sigmoid(values)
    return sigm * (1.0 + values * (1.0 - sigm))


def bits_of(size):
    assert size & (size - 1) == 0
    return [1 << k for k in range(size.bit_length() - 1)]


def swap(value, axis, size, bit):
    return lax.ppermute(value, axis, [(i, i ^ bit) for i in range(size)])


def has_bit(axis, bit):
    return (lax.axis_index(axis) & bit) != 0


def _nt(left, right):
    return lax.dot_general(
        left, right, (((1,), (1,)), ((), ())), preferred_element_type=jnp.float32
    )


def _nn(left, right):
    return jnp.dot(left, right, preferred_element_type=jnp.float32)


def _tn(left, right):
    return lax.dot_general(
        left, right, (((0,), (0,)), ((), ())), preferred_element_type=jnp.float32
    )


def lane_halves(pair):
    lane = lax.broadcasted_iota(jnp.int32, (1, pair), 1)
    first = (lane < pair // 2).astype(jnp.float32)
    return first.astype(jnp.bfloat16), (1.0 - first).astype(jnp.bfloat16)


def block_order(shards):
    bits = shards.bit_length() - 1
    return [sum(((n >> k) & 1) << (bits - 1 - k) for k in range(bits)) for n in range(shards)]


def attn_plan(pieces, w_qkv, w_proj, sems, me):
    rows = w_qkv.shape[0] // len(pieces)
    triple, width = w_qkv.shape[1], w_proj.shape[1]
    plan = [[], []]
    for j, piece in enumerate(pieces):
        at = pl.ds(pl.multiple_of((me ^ j) * rows, rows), rows)
        for n, (target, col, size) in enumerate(((w_qkv, 0, triple), (w_proj, triple, width))):
            source = piece.at[:, pl.ds(col, size)]
            plan[n].append(pltpu.make_async_copy(source, target.at[at, :], sems.at[j, n]))
    return plan


def mlp_plan(pieces, w_up, w_down, sems, me):
    rows = w_up.shape[0] // len(pieces)
    inner, width = w_down.shape
    ratio = inner // width
    plan = [[], []]
    for j, piece in enumerate(pieces):
        own = me ^ j
        at = pl.ds(pl.multiple_of(own * rows, rows), rows)
        source = piece.at[:, pl.ds(0, inner)]
        plan[0].append(pltpu.make_async_copy(source, w_up.at[at, :], sems.at[j, 0]))
        for q in range(ratio):
            at = pl.ds(pl.multiple_of((own * ratio + q) * rows, rows), rows)
            source = piece.at[:, pl.ds(inner + q * width, width)]
            plan[1].append(pltpu.make_async_copy(source, w_down.at[at, :], sems.at[j, 1 + q]))
    return plan


def start_all(plan):
    for group in plan:
        for copy in group:
            copy.start()


def wait_first(slot, group):
    @pl.when(slot == 0)
    def _():
        for copy in group:
            copy.wait()


def forward_body(slot, heads, value, mods, biases, weights, plans, saved):
    w_qkv, w_proj, w_up, w_down = weights
    one_out, qkv, probs_out, mixed, attn_out, hidden_out, slope_out, branch_out = saved
    bf16 = jnp.bfloat16
    width, inner = w_proj.shape[1], w_up.shape[1]
    normed, _ = norm_rows(value)
    attn_in = (normed * (1.0 + mods[1:2]) + mods[0:1]).astype(bf16)
    wait_first(slot, plans[0][0])
    qkv[...] = _nn(attn_in, w_qkv[...]).astype(bf16)
    pair = 2 * width // heads
    scale = 1.0 / (width // heads) ** 0.5
    masks = lane_halves(pair)
    for p in range(heads // 2):
        query = qkv[:, p * pair : (p + 1) * pair]
        key = qkv[:, width + p * pair : width + (p + 1) * pair]
        val = qkv[:, 2 * width + p * pair : 2 * width + (p + 1) * pair]
        total = None
        for h in range(2):
            scores = _nt(query * masks[h], key) * scale
            expo = jnp.exp(scores - jnp.max(scores, axis=-1, keepdims=True))
            probs = (expo * (1.0 / jnp.sum(expo, axis=-1, keepdims=True))).astype(bf16)
            probs_out[2 * p + h] = probs
            term = _nn(probs, val * masks[h])
            total = term if total is None else total + term
        mixed[:, p * pair : (p + 1) * pair] = total.astype(bf16)
    wait_first(slot, plans[0][1])
    attn = _nn(mixed[...], w_proj[...]) + biases[:, :width]
    attn_out[...] = attn.astype(bf16)
    one = value + mods[2:3] * attn
    one_out[...] = one
    normed, _ = norm_rows(one)
    mlp_in = (normed * (1.0 + mods[4:5]) + mods[3:4]).astype(bf16)
    wait_first(slot, plans[1][0])
    u = _nn(mlp_in, w_up[...]) + biases[:, width : width + inner]
    square = u * u
    tangent = jnp.tanh(GELU_K * (u + GELU_C * square * u))
    half = 0.5 * (1.0 + tangent)
    hidden_out[...] = (u * half).astype(bf16)
    slope = half + 0.5 * u * (1.0 - tangent * tangent) * (
        GELU_K + (3.0 * GELU_C * GELU_K) * square
    )
    slope_out[...] = slope.astype(bf16)
    wait_first(slot, plans[1][1])
    branch = _nn(hidden_out[...], w_down[...]) + biases[:, width + inner :]
    branch_out[...] = branch.astype(bf16)
    return one + mods[5:6] * branch


def mlp_back_body(slot, g, mods, one, hidden, slope, branch, weights, plan, sums, gada, bias_up, bias_down):
    w_up, w_down = weights
    a_up, a_down = sums
    f32, bf16 = jnp.float32, jnp.bfloat16
    gada[2:3, :] = jnp.sum(g * branch[...].astype(f32), axis=0, keepdims=True)
    gbranch = g * mods[5:6]
    bias_down[...] += jnp.sum(gbranch, axis=0, keepdims=True)
    gb = gbranch.astype(bf16)
    a_down[...] += _tn(hidden[...], gb)
    wait_first(slot, plan[1])
    gpre = _nt(gb, w_down[...]) * slope[...].astype(f32)
    bias_up[...] += jnp.sum(gpre, axis=0, keepdims=True)
    gp = gpre.astype(bf16)
    normed, inv = norm_rows(one[...])
    mlp_in = (normed * (1.0 + mods[4:5]) + mods[3:4]).astype(bf16)
    a_up[...] += _tn(mlp_in, gp)
    wait_first(slot, plan[0])
    gmlp = _nt(gp, w_up[...])
    gada[0:1, :] = jnp.sum(gmlp, axis=0, keepdims=True)
    gada[1:2, :] = jnp.sum(gmlp * normed, axis=0, keepdims=True)
    return g + norm_back(normed, inv, gmlp * (1.0 + mods[4:5]))


def attn_back_body(slot, heads, g1, mods, resid, qkv, probs, mixed, attn, weights, plan, sums, g_heads, gada, bias_proj):
    w_qkv, w_proj = weights
    a_qkv, a_proj = sums
    f32, bf16 = jnp.float32, jnp.bfloat16
    width = w_proj.shape[1]
    gada[2:3, :] = jnp.sum(g1 * attn[...].astype(f32), axis=0, keepdims=True)
    gattn = g1 * mods[2:3]
    bias_proj[...] += jnp.sum(gattn, axis=0, keepdims=True)
    ga = gattn.astype(bf16)
    a_proj[...] += _tn(mixed[...], ga)
    wait_first(slot, plan[1])
    gmixed = _nt(ga, w_proj[...]).astype(bf16)
    pair = 2 * width // heads
    scale = 1.0 / (width // heads) ** 0.5
    masks = lane_halves(pair)
    for p in range(heads // 2):
        query = qkv[:, p * pair : (p + 1) * pair]
        key = qkv[:, width + p * pair : width + (p + 1) * pair]
        val = qkv[:, 2 * width + p * pair : 2 * width + (p + 1) * pair]
        gm = gmixed[:, p * pair : (p + 1) * pair]
        gq, gk, gv = 0.0, 0.0, 0.0
        for h in range(2):
            low = probs[2 * p + h]
            gm_h = gm * masks[h]
            gprobs = _nt(gm_h, val)
            full = low.astype(f32)
            dot = jnp.sum(full * gprobs, axis=-1, keepdims=True)
            gscores = (full * (gprobs - dot) * scale).astype(bf16)
            gv = gv + _tn(low, gm_h)
            gq = gq + _nn(gscores, key * masks[h])
            gk = gk + _tn(gscores, query * masks[h])
        g_heads[:, p * pair : (p + 1) * pair] = gq.astype(bf16)
        g_heads[:, width + p * pair : width + (p + 1) * pair] = gk.astype(bf16)
        g_heads[:, 2 * width + p * pair : 2 * width + (p + 1) * pair] = gv.astype(bf16)
    normed, inv = norm_rows(resid)
    attn_in = (normed * (1.0 + mods[1:2]) + mods[0:1]).astype(bf16)
    a_qkv[...] += _tn(attn_in, g_heads[...])
    wait_first(slot, plan[0])
    gin = _nt(g_heads[...], w_qkv[...])
    gada[0:1, :] = jnp.sum(gin, axis=0, keepdims=True)
    gada[1:2, :] = jnp.sum(gin * normed, axis=0, keepdims=True)
    return g1 + norm_back(normed, inv, gin * (1.0 + mods[1:2]))


def emit_attn(shards, me, a_qkv, a_proj, keep, send):
    rows, triple = a_qkv.shape[0] // shards, a_qkv.shape[1]
    for n, j in enumerate(block_order(shards)):
        out, row = (keep, n) if n < shards // 2 else (send, n - shards // 2)
        at = pl.ds(pl.multiple_of((me ^ j) * rows, rows), rows)
        out[row, :, :triple] = a_qkv[at, :].astype(jnp.bfloat16)
        out[row, :, triple:] = a_proj[at, :].astype(jnp.bfloat16)


def emit_mlp(shards, me, a_up, a_down, keep, send):
    rows, inner = a_up.shape[0] // shards, a_up.shape[1]
    width = a_down.shape[1]
    ratio = inner // width
    for n, j in enumerate(block_order(shards)):
        out, row = (keep, n) if n < shards // 2 else (send, n - shards // 2)
        own = me ^ j
        at = pl.ds(pl.multiple_of(own * rows, rows), rows)
        out[row, :, :inner] = a_up[at, :].astype(jnp.bfloat16)
        for q in range(ratio):
            at = pl.ds(pl.multiple_of((own * ratio + q) * rows, rows), rows)
            col = inner + q * width
            out[row, :, col : col + width] = a_down[at, :].astype(jnp.bfloat16)


def clear(*refs):
    for ref in refs:
        ref[...] = jnp.zeros_like(ref[...])


def forward_kernel(shards, heads, info, resid, ada, biases, *rest):
    attn_pieces, mlp_pieces, rest = rest[:shards], rest[shards : 2 * shards], rest[2 * shards :]
    result, saved, rest = rest[0], rest[1:9], rest[9:]
    w_qkv, w_proj, w_up, w_down, attn_sems, mlp_sems = rest
    slot = pl.program_id(0)
    plans = (
        attn_plan(attn_pieces, w_qkv, w_proj, attn_sems, info[1]),
        mlp_plan(mlp_pieces, w_up, w_down, mlp_sems, info[1]),
    )

    @pl.when(slot == 0)
    def _():
        start_all(plans[0])
        start_all(plans[1])

    @pl.when(slot < info[0])
    def _():
        result[0] = forward_body(
            slot,
            heads,
            resid[0],
            ada[0],
            biases,
            (w_qkv, w_proj, w_up, w_down),
            plans,
            [ref.at[0] for ref in saved],
        )

    @pl.when(slot >= info[0])
    def _():
        clear(result)


def last_block_kernel(shards, heads, info, resid, grad, ada, biases, *rest):
    attn_pieces, mlp_pieces, rest = rest[:shards], rest[shards : 2 * shards], rest[2 * shards :]
    result, grad_out, gada_attn, gada_mlp, bias_proj, bias_up, bias_down = rest[:7]
    attn_keep, attn_send, mlp_keep, mlp_send = rest[7:11]
    w_qkv, w_proj, w_up, w_down, a_qkv, a_proj, a_up, a_down, g_heads = rest[11:20]
    saved, attn_sems, mlp_sems = rest[20:28], rest[28], rest[29]
    one, qkv, probs, mixed, attn, hidden, slope, branch = saved
    slot, me = pl.program_id(0), info[1]
    plans = (
        attn_plan(attn_pieces, w_qkv, w_proj, attn_sems, me),
        mlp_plan(mlp_pieces, w_up, w_down, mlp_sems, me),
    )
    done = [[], []]

    @pl.when(slot == 0)
    def _():
        start_all(plans[0])
        start_all(plans[1])
        clear(a_qkv, a_proj, a_up, a_down, bias_proj, bias_up, bias_down)

    @pl.when(slot < info[0])
    def _():
        mods, value = ada[0], resid[0]
        weights = (w_qkv, w_proj, w_up, w_down)
        result[0] = forward_body(slot, heads, value, mods, biases, weights, plans, saved)
        g1 = mlp_back_body(
            slot, grad[0], mods, one, hidden, slope, branch, weights[2:], done, (a_up, a_down),
            gada_mlp.at[0], bias_up, bias_down,
        )
        grad_out[0] = attn_back_body(
            slot, heads, g1, mods, value, qkv, probs, mixed, attn, weights[:2], done,
            (a_qkv, a_proj), g_heads, gada_attn.at[0], bias_proj,
        )

    @pl.when(slot >= info[0])
    def _():
        clear(result, grad_out, gada_attn, gada_mlp)

    @pl.when(slot == pl.num_programs(0) - 1)
    def _():
        emit_attn(shards, me, a_qkv, a_proj, attn_keep, attn_send)
        emit_mlp(shards, me, a_up, a_down, mlp_keep, mlp_send)


def mlp_back_kernel(shards, heads, info, grad, ada, one, hidden, slope, branch, *rest):
    pieces, rest = rest[:shards], rest[shards:]
    grad_out, gada, bias_up, bias_down, keep, send, w_up, w_down, a_up, a_down, sems = rest
    slot, me = pl.program_id(0), info[1]
    plan = mlp_plan(pieces, w_up, w_down, sems, me)

    @pl.when(slot == 0)
    def _():
        start_all(plan)
        clear(a_up, a_down, bias_up, bias_down)

    @pl.when(slot < info[0])
    def _():
        grad_out[0] = mlp_back_body(
            slot, grad[0], ada[0], one.at[0], hidden.at[0], slope.at[0], branch.at[0],
            (w_up, w_down), plan, (a_up, a_down), gada.at[0], bias_up, bias_down,
        )

    @pl.when(slot >= info[0])
    def _():
        clear(gada)

    @pl.when(slot == pl.num_programs(0) - 1)
    def _():
        emit_mlp(shards, me, a_up, a_down, keep, send)


def attn_back_kernel(shards, heads, info, grad, resid, ada, qkv, probs, mixed, attn, *rest):
    pieces, rest = rest[:shards], rest[shards:]
    grad_out, gada, bias_proj, keep, send, w_qkv, w_proj, a_qkv, a_proj, g_heads, sems = rest
    slot, me = pl.program_id(0), info[1]
    plan = attn_plan(pieces, w_qkv, w_proj, sems, me)

    @pl.when(slot == 0)
    def _():
        start_all(plan)
        clear(a_qkv, a_proj, bias_proj)

    @pl.when(slot < info[0])
    def _():
        grad_out[0] = attn_back_body(
            slot, heads, grad[0], ada[0], resid[0], qkv.at[0], probs.at[0], mixed.at[0],
            attn.at[0], (w_qkv, w_proj), plan, (a_qkv, a_proj), g_heads, gada.at[0], bias_proj,
        )

    @pl.when(slot >= info[0])
    def _():
        clear(grad_out, gada)

    @pl.when(slot == pl.num_programs(0) - 1)
    def _():
        emit_attn(shards, me, a_qkv, a_proj, keep, send)


def unpack_kernel(flag, *refs):
    g_qkv, g_proj, g_up, g_down = refs[-4:]
    triple, width, inner = g_qkv.shape[2], g_proj.shape[2], g_up.shape[2]
    rows, edge = g_qkv.shape[1], (triple + width) // 2

    def write(first):
        for n in range(LAYERS):
            low, high = refs[2 * n + first], refs[2 * n + 1 - first]
            g_qkv[n, :, :edge] = low[:, :edge].astype(jnp.float32)
            g_qkv[n, :, edge:] = high[:, : triple - edge].astype(jnp.float32)
            g_proj[n] = high[:, triple - edge : edge].astype(jnp.float32)
            g_up[n] = low[:, edge:].astype(jnp.float32)
            for q in range(inner // width):
                part = high[:, edge + q * width : edge + (q + 1) * width]
                g_down[n, q * rows : (q + 1) * rows, :] = part.astype(jnp.float32)

    @pl.when(flag[0] == 0)
    def _():
        write(0)

    @pl.when(flag[0] != 0)
    def _():
        write(1)


def unpack_call(flag, sums, sizes):
    triple, width, inner = sizes
    rows = sums[0][0].shape[0]
    shapes = [
        (LAYERS, rows, triple),
        (LAYERS, rows, width),
        (LAYERS, rows, inner),
        (LAYERS, inner // width * rows, width),
    ]
    parts = [half for pair in sums for half in pair]
    return pl.pallas_call(
        unpack_kernel,
        out_shape=[jax.ShapeDtypeStruct(s, jnp.float32) for s in shapes],
        in_specs=[pl.BlockSpec(memory_space=pltpu.SMEM)]
        + [pl.BlockSpec(memory_space=pltpu.VMEM)] * len(parts),
        out_specs=[pl.BlockSpec(memory_space=pltpu.VMEM)] * len(shapes),
        name="unpack",
    )(flag, *parts)


def small_kernel(starts, act, *refs):
    out, work = refs[-2:]
    work[...] = jnp.zeros_like(work[...])
    for part, start in zip(refs[:-2], starts):
        work[:LAYERS, start : start + part.shape[1]] = part[...].astype(jnp.float32)
    work[LAYERS : LAYERS + act.shape[0], : act.shape[1]] = act[...].astype(jnp.float32)
    out[...] = work[...].astype(out.dtype)


def small_call(act, parts):
    starts, total = [], 0
    for part in parts:
        starts.append(total)
        total += -(-part.shape[1] // 128) * 128
    shape = (-(-(LAYERS + act.shape[0]) // 16) * 16, max(total, act.shape[1]))
    out = pl.pallas_call(
        functools.partial(small_kernel, starts),
        out_shape=jax.ShapeDtypeStruct(shape, jnp.bfloat16),
        in_specs=[pl.BlockSpec(memory_space=pltpu.VMEM)] * (1 + len(parts)),
        out_specs=pl.BlockSpec(memory_space=pltpu.VMEM),
        scratch_shapes=[pltpu.VMEM(shape, jnp.float32)],
        name="small_rows",
    )(act, *parts)
    return out, starts


def pack_kernel(qkv, proj, up, down, *outs):
    rows, triple = qkv.shape[1:]
    inner, width = up.shape[2], down.shape[2]
    for n in range(LAYERS):
        attn, mlp = outs[2 * n], outs[2 * n + 1]
        attn[:, :triple] = qkv[n]
        attn[:, triple:] = proj[n]
        mlp[:, :inner] = up[n]
        for q in range(inner // width):
            mlp[:, inner + q * width : inner + (q + 1) * width] = down[n, q * rows : (q + 1) * rows, :]


def pack_call(qkv, proj, up, down):
    rows, triple = qkv.shape[1:]
    inner, width = up.shape[2], down.shape[2]
    shapes = [(rows, triple + width), (rows, 2 * inner)] * LAYERS
    return pl.pallas_call(
        pack_kernel,
        out_shape=[jax.ShapeDtypeStruct(s, qkv.dtype) for s in shapes],
        in_specs=[pl.BlockSpec(memory_space=pltpu.VMEM)] * 4,
        out_specs=[pl.BlockSpec(memory_space=pltpu.VMEM)] * len(shapes),
        name="pack_weights",
    )(qkv, proj, up, down)


def gad_kernel(*refs):
    out, work = refs[-2:]
    if work.shape[0] > LAYERS * (refs[0].shape[0] + 1):
        work[...] = jnp.zeros_like(work[...])
    for n in range(LAYERS):
        attn, mlp, proj, up, down = refs[5 * n : 5 * n + 5]
        slots, _, width = attn.shape
        base = n * (slots + 1)
        for s in range(slots):
            for k in range(3):
                row = slice(base + s, base + s + 1)
                work[row, k * width : (k + 1) * width] = attn[s, k : k + 1, :]
                work[row, (3 + k) * width : (4 + k) * width] = mlp[s, k : k + 1, :]
        row = slice(base + slots, base + slots + 1)
        inner = up.shape[1]
        work[row, :width] = proj[...]
        work[row, width : width + inner] = up[...]
        work[row, width + inner :] = down[...]
    out[...] = work[...].astype(out.dtype)


def gad_call(layers, wide):
    slots = layers[0][0].shape[0]
    shape = (-(-LAYERS * (slots + 1) // 8) * 8, wide)
    parts = [part for layer in layers for part in layer]
    return pl.pallas_call(
        gad_kernel,
        out_shape=jax.ShapeDtypeStruct(shape, jnp.bfloat16),
        in_specs=[pl.BlockSpec(memory_space=pltpu.VMEM)] * len(parts),
        out_specs=pl.BlockSpec(memory_space=pltpu.VMEM),
        scratch_shapes=[pltpu.VMEM(shape, jnp.float32)],
        name="gad_rows",
    )(*parts)


def per_slot(shape):
    rest = (0,) * (len(shape) - 1)
    return pl.BlockSpec((1,) + tuple(shape[1:]), lambda slot, info: (slot,) + rest)


def whole_block(shape):
    zeros = (0,) * len(shape)
    return pl.BlockSpec(tuple(shape), lambda slot, info: zeros)


def run_kernel(kernel, dims, info, blocked, fixed, pieces, outs, fixed_outs, scratch, passes):
    slots, length, width, triple, inner, heads, shards = dims
    shapes = list(outs) + list(fixed_outs)
    return pl.pallas_call(
        functools.partial(kernel, shards, heads),
        out_shape=[jax.ShapeDtypeStruct(s, d) for s, d in shapes],
        grid_spec=pltpu.PrefetchScalarGridSpec(
            num_scalar_prefetch=1,
            grid=(slots,),
            in_specs=[per_slot(a.shape) for a in blocked]
            + [whole_block(a.shape) for a in fixed]
            + [pl.BlockSpec(memory_space=pl.ANY)] * len(pieces),
            out_specs=[per_slot(s) for s, _ in outs] + [whole_block(s) for s, _ in fixed_outs],
            scratch_shapes=scratch,
        ),
        compiler_params=pltpu.CompilerParams(vmem_limit_bytes=VMEM_GRANT),
        cost_estimate=pl.CostEstimate(
            flops=passes * slots * length * width * (triple + width + 2 * inner),
            bytes_accessed=passes * slots * length * inner * 4,
            transcendentals=slots * length * inner,
        ),
    )(info, *blocked, *fixed, *pieces)


def kernel_parts(dims):
    slots, length, width, triple, inner, heads, shards = dims
    f32, bf16 = jnp.float32, jnp.bfloat16
    rows, ratio = width // shards, inner // width
    saved = [
        ((length, width), f32),
        ((length, triple), bf16),
        ((heads, length, length), bf16),
        ((length, width), bf16),
        ((length, width), bf16),
        ((length, inner), bf16),
        ((length, inner), bf16),
        ((length, width), bf16),
    ]
    w_attn = [pltpu.VMEM((width, triple), bf16), pltpu.VMEM((width, width), bf16)]
    w_mlp = [pltpu.VMEM((width, inner), bf16), pltpu.VMEM((inner, width), bf16)]
    a_attn = [pltpu.VMEM((width, triple), f32), pltpu.VMEM((width, width), f32)]
    a_mlp = [pltpu.VMEM((width, inner), f32), pltpu.VMEM((inner, width), f32)]
    heads_buf = [pltpu.VMEM((length, triple), bf16)]
    sems = [pltpu.SemaphoreType.DMA((shards, 2)), pltpu.SemaphoreType.DMA((shards, 1 + ratio))]
    rows_of = ((slots, length, width), f32)
    gada = ((slots, 3, width), f32)
    bias = [((1, width), f32), ((1, inner), f32), ((1, width), f32)]
    half = (shards // 2, rows)
    out_attn = [(half + (triple + width,), bf16)] * 2
    out_mlp = [(half + (2 * inner,), bf16)] * 2
    return saved, w_attn, w_mlp, a_attn, a_mlp, heads_buf, sems, rows_of, gada, bias, out_attn, out_mlp


def forward_call(dims, info, resid, ada, biases, attn_pieces, mlp_pieces):
    saved, w_attn, w_mlp, _, _, _, sems, rows_of, *_ = kernel_parts(dims)
    outs = [rows_of] + [((dims[0],) + s, d) for s, d in saved]
    return run_kernel(
        forward_kernel, dims, info, (resid, ada), (biases,),
        attn_pieces + mlp_pieces, outs, [], w_attn + w_mlp + sems, 2,
    )


def last_block_call(dims, info, resid, grad, ada, biases, attn_pieces, mlp_pieces):
    parts = kernel_parts(dims)
    saved, w_attn, w_mlp, a_attn, a_mlp, heads_buf, sems, rows_of, gada, bias, out_attn, out_mlp = parts
    scratch = w_attn + w_mlp + a_attn + a_mlp + heads_buf
    scratch += [pltpu.VMEM(s, d) for s, d in saved] + sems
    return run_kernel(
        last_block_kernel, dims, info, (resid, grad, ada), (biases,),
        attn_pieces + mlp_pieces, [rows_of, rows_of, gada, gada], bias + out_attn + out_mlp,
        scratch, 6,
    )


def mlp_back_call(dims, info, grad, ada, one, hidden, slope, branch, pieces):
    parts = kernel_parts(dims)
    _, _, w_mlp, _, a_mlp, _, sems, rows_of, gada, bias, _, out_mlp = parts
    return run_kernel(
        mlp_back_kernel, dims, info, (grad, ada, one, hidden, slope, branch), (),
        pieces, [rows_of, gada], bias[1:] + out_mlp, w_mlp + a_mlp + sems[1:], 2,
    )


def attn_back_call(dims, info, grad, resid, ada, qkv, probs, mixed, attn, pieces):
    parts = kernel_parts(dims)
    _, w_attn, _, a_attn, _, heads_buf, sems, rows_of, gada, bias, out_attn, _ = parts
    return run_kernel(
        attn_back_kernel, dims, info,
        (grad, resid, ada, qkv, probs, mixed, attn), (), pieces, [rows_of, gada],
        bias[:1] + out_attn, w_attn + a_attn + heads_buf + sems[:1], 2,
    )


def gather_rel(value, axis, size):
    pieces = {0: value}
    for bit in reversed(bits_of(size)):
        for j in list(pieces):
            pieces[j ^ bit] = swap(pieces[j], axis, size, bit)
    return [pieces[j] for j in range(size)]


def gather_all(value, stages, fast=False):
    for axis, size, bit in stages:
        other = swap(value, axis, size, bit)
        upper = has_bit(axis, bit)
        both = [jnp.where(upper, other, value), jnp.where(upper, value, other)]
        if fast:
            value = jnp.stack(both, axis=1).reshape((-1,) + value.shape[1:])
        else:
            value = jnp.concatenate(both, axis=0)
    return value


def to_absolute(pieces, axis):
    me = lax.axis_index(axis)
    out = jnp.zeros((len(pieces),) + pieces[0].shape, pieces[0].dtype)
    for j, piece in enumerate(pieces):
        out = lax.dynamic_update_index_in_dim(out, piece, me ^ j, 0)
    return out


def scatter_sum(blocks, axis, size):
    blocks = dict(enumerate(blocks))
    for bit in bits_of(size):
        keep = [j for j in blocks if not j & bit]
        got = swap(jnp.stack([blocks[j | bit] for j in keep]), axis, size, bit)
        blocks = {j: blocks[j] + got[n] for n, j in enumerate(keep)}
    return blocks[0]


def halves_of(left, right, kind, upper):
    if kind == "rows":
        half = left.shape[0] // 2
        return left[:half] + right[:half], left[half:] + right[half:]
    if kind == "columns":
        half = left.shape[-1] // 2
        low = left[..., :half] + right[..., :half]
        high = left[..., half:] + right[..., half:]
        return jnp.where(upper, high, low), jnp.where(upper, low, high)
    value = left + right
    return value, value


def run_stages(left, right, plan):
    trail = []
    for axis, size, bit, kind in plan:
        stay, go = halves_of(left, right, kind, has_bit(axis, bit))
        left, right = stay, swap(go, axis, size, bit)
        if kind == "columns":
            trail.append((axis, size, bit))
    return left, right, trail


def widen(value, axis, size, bit):
    other = swap(value, axis, size, bit)
    upper = has_bit(axis, bit)
    return jnp.where(upper, other, value), jnp.where(upper, value, other)


def early_plans(groups, shards):
    first, *others = [("fsdp", shards, bit, "rows") for bit in bits_of(shards)]
    cut = [("dp", groups, 1, "columns")]
    return first, cut + others, others + cut


def late_plan(groups, columns):
    plan = []
    for bit in bits_of(groups)[1:]:
        if 2 * bit < groups and (columns // 2) % 128 == 0:
            columns //= 2
            plan.append(("dp", groups, bit, "columns"))
        else:
            plan.append(("dp", groups, bit, "full"))
    return plan


def early_sum(kept, sent, first, plan):
    got = swap(sent, *first[:3])
    left, right, _ = run_stages(kept, got, plan)
    return left, right


def late_sum(attn, mlp, groups):
    value = jnp.concatenate([attn[0][0] + attn[1][0], mlp[0][0] + mlp[1][0]], axis=-1)
    left, right, trail = value, None, []
    plan = late_plan(groups, value.shape[-1])
    for axis, size, bit, kind in plan:
        if right is None:
            half = left.shape[-1] // 2
            upper = has_bit(axis, bit)
            stay, go = left, left
            if kind == "columns":
                low, high = left[:, :half], left[:, half:]
                stay, go = jnp.where(upper, high, low), jnp.where(upper, low, high)
        else:
            stay, go = halves_of(left, right, kind, has_bit(axis, bit))
        left, right = stay, swap(go, axis, size, bit)
        if kind == "columns":
            trail.append((axis, size, bit))
    value = left if right is None else left + right
    for stage in reversed(trail):
        value = jnp.concatenate(widen(value, *stage), axis=-1)
    return value, swap(value, "dp", groups, 1)


def on_device(
    sizes,
    latents,
    conditioning,
    seq_counts,
    cotangent,
    ada_weight,
    ada_bias,
    qkv_weight,
    proj_weight,
    proj_bias,
    up_weight,
    up_bias,
    down_weight,
    down_bias,
):
    groups, shards = sizes
    bf16, f32 = jnp.bfloat16, jnp.float32
    slots, length, width = latents.shape
    rows = qkv_weight.shape[1]
    triple, inner = qkv_weight.shape[2], up_weight.shape[2]
    wide = ada_weight.shape[2]
    me = lax.axis_index("fsdp")
    shard_stages = [("fsdp", shards, bit) for bit in bits_of(shards)]

    act = jax.nn.silu(conditioning).astype(bf16)
    parts = (ada_bias, proj_bias, up_bias, down_bias)
    small, starts = small_call(act, parts)
    small = gather_all(small[None], shard_stages[::-1], fast=True)

    attn_pieces, mlp_pieces = [], []
    packs = pack_call(qkv_weight, proj_weight, up_weight, down_weight)
    for n in range(LAYERS):
        attn_pieces.append(gather_rel(packs[2 * n], "fsdp", shards))
        mlp_pieces.append(gather_rel(packs[2 * n + 1], "fsdp", shards))

    act_group = small[:, LAYERS : LAYERS + slots, :width].reshape(shards * slots, width)
    group_stages = [("dp", groups, bit) for bit in bits_of(groups)[:1] + bits_of(groups)[:0:-1]]
    acts = gather_all(act_group.reshape(1, shards, slots, width), group_stages)
    counts = len(group_stages), len(shard_stages)
    acts = acts.reshape([2] * sum(counts) + [slots, width])
    order = list(range(sum(counts)))[: counts[0] - 1 : -1] + list(range(counts[0]))
    acts = acts.transpose(order + [sum(counts), sum(counts) + 1]).reshape(-1, slots, width)
    act_cols = lax.dynamic_slice(act_group, (0, me * rows), (shards * slots, rows))
    partial = jnp.stack(
        [jnp.dot(act_cols, ada_weight[n], preferred_element_type=f32) for n in range(LAYERS)]
    ).reshape(LAYERS, shards, slots, wide)
    blocks = [
        lax.dynamic_index_in_dim(partial, me ^ j, 1, keepdims=False).reshape(LAYERS * slots, wide)
        for j in range(shards)
    ]
    ada = scatter_sum(blocks, "fsdp", shards).reshape(LAYERS, slots, wide)
    bias_of = [
        [
            small[:, n, start : start + part.shape[1]].reshape(-1).astype(f32)
            for part, start in zip(parts, starts)
        ]
        for n in range(LAYERS)
    ]
    modulation = [(ada[n] + bias_of[n][0]).reshape(slots, 6, width) for n in range(LAYERS)]
    bias_rows = [jnp.concatenate(bias_of[n][1:])[None] for n in range(LAYERS)]

    dims = (slots, length, width, triple, inner, HEADS, shards)
    info = jnp.stack([seq_counts[0], me.astype(jnp.int32)])
    top = LAYERS - 1
    inputs, saved = [], []
    current = latents
    for n in range(top):
        inputs.append(current)
        current, *kept = forward_call(
            dims, info, current, modulation[n], bias_rows[n], attn_pieces[n], mlp_pieces[n]
        )
        saved.append(kept)
    sums = [None] * LAYERS
    small_rows = [None] * LAYERS
    first, attn_plan_of, mlp_plan_of = early_plans(groups, shards)

    def reduce_layer(n, attn_pair, mlp_pair):
        mlp = early_sum(*mlp_pair, first, mlp_plan_of)
        attn = early_sum(*attn_pair, first, attn_plan_of)
        sums[n] = late_sum(attn, mlp, groups)

    outs = last_block_call(
        dims, info, current, cotangent, modulation[top], bias_rows[top],
        attn_pieces[top], mlp_pieces[top],
    )
    block_out, grad, gada_attn, gada_mlp, b_proj, b_up, b_down = outs[:7]
    reduce_layer(top, outs[7:9], outs[9:11])
    small_rows[top] = (gada_attn, gada_mlp, b_proj, b_up, b_down)
    for n in reversed(range(top)):
        one, qkv, probs, mixed, attn, hidden, slope, branch = saved[n]
        g1, gada_mlp, b_up, b_down, *mlp_pair = mlp_back_call(
            dims, info, grad, modulation[n], one, hidden, slope, branch, mlp_pieces[n]
        )
        grad, gada_attn, b_proj, *attn_pair = attn_back_call(
            dims, info, g1, inputs[n], modulation[n], qkv, probs, mixed, attn, attn_pieces[n]
        )
        reduce_layer(n, attn_pair, mlp_pair)
        small_rows[n] = (gada_attn, gada_mlp, b_proj, b_up, b_down)

    message = gad_call(small_rows, wide)
    stages = group_stages + shard_stages[::-1]
    every = gather_all(message[None], stages)
    per_layer = slots + 1
    acts_cols = lax.dynamic_slice(acts, (0, 0, me * rows), acts.shape[:2] + (rows,))
    tail_rows = message.shape[0] - slots
    flat = every.reshape(-1, wide)
    g_ada = jnp.stack(
        [
            outer_total(
                jnp.pad(
                    acts_cols, ((0, 0), (n * per_layer, tail_rows - n * per_layer), (0, 0))
                ).reshape(-1, rows),
                flat,
            )
            for n in range(LAYERS)
        ]
    )
    totals = jnp.sum(every.astype(f32), axis=0)
    g_ada_bias = jnp.stack(
        [jnp.sum(totals[n * per_layer : n * per_layer + slots], axis=0) for n in range(LAYERS)]
    )
    g_bias = jnp.stack([totals[n * per_layer + slots] for n in range(LAYERS)])

    begin = [
        has_bit(axis, bit).astype(jnp.int32) if axis == "dp" else jnp.int32(0)
        for axis, _, bit in reversed(stages)
    ]
    extent = [1 if axis == "dp" else 2 for axis, _, _ in stages[::-1]]
    grid = every.reshape([2] * len(stages) + list(message.shape))
    zero = jnp.int32(0)
    mine = lax.dynamic_slice(grid, begin + [zero, zero], extent + list(message.shape))
    mine = mine.reshape(-1, wide)
    total = 0.0
    for n in range(LAYERS):
        part = matmul_back(mine, ada_weight[n]).reshape(shards, -1, rows)
        total = total + part[:, n * per_layer : n * per_layer + slots]
    total = total.reshape([2] * len(bits_of(shards)) + [slots, rows])
    order = tuple(reversed(range(len(bits_of(shards)))))
    total = total.transpose(order + (len(order), len(order) + 1)).reshape(shards, slots, rows)
    got = [lax.dynamic_index_in_dim(total, me, 0, keepdims=False)]
    for j in range(1, shards):
        sent = lax.dynamic_index_in_dim(total, me ^ j, 0, keepdims=False)
        got.append(swap(sent, "fsdp", shards, j))
    grad_cond = to_absolute(got, "fsdp").transpose(1, 0, 2).reshape(slots, width)
    grad_cond = grad_cond * silu_slope(conditioning)

    upper = has_bit("dp", 1).astype(jnp.int32)[None]
    g_qkv, g_proj, g_up, down_sum = unpack_call(upper, sums, (triple, width, inner))
    own_inner = inner // shards
    return (
        block_out,
        grad,
        grad_cond,
        g_ada,
        lax.dynamic_slice_in_dim(g_ada_bias, me * (wide // shards), wide // shards, 1),
        g_qkv,
        g_proj,
        lax.dynamic_slice_in_dim(g_bias, me * rows, rows, 1),
        g_up,
        lax.dynamic_slice_in_dim(g_bias, width + me * own_inner, own_inner, 1),
        down_sum,
        lax.dynamic_slice_in_dim(g_bias, width + inner + me * rows, rows, 1),
    )


def solution(mesh):
    in_specs = (
        P(("dp", "fsdp"), None, None),
        P(("dp", "fsdp"), None),
        P(("dp", "fsdp")),
        P(("dp", "fsdp"), None, None),
        P(None, "fsdp", None),
        P(None, "fsdp"),
        P(None, "fsdp", None),
        P(None, "fsdp", None),
        P(None, "fsdp"),
        P(None, "fsdp", None),
        P(None, "fsdp"),
        P(None, "fsdp", None),
        P(None, "fsdp"),
    )
    out_specs = (
        P(("dp", "fsdp"), None, None),
        P(("dp", "fsdp"), None, None),
        P(("dp", "fsdp"), None),
        P(None, "fsdp", None),
        P(None, "fsdp"),
        P(None, "fsdp", None),
        P(None, "fsdp", None),
        P(None, "fsdp"),
        P(None, "fsdp", None),
        P(None, "fsdp"),
        P(None, "fsdp", None),
        P(None, "fsdp"),
    )
    sizes = (mesh.shape["dp"], mesh.shape["fsdp"])
    return jax.shard_map(
        functools.partial(on_device, sizes),
        mesh=mesh,
        in_specs=in_specs,
        out_specs=out_specs,
        check_vma=False,
    )
```
